32 devices in a mesh: clips: 2 (over x), sw: 16 (over z, y, core).
Axes of the slice: x: 2, y: 2, z: 4, core: 2. Of those that a mesh axis runs over, the one named last changes fastest.
Arguments:
- queries: bfloat16 [12, 16, 320, 384], P('clips', None, 'sw'), parts along dimension 0
- keys: bfloat16 [12, 16, 320, 384], P('clips', None, 'sw'), parts along dimension 0
- values: bfloat16 [12, 16, 320, 384], P('clips', None, 'sw'), parts along dimension 0, may hold values from -6 to 6
- out_grad: bfloat16 [12, 16, 320, 384], P('clips', None, 'sw'), parts along dimension 0, may hold values from -6 to 6
- extents: int32 [12, 2], replicated, may hold values from 1 to 3, as said below
- counts: int32 [2, 10], replicated, may hold values from 96 to 384, as said below
Outputs:
- query_grad: bfloat16 [12, 16, 320, 384], P('clips', None, 'sw'), parts along dimension 0
- key_grad: bfloat16 [12, 16, 320, 384], P('clips', None, 'sw'), parts along dimension 0
- value_grad: bfloat16 [12, 16, 320, 384], P('clips', None, 'sw'), parts along dimension 0
The draws below stay inside these ranges and needn't reach their ends.
There are 2 independent parts, one for each index of `clips`. The reference program is written for one: setup_inputs(seed, part) draws one part's arguments, and reference() takes and returns one part's arrays. A program takes and returns all parts, laid end to end along the dimension named above; an argument that names none is the same for every part. Nothing has to cross between parts.
Inputs may be any that keep to these rules, and one draw needn't show every extreme that they name: `extents`: each extent is 1 or 3; some head has 3 along the height and some head has 3 along the width. `counts`: tiles other than the first and last width tile are full.
All inputs are finite; a program needn't handle non-finite values.
Results may differ from the reference program's by a relative error of at most 0.011.
Values may be sent and summed in bfloat16 or wider, within the bound.
No kernel may reach another device: no remote copies, remote signals or barrier semaphores. Data moves between devices by JAX's collectives and lax.ppermute only.
A program may use at most 320 MiB of HBM per device.

```python
import jax
import jax.numpy as jnp
from jax import lax

HEADS = 12
HD = 128
HEAD_GROUPS = 4
TILE_T = 6
TILE_H = 8
TILE_W = 8
HT = 2
LW = 80
ROWS = 16
NWT = 10
HPG = 3
HCG = 384
SPAN = 320


def drawn_pair(key):
    shape = (TILE_T, ROWS, SPAN, HCG)
    base_key = jax.random.fold_in(key, 7)
    parts = jax.random.split(base_key, 2)
    query_base = jax.random.normal(parts[0], shape, jnp.float32)
    key_base = jax.random.normal(parts[1], shape, jnp.float32)
    return (query_base, key_base)


def draw_queries(key, part):
    query_base, key_base = drawn_pair(key)
    return query_base.astype(jnp.bfloat16)


def draw_keys(key, part):
    query_base, key_base = drawn_pair(key)
    return key_base.astype(jnp.bfloat16)


def draw_extents(key, part):
    first_key = jax.random.fold_in(key, 11)
    second_key = jax.random.fold_in(key, 12)
    radius = jax.random.randint(first_key, (HEADS, 2), 0, 2)
    forced = jax.random.randint(second_key, (2,), 0, HEADS)
    heads_ids = jnp.arange(HEADS)
    radius = radius.at[:, 0].set(jnp.where(heads_ids == forced[0], 1, radius[:, 0]))
    radius = radius.at[:, 1].set(jnp.where(heads_ids == forced[1], 1, radius[:, 1]))
    return (1 + 2 * radius).astype(jnp.int32)


def draw_counts(key, part):
    full_tile = TILE_T * TILE_H * TILE_W
    edge_key = jax.random.fold_in(key, 21)
    edges = jax.random.randint(edge_key, (HT, 2), full_tile // 4, full_tile + 1)
    position = jnp.arange(NWT)[None, :]
    result = jnp.full((HT, NWT), full_tile, jnp.int32)
    result = jnp.where(position == 0, edges[:, 0:1], result)
    result = jnp.where(position == NWT - 1, edges[:, 1:2], result)
    return result.astype(jnp.int32)


def shard_levels(stream_key, extent, pieces, smallest, high):
    gain = 1.0
    for axis_at, blocks in pieces:
        steps = jax.random.uniform(jax.random.fold_in(jax.random.fold_in(stream_key, 6), axis_at), (blocks,), jnp.float32, smallest / len(pieces), high / len(pieces))
        gain = gain * jnp.repeat(jnp.exp(steps), extent[axis_at] // blocks).reshape((-1,) + (1,) * (len(extent) - 1 - axis_at))
    return gain


def gaussian(stream_key, dims, width, bound, shards=(), kind=jnp.bfloat16):
    entries = jax.random.normal(stream_key, dims, jnp.float32) * width
    if len(shards) > 0:
        entries = shard_levels(stream_key, dims, shards, -0.22, 0.18) * entries
    return jnp.clip(entries, min=-bound, max=bound).astype(kind)


def setup_inputs(seed: int = 0, part: int = 0) -> dict:
    arg_keys = jax.random.split(jax.random.key(seed), 7)
    own_keys = jax.random.split(jax.random.fold_in(arg_keys[6], part), 7)
    queries = draw_queries(jax.random.fold_in(jax.random.fold_in(arg_keys[6], part), 71), part)
    keys = draw_keys(jax.random.fold_in(jax.random.fold_in(arg_keys[6], part), 71), part)
    values = gaussian(own_keys[2], (TILE_T, ROWS, SPAN, HCG), 1.0, 6.0, ((2, 16),))
    out_grad = gaussian(own_keys[3], (TILE_T, ROWS, SPAN, HCG), 1.0, 6.0, ((2, 16),))
    extents = draw_extents(jax.random.fold_in(arg_keys[6], 71), part)
    counts = draw_counts(jax.random.fold_in(arg_keys[6], 71), part)
    return dict(queries=queries, keys=keys, values=values, out_grad=out_grad, extents=extents, counts=counts)


def assemble(parts):
    first = jnp.pad(parts[:, :, :, :, 0], ((0, 0), (0, 2), (0, 0), (0, 0), (0, 0), (0, 0)))
    middle = jnp.pad(parts[:, :, :, :, 1], ((0, 0), (1, 1), (0, 0), (0, 0), (0, 0), (0, 0)))
    last = jnp.pad(parts[:, :, :, :, 2], ((0, 0), (2, 0), (0, 0), (0, 0), (0, 0), (0, 0)))
    summed = (first + middle + last)[:, 1:NWT + 1]
    whole = jnp.transpose(summed, (2, 3, 0, 1, 4, 5)).reshape(TILE_T, ROWS, SPAN, HCG).astype(jnp.bfloat16)
    return jnp.roll(whole, -(LW // 2), axis=2)


def reference(queries, keys, values, out_grad, extents, counts):
    scale = 1.0 / (HD ** 0.5)
    radius = (extents - 1) // 2
    grouped = [jnp.roll(item, LW // 2, axis=2).reshape(TILE_T, ROWS, HEAD_GROUPS, LW, HCG) for item in (queries, keys, values, out_grad)]
    width_pad = ((0, 0), (0, 0), (0, 0), (TILE_W, TILE_W), (0, 0))
    key_pad = jnp.pad(grouped[1], width_pad)
    value_pad = jnp.pad(grouped[2], width_pad)
    frame_ids = jnp.arange(TILE_T)[:, None, None]
    row_ids = jnp.arange(ROWS)[None, :, None]
    column = jnp.arange(3 * TILE_W)[None, None, :]
    offset = column // TILE_W - 1
    row_tile = row_ids // TILE_H
    in_tile = (frame_ids * TILE_H + row_ids % TILE_H) * TILE_W + column % TILE_W
    key_shape = (TILE_T, ROWS, 3 * TILE_W)
    query_shape = (TILE_T, ROWS, TILE_W)
    key_rowtile = jnp.broadcast_to(row_tile, key_shape).reshape(-1)
    query_rowtile = jnp.broadcast_to(row_tile, query_shape).reshape(-1)
    key_offset = jnp.broadcast_to(offset, key_shape).reshape(-1)
    height_gap = jnp.abs(query_rowtile[:, None] - key_rowtile[None, :])

    def block(index):
        group = index // NWT
        tile = index % NWT
        start = (tile * TILE_W).astype(jnp.int32)

        def take(source, span):
            chosen = lax.dynamic_index_in_dim(source, group, 2, keepdims=False)
            return lax.dynamic_slice_in_dim(chosen, start, span, 2).reshape(-1, HPG, HD).astype(jnp.float32)

        query_block = take(grouped[0], TILE_W)
        grad_block = take(grouped[3], TILE_W)
        key_block = take(key_pad, 3 * TILE_W)
        value_block = take(value_pad, 3 * TILE_W)
        near_tile = tile + offset
        inside = (near_tile >= 0) & (near_tile < NWT)
        safe = jnp.clip(near_tile, 0, NWT - 1)
        limit = counts[row_tile, safe]
        key_ok = jnp.broadcast_to(inside & (in_tile < limit), key_shape).reshape(-1)
        head_radius = lax.dynamic_slice_in_dim(radius, (group * HPG).astype(jnp.int32), HPG, 0)
        allowed = (key_ok[None, None, :]
                   & (jnp.abs(key_offset)[None, None, :] <= head_radius[:, 1][:, None, None])
                   & (height_gap[None, :, :] <= head_radius[:, 0][:, None, None]))
        scores = jnp.einsum('qhd,khd->hqk', query_block, key_block) * scale
        masked = jnp.where(allowed, scores, -1e30)
        row_peak = jnp.max(masked, axis=-1, keepdims=True)
        row_total = jnp.sum(jnp.where(allowed, jnp.exp(masked - row_peak), 0.0), axis=-1, keepdims=True)
        log_total = row_peak + jnp.log(row_total)
        probs = jnp.exp(masked - log_total)
        probs_b = lax.optimization_barrier(probs.astype(jnp.bfloat16)).astype(jnp.float32)
        attended = jnp.einsum('hqk,khd->qhd', probs_b, value_block)
        delta = jnp.sum(grad_block * attended, axis=-1)
        dprobs = jnp.einsum('qhd,khd->hqk', grad_block, value_block)
        dscores = probs * (dprobs - jnp.transpose(delta)[:, :, None])
        dscores_b = lax.optimization_barrier(dscores.astype(jnp.bfloat16)).astype(jnp.float32)
        query_part = (jnp.einsum('hqk,khd->qhd', dscores_b, key_block) * scale).astype(jnp.bfloat16)
        key_part = jnp.einsum('hqk,qhd->khd', dscores_b, query_block) * scale
        value_part = jnp.einsum('hqk,qhd->khd', probs_b, grad_block)
        return (query_part.reshape(TILE_T, ROWS, TILE_W, HCG),
                key_part.reshape(TILE_T, ROWS, 3, TILE_W, HCG),
                value_part.reshape(TILE_T, ROWS, 3, TILE_W, HCG))

    query_parts, key_parts, value_parts = lax.map(block, jnp.arange(HEAD_GROUPS * NWT, dtype=jnp.int32))
    query_parts = query_parts.reshape(HEAD_GROUPS, NWT, TILE_T, ROWS, TILE_W, HCG)
    query_grad = jnp.transpose(query_parts, (2, 3, 0, 1, 4, 5)).reshape(TILE_T, ROWS, SPAN, HCG)
    query_grad = jnp.roll(query_grad, -(LW // 2), axis=2)
    key_parts = key_parts.reshape(HEAD_GROUPS, NWT, TILE_T, ROWS, 3, TILE_W, HCG)
    value_parts = value_parts.reshape(HEAD_GROUPS, NWT, TILE_T, ROWS, 3, TILE_W, HCG)
    return (query_grad, assemble(key_parts), assemble(value_parts))
```

```python
import functools

import jax
import jax.numpy as jnp
from jax import lax
from jax.experimental import pallas as pl
from jax.experimental.pallas import tpu as pltpu
from jax.sharding import PartitionSpec as P

HD = 128
HEAD_GROUPS = 4
TILE_H = 8
TILE_W = 8
LW = 80
KC = 128


def attention_kernel(
    info, q_ref, k_ref, v_ref, g_ref, near_ref, far_ref,
    dq_ref, own_ref, near_out, far_out,
    kw, vw, kt, qs, gs, dqs, dkw, dvw, s_scr, p_scr,
):
    frames = q_ref.shape[0]
    full = frames * TILE_H * TILE_W
    half = full // 2
    both = 2 * full
    head = pl.program_id(0)
    parity = info[0]
    border = info[1]
    high = info[4 + 2 * head]
    wide = info[5 + 2 * head]
    scale = 1.0 / HD**0.5
    c_off = parity * 12
    b_off = 8 - parity * 4
    a_off = 16 - parity * 16
    mix_off = parity * 8
    out_off = 4 - parity * 4

    def rows(ref, lead, start, cols, ht):
        block = ref[lead + (slice(None), pl.ds(start, cols), pl.ds(ht * 8, 8), slice(None))]
        return block.astype(jnp.float32).reshape(frames * cols * 8, HD).astype(jnp.bfloat16)

    for ht in range(2):
        for dst, src in ((qs, q_ref), (gs, g_ref)):
            dst[ht * full : (ht + 1) * full, :] = rows(src, (), c_off, 8, ht)
            dst[both + ht * full : both + (ht + 1) * full, :] = rows(src, (), b_off, 8, ht)
            dst[2 * both + ht * half : 2 * both + (ht + 1) * half, :] = rows(src, (), a_off, 4, ht)
        for which, dst, src in ((0, kw, k_ref), (1, vw, v_ref)):
            lo = ht * full
            dst[lo : lo + full, :] = rows(far_ref, (which,), 0, 8, ht)
            lo += both
            dst[lo : lo + full, :] = rows(src, (), c_off, 8, ht)
            lo += both
            dst[lo : lo + full, :] = rows(src, (), b_off, 8, ht)
            lo += both
            dst[lo : lo + half, :] = rows(src, (), a_off, 4, ht)
            dst[lo + half : lo + full, :] = rows(near_ref, (which,), mix_off, 4, ht)
            lo += both
            dst[lo : lo + full, :] = rows(near_ref, (which,), out_off, 8, ht)
    dkw[...] = jnp.zeros_like(dkw)
    dvw[...] = jnp.zeros_like(dvw)

    def transpose_step(i, carry):
        start = pl.multiple_of(i * KC, KC)
        kt[:, pl.ds(start, KC)] = jnp.transpose(kw[pl.ds(start, KC), :])
        return carry

    lax.fori_loop(0, 5 * both // KC, transpose_step, 0)

    def unit(q_lo, n_q, tile, key_lo, n_k):
        queries = qs[q_lo : q_lo + n_q, :]
        grads = gs[q_lo : q_lo + n_q, :]
        first = tile - wide
        if tile == 1:
            first = jnp.where(border == 1, 1, first)
        last = tile + wide + 1
        per = n_k // KC

        def key_start(i):
            w = i // per
            return pl.multiple_of(w * both + key_lo + (i - w * per) * KC, KC)

        def fold(x, op):
            return op(x.reshape(KC // 8, 8, n_q), axis=0)

        def scores(start):
            return lax.dot_general(
                kw[pl.ds(start, KC), :], queries, (((1,), (1,)), ((), ())),
                preferred_element_type=jnp.float32,
            )

        def first_pass(i, peak):
            start = key_start(i)
            s = scores(start)
            s_scr[pl.ds(pl.multiple_of(i * KC, KC), KC), :n_q] = s
            return jnp.maximum(peak, fold(s, jnp.max))

        def masked_pass(i, peak):
            start = key_start(i)
            s = scores(start)
            at = start - both + lax.broadcasted_iota(jnp.int32, (KC, n_q), 0)
            ht = at // full
            at = at - ht * full
            t = at // 64
            c = at // 8 - t * 8
            r = at - at // 8 * 8
            place = t * 64 + r * 8 + c
            limit = jnp.where(ht == 0, info[2], info[3])
            s = jnp.where(place < limit, s, -1e30)
            s_scr[pl.ds(pl.multiple_of(i * KC, KC), KC), :n_q] = s
            return jnp.maximum(peak, fold(s, jnp.max))

        peak = jnp.full((8, n_q), -3e38, jnp.float32)
        if tile <= 2:
            split = jnp.where(border == 1, 2 * per, first * per)
            begin = jnp.where(border == 1, jnp.where(first <= 1, per, 2 * per), first * per)
            peak = lax.fori_loop(begin, split, masked_pass, peak)
            peak = lax.fori_loop(split, last * per, first_pass, peak)
        else:
            peak = lax.fori_loop(first * per, last * per, first_pass, peak)
        top = jnp.max(peak, axis=0, keepdims=True) * scale

        def second_pass(i, carry):
            total, weighted = carry
            start = key_start(i)
            at = pl.ds(pl.multiple_of(i * KC, KC), KC)
            e = jnp.exp(s_scr[at, :n_q] * scale - top)
            dp = lax.dot_general(
                vw[pl.ds(start, KC), :], grads, (((1,), (1,)), ((), ())),
                preferred_element_type=jnp.float32,
            )
            s_scr[at, :n_q] = e
            p_scr[at, :n_q] = dp
            return (total + fold(e, jnp.sum), weighted + fold(e * dp, jnp.sum))

        zero = jnp.zeros((8, n_q), jnp.float32)
        total, weighted = lax.fori_loop(first * per, last * per, second_pass, (zero, zero))
        inverse = 1.0 / jnp.sum(total, axis=0, keepdims=True)
        delta = jnp.sum(weighted, axis=0, keepdims=True) * inverse

        def third_pass(i, dqt):
            start = key_start(i)
            at = pl.ds(pl.multiple_of(i * KC, KC), KC)
            p = s_scr[at, :n_q] * inverse
            ds = (p * (p_scr[at, :n_q] - delta)).astype(jnp.bfloat16)
            pb = p.astype(jnp.bfloat16)
            here = pl.ds(start, KC)
            dvw[here, :] += jnp.dot(pb, grads, preferred_element_type=jnp.float32)
            dkw[here, :] += jnp.dot(ds, queries, preferred_element_type=jnp.float32)
            return dqt + jnp.dot(kt[:, here], ds, preferred_element_type=jnp.float32)

        dqt = lax.fori_loop(
            first * per, last * per, third_pass, jnp.zeros((HD, n_q), jnp.float32)
        )
        dqs[q_lo : q_lo + n_q, :] = jnp.transpose(dqt) * scale

    @pl.when(high == 1)
    def _():
        unit(0, both, 1, 0, both)
        unit(both, both, 2, 0, both)
        unit(2 * both, full, 3, 0, both)

    @pl.when(high == 0)
    def _():
        for ht in range(2):
            unit(ht * full, full, 1, ht * full, full)
            unit(both + ht * full, full, 2, ht * full, full)
            unit(2 * both + ht * half, half, 3, ht * full, full)

    def block(src, lo, cols):
        n = frames * cols * 8
        step = full
        x0 = src[lo : lo + n, :]
        x1 = src[lo + step : lo + step + n, :]
        shape = (frames, cols, 8, HD)
        return jnp.concatenate([x0.reshape(shape), x1.reshape(shape)], axis=2)

    def put(ref, lead, start, cols, x):
        ref[lead + (slice(None), pl.ds(start, cols), slice(None), slice(None))] = x.astype(ref.dtype)

    put(dq_ref, (), c_off, 8, block(dqs, 0, 8))
    put(dq_ref, (), b_off, 8, block(dqs, both, 8))
    shape = (frames, 4, 8, HD)
    tail = jnp.concatenate(
        [dqs[2 * both : 2 * both + half, :].reshape(shape),
         dqs[2 * both + half : 2 * both + full, :].reshape(shape)], axis=2)
    put(dq_ref, (), a_off, 4, tail)
    for which, src, factor in ((0, dkw, scale), (1, dvw, 1.0)):
        lead = (which,)
        put(far_out, lead, 0, 8, block(src, 0, 8) * factor)
        put(own_ref, lead, c_off, 8, block(src, both, 8) * factor)
        put(own_ref, lead, b_off, 8, block(src, 2 * both, 8) * factor)
        put(own_ref, lead, a_off, 4, block(src, 3 * both, 4) * factor)
        put(near_out, lead, mix_off, 4, block(src, 3 * both + half, 4) * factor)
        put(near_out, lead, out_off, 8, block(src, 4 * both, 8) * factor)


def attention(info, q, k, v, g, near, far, heads):
    frames, width, rows, _ = q.shape
    full = frames * 64
    own = pl.BlockSpec((frames, width, rows, HD), lambda h, *_: (0, 0, 0, h))

    def pair(cols):
        return pl.BlockSpec((2, frames, cols, rows, HD), lambda h, *_: (0, 0, 0, 0, h))

    channels = heads * HD
    shape = lambda n, dt: jax.ShapeDtypeStruct((2, frames, n, rows, channels), dt)
    return pl.pallas_call(
        attention_kernel,
        grid_spec=pltpu.PrefetchScalarGridSpec(
            num_scalar_prefetch=1,
            grid=(heads,),
            in_specs=[own, own, own, own, pair(12), pair(8)],
            out_specs=[own, pair(width), pair(12), pair(8)],
            scratch_shapes=[
                pltpu.VMEM((10 * full, HD), jnp.bfloat16),
                pltpu.VMEM((10 * full, HD), jnp.bfloat16),
                pltpu.VMEM((HD, 10 * full), jnp.bfloat16),
                pltpu.VMEM((5 * full, HD), jnp.bfloat16),
                pltpu.VMEM((5 * full, HD), jnp.bfloat16),
                pltpu.VMEM((5 * full, HD), jnp.float32),
                pltpu.VMEM((10 * full, HD), jnp.float32),
                pltpu.VMEM((10 * full, HD), jnp.float32),
                pltpu.VMEM((10 * full, 2 * full), jnp.float32),
                pltpu.VMEM((10 * full, 2 * full), jnp.float32),
            ],
        ),
        out_shape=[
            jax.ShapeDtypeStruct(q.shape, jnp.bfloat16),
            shape(width, jnp.float32),
            shape(12, jnp.bfloat16),
            shape(8, jnp.bfloat16),
        ],
        compiler_params=pltpu.CompilerParams(vmem_limit_bytes=60 * 1024 * 1024),
    )(info, q, k, v, g, near, far)


def quarter_body(queries, keys, values, out_grad, extents, counts):
    frames, rows, width, channels = queries.shape
    heads = channels // HD
    devices = lax.axis_size("sw")
    position = lax.axis_index("sw")
    shifted = position * width + LW // 2
    group = shifted // LW % HEAD_GROUPS
    place = shifted % LW // width
    parity = place % 2
    border = ((place == 0) | (place == 3)).astype(jnp.int32)
    edge = jnp.where(place == 0, 0, counts.shape[1] - 1)
    limits = lax.dynamic_slice_in_dim(counts, edge, 1, 1)[:, 0]
    radius = lax.dynamic_slice_in_dim((extents - 1) // 2, group * heads, heads, 0)
    info = jnp.concatenate(
        [jnp.stack([parity, border]).astype(jnp.int32), limits, radius.reshape(-1)]
    )
    q, k, v, g = [jnp.transpose(x, (0, 2, 1, 3)) for x in (queries, keys, values, out_grad)]
    first = LW // 2 // width
    near_route = []
    far_route = []
    for i in range(devices):
        at = (i + first) % 4
        near_route.append((i, i + 1 if at % 2 == 0 else i - 1))
        if at == 1:
            far_route.append((i, (i + 1) % devices))
        if at == 2:
            far_route.append((i, (i - 1) % devices))
    near_route = [(a, b % devices) for a, b in near_route]
    stacked = jnp.stack([k, v])
    near_own = lax.dynamic_slice_in_dim(stacked, 8 - 8 * parity, 12, 2)
    far_own = lax.dynamic_slice_in_dim(stacked, 12 * parity, 8, 2)
    near = lax.ppermute(near_own, "sw", near_route)
    far = lax.ppermute(far_own, "sw", far_route)
    dq, own, near_part, far_part = attention(info, q, k, v, g, near, far, heads)
    near_back = lax.ppermute(near_part, "sw", near_route)
    far_back = lax.ppermute(far_part, "sw", far_route)
    back = jnp.where(
        parity == 0,
        jnp.concatenate([far_back, near_back], axis=2),
        jnp.concatenate([near_back, far_back], axis=2),
    )
    total = (own + back.astype(jnp.float32)).astype(jnp.bfloat16)
    outs = (dq, total[0], total[1])
    return tuple(jnp.transpose(x, (0, 2, 1, 3)) for x in outs)


def from_behind(block, axis, distance):
    devices = range(lax.axis_size(axis))
    route = [((i - distance) % len(devices), i) for i in devices]
    return lax.ppermute(block, axis, route)


def layout(cols, counts, frames, rows):
    tile_rows, tile_cols = counts.shape
    col_tile = cols // TILE_W
    col_ok = (cols >= 0) & (cols < LW)
    safe = jnp.clip(col_tile, 0, tile_cols - 1)
    row_ids = jnp.arange(rows)
    frame_ids = jnp.arange(frames)
    row_tile = row_ids // TILE_H
    pick_rows = (row_tile[:, None] == jnp.arange(tile_rows)[None, :]).astype(jnp.int32)
    pick_cols = (safe[:, None] == jnp.arange(tile_cols)[None, :]).astype(jnp.int32)
    limit = jnp.dot(jnp.dot(pick_rows, counts), jnp.transpose(pick_cols))
    place = (frame_ids[:, None, None] * TILE_H + (row_ids % TILE_H)[None, :, None]) * TILE_W + (
        cols % TILE_W
    )[None, None, :]
    valid = col_ok[None, None, :] & (place < limit[None, :, :])
    shape = (frames, rows, cols.shape[0])
    flat_tile = jnp.broadcast_to(col_tile[None, None, :], shape).reshape(-1)
    flat_rowtile = jnp.broadcast_to(row_tile[None, :, None], shape).reshape(-1)
    flat_colok = jnp.broadcast_to(col_ok[None, None, :], shape).reshape(-1)
    return (flat_tile, flat_rowtile, flat_colok, valid.reshape(-1))


def contract_rows(left, right):
    return lax.dot_general(
        left, right, (((0,), (0,)), ((), ())), preferred_element_type=jnp.float32
    )


def contract_cols(left, right):
    return lax.dot_general(
        left, right, (((1,), (1,)), ((), ())), preferred_element_type=jnp.float32
    )


def near_keys_values(stacked, reach):
    pieces = []
    for step_by in range(reach, -reach - 1, -1):
        if step_by == 0:
            pieces.append(stacked)
        else:
            pieces.append(from_behind(stacked, "sw", step_by))
    return jnp.concatenate(pieces, axis=3)


def query_side(
    local_q, local_g, near_keys, near_values, width_gap, height_gap, key_ok, radius, scale
):
    heads = radius.shape[0]
    channels = local_q.shape[1]
    head_dim = channels // heads
    query_rows = local_q.shape[0]
    key_rows = near_keys.shape[0]

    def step(carry, head):
        column_start = head * head_dim
        head_query = lax.dynamic_slice_in_dim(local_q, column_start, head_dim, 1)
        head_grad = lax.dynamic_slice_in_dim(local_g, column_start, head_dim, 1)
        head_key = lax.dynamic_slice_in_dim(near_keys, column_start, head_dim, 1)
        head_value = lax.dynamic_slice_in_dim(near_values, column_start, head_dim, 1)
        allowed = key_ok[None, :] & (width_gap <= radius[head, 1]) & (height_gap <= radius[head, 0])
        scores = contract_cols(head_query, head_key) * scale
        masked = jnp.where(allowed, scores, -1e30)
        row_peak = jnp.max(masked, axis=1, keepdims=True)
        row_total = jnp.sum(
            jnp.where(allowed, jnp.exp(masked - row_peak), 0.0), axis=1, keepdims=True
        )
        log_total = row_peak + jnp.log(row_total)
        probs = jnp.exp(masked - log_total)
        probs_b = probs.astype(jnp.bfloat16)
        attended = jnp.dot(probs_b, head_value, preferred_element_type=jnp.float32)
        delta = jnp.sum(head_grad.astype(jnp.float32) * attended, axis=1, keepdims=True)
        dprobs = contract_cols(head_grad, head_value)
        dscores_b = (probs * (dprobs - delta)).astype(jnp.bfloat16)
        query_part = (
            jnp.dot(dscores_b, head_key, preferred_element_type=jnp.float32) * scale
        ).astype(jnp.bfloat16)
        query_acc = lax.dynamic_update_slice_in_dim(carry[0], query_part, column_start, 1)
        key_part = contract_rows(dscores_b, head_query) * scale
        value_part = contract_rows(probs_b, head_grad)
        key_acc = lax.dynamic_update_slice_in_dim(carry[1], key_part, column_start, 1)
        value_acc = lax.dynamic_update_slice_in_dim(carry[2], value_part, column_start, 1)
        return ((query_acc, key_acc, value_acc), None)

    query_init = jnp.zeros((query_rows, channels), jnp.bfloat16)
    init = (
        query_init,
        jnp.zeros((key_rows, channels), jnp.float32),
        jnp.zeros((key_rows, channels), jnp.float32),
    )
    result, unused = lax.scan(step, init, jnp.arange(heads))
    return result


def general_body(queries, keys, values, out_grad, extents, counts):
    frames, rows, width, channels = queries.shape
    group_heads = channels // HD
    scale = 1.0 / HD**0.5
    reach = (2 * TILE_W - 2 + width) // width
    rim_width = reach * width
    key_span = width + 2 * rim_width
    position = lax.axis_index("sw")
    shifted = position * width + LW // 2
    group = shifted // LW % HEAD_GROUPS
    own_start = shifted % LW
    radius = lax.dynamic_slice_in_dim((extents - 1) // 2, group * group_heads, group_heads, 0)
    near_cols = own_start - rim_width + jnp.arange(key_span)
    own_cols = own_start + jnp.arange(width)
    near_tile, near_rowtile, near_colok, near_ok = layout(near_cols, counts, frames, rows)
    own_tile, own_rowtile, own_colok, own_ok = layout(own_cols, counts, frames, rows)
    local_q = queries.reshape(-1, channels)
    local_g = out_grad.reshape(-1, channels)
    stacked = jnp.stack([keys, values])
    near = near_keys_values(stacked, reach)
    near_keys = near[0].reshape(-1, channels)
    near_values = near[1].reshape(-1, channels)
    width_gap = jnp.abs(own_tile[:, None] - near_tile[None, :])
    height_gap = jnp.abs(own_rowtile[:, None] - near_rowtile[None, :])
    query_grad, key_near, value_near = query_side(
        local_q, local_g, near_keys, near_values, width_gap, height_gap, near_ok, radius, scale
    )
    partial_value = jnp.stack(
        [
            key_near.reshape(frames, rows, key_span, channels),
            value_near.reshape(frames, rows, key_span, channels),
        ]
    )
    summed = lax.slice_in_dim(partial_value, rim_width, rim_width + width, axis=3)
    for step_by in range(-reach, reach + 1):
        if step_by != 0:
            piece = lax.slice_in_dim(
                partial_value,
                rim_width + step_by * width,
                rim_width + (step_by + 1) * width,
                axis=3,
            )
            summed = summed + from_behind(piece, "sw", step_by)
    key_grad = summed[0].astype(jnp.bfloat16)
    value_grad = summed[1].astype(jnp.bfloat16)
    return (query_grad.reshape(frames, rows, width, channels), key_grad, value_grad)


def body(queries, keys, values, out_grad, extents, counts):
    frames, rows, width, channels = queries.shape
    quarters = width == 20 and rows == 16 and LW == 4 * width and counts.shape[0] == 2
    chosen = quarter_body if quarters else general_body
    return chosen(queries, keys, values, out_grad, extents, counts)


def solution(mesh):
    placed = P("clips", None, "sw", None)
    return jax.shard_map(
        body,
        mesh=mesh,
        in_specs=(placed, placed, placed, placed, P(), P()),
        out_specs=(placed, placed, placed),
        check_vma=False,
    )
```

```python
import functools

import jax
import jax.numpy as jnp
from jax import lax
from jax.experimental import pallas as pl
from jax.experimental.pallas import tpu as pltpu
from jax.sharding import PartitionSpec as P

HD = 128
HEAD_GROUPS = 4
TILE_H = 8
TILE_W = 8
LW = 80
ROWS_A = 192
COLS_A = 256
ROWS_B = 768
LOG2E = 1.4426950408889634


def attend(role, n_q, n_half, border, high, wide, kw, vw, kt, qs, gs, dqs, dkw, dvw,
           s_scr, p_scr, peaks, totals, weights, dqt, bias):
    scale = 1.0 / HD**0.5
    rate = scale * LOG2E
    both = kw.shape[0] // 3
    full = both // 2

    identity = (
        lax.broadcasted_iota(jnp.int32, (HD, HD), 0) == lax.broadcasted_iota(jnp.int32, (HD, HD), 1)
    ).astype(jnp.float32).astype(jnp.bfloat16)
    for x in range(0, 3 * both, full):
        kt[:, x : x + full] = lax.dot_general(
            identity, kw[x : x + full, :], (((1,), (1,)), ((), ())),
            preferred_element_type=jnp.float32,
        ).astype(jnp.bfloat16)

    def unit(q_lo, n_q, key_lo, n_k):
        first = 1 - wide
        if role == "C":
            first = jnp.where(border == 1, 1, first)
        last = 2 + wide
        blocks = n_k // ROWS_A
        slices = [(x, min(COLS_A, n_q - x)) for x in range(0, n_q, COLS_A)]

        def products(w, masked):
            start = pl.multiple_of(w * both + key_lo, 128)
            for b in range(blocks):
                key_rows = pl.ds(start + b * ROWS_A, ROWS_A)
                to = pl.ds(pl.multiple_of(w * n_k, 128) + b * ROWS_A, ROWS_A)
                for x, n in slices:
                    s = lax.dot_general(
                        kw[key_rows, :], qs[q_lo + x : q_lo + x + n, :],
                        (((1,), (1,)), ((), ())), preferred_element_type=jnp.float32,
                    )
                    dp = lax.dot_general(
                        vw[key_rows, :], gs[q_lo + x : q_lo + x + n, :],
                        (((1,), (1,)), ((), ())), preferred_element_type=jnp.float32,
                    )
                    if masked:
                        off = bias[key_lo + b * ROWS_A : key_lo + (b + 1) * ROWS_A, :]
                        s = s + jnp.concatenate([off] * pl.cdiv(n, HD), axis=1)[:, :n]
                    s = s.reshape(ROWS_A // 8, 8, n)
                    peak = jnp.max(s, axis=0)
                    e = jnp.exp2(s * rate - peak * rate)
                    dp3 = dp.reshape(ROWS_A // 8, 8, n)
                    at = w * blocks + b
                    peaks[at, :, x : x + n] = peak
                    totals[at, :, x : x + n] = jnp.sum(e, axis=0)
                    weights[at, :, x : x + n] = jnp.sum(e * dp3, axis=0)
                    s_scr[to, x : x + n] = e.reshape(ROWS_A, n)
                    p_scr[to, x : x + n] = dp

        def plain_step(w, carry):
            products(w, False)
            return carry

        def masked_step(w, carry):
            products(w, True)
            return carry

        if role != "A":
            edge = 1 if role == "C" else 0
            split = jnp.where(border == 1, jnp.maximum(first, edge + 1), first)
            lax.fori_loop(first, split, masked_step, 0)
            lax.fori_loop(split, last, plain_step, 0)
        else:
            lax.fori_loop(first, last, plain_step, 0)

        low = first * blocks
        top_group = last * blocks
        wide_shape = (8, n_q)
        peak = lax.fori_loop(
            low, top_group, lambda i, c: jnp.maximum(c, peaks[i, :, :n_q]),
            jnp.full(wide_shape, -3e38, jnp.float32),
        )
        peak = jnp.max(peak, axis=0, keepdims=True)

        def combine(i, carry):
            total, weighted = carry
            f = jnp.exp2((peaks[i, :, :n_q] - peak) * rate)
            peaks[i, :, :n_q] = f
            return total + f * totals[i, :, :n_q], weighted + f * weights[i, :, :n_q]

        zero = jnp.zeros(wide_shape, jnp.float32)
        total, weighted = lax.fori_loop(low, top_group, combine, (zero, zero))
        inverse = 1.0 / jnp.sum(total, axis=0, keepdims=True)
        delta = jnp.sum(weighted, axis=0, keepdims=True) * inverse
        dqt[:, :n_q] = jnp.zeros((HD, n_q), jnp.float32)

        def gradients(w, carry):
            start = pl.multiple_of(w * both + key_lo, 128)
            base = pl.multiple_of(w * n_k, 128)
            size = ROWS_B if n_k % ROWS_B == 0 else n_k
            for b in range(n_k // size):
                here = pl.ds(pl.multiple_of(start + b * size, 128), size)
                pbs, dss = [], []
                for r in range(b * size, (b + 1) * size, ROWS_A):
                    f = peaks[w * blocks + r // ROWS_A, :, :n_q] * inverse
                    at = pl.ds(base + r, ROWS_A)
                    e = s_scr[at, :n_q].reshape(ROWS_A // 8, 8, n_q)
                    p = (e * f).reshape(ROWS_A, n_q)
                    dss.append((p * (p_scr[at, :n_q] - delta)).astype(jnp.bfloat16))
                    pbs.append(p.astype(jnp.bfloat16))
                pb = jnp.concatenate(pbs, axis=0)
                ds = jnp.concatenate(dss, axis=0)
                grads = gs[q_lo : q_lo + n_q, :]
                queries = qs[q_lo : q_lo + n_q, :]
                dvw[here, :] += jnp.dot(pb, grads, preferred_element_type=jnp.float32)
                dkw[here, :] += jnp.dot(ds, queries, preferred_element_type=jnp.float32)
                dqt[:, :n_q] += jnp.dot(kt[:, here], ds, preferred_element_type=jnp.float32)
            return carry

        lax.fori_loop(first, last, gradients, 0)
        dqs[q_lo : q_lo + n_q, :] = jnp.transpose(dqt[:, :n_q]) * scale

    @pl.when(high == 1)
    def _():
        unit(0, n_q, 0, both)

    @pl.when(high == 0)
    def _():
        for ht in range(2):
            unit(ht * n_half, n_half, ht * full, full)


def rows_of(ref, lead, start, cols, ht):
    block = ref[lead + (slice(None), pl.ds(start, cols), pl.ds(ht * 8, 8), slice(None))]
    n = block.shape[0] * cols * 8
    return block.astype(jnp.float32).reshape(n, HD).astype(jnp.bfloat16)


def block_of(src, lo, step, frames, cols):
    n = frames * cols * 8
    shape = (frames, cols, 8, HD)
    low = src[lo : lo + n, :].reshape(shape)
    return jnp.concatenate([low, src[lo + step : lo + step + n, :].reshape(shape)], axis=2)


def put(ref, lead, start, cols, x):
    ref[lead + (slice(None), pl.ds(start, cols), slice(None), slice(None))] = x.astype(ref.dtype)


def fill_bias(bias, info, full):
    at = lax.broadcasted_iota(jnp.int32, (full, HD), 0)
    t = at // 64
    c = at // 8 - t * 8
    r = at - at // 8 * 8
    place = t * 64 + r * 8 + c
    for ht in range(2):
        bias[ht * full : (ht + 1) * full, :] = jnp.where(place < info[2 + ht], 0.0, -1e30)


def flags(info):
    head = pl.program_id(0)
    return info[0], info[1], info[4 + 2 * head], info[5 + 2 * head]


def mixed_kernel(info, q_ref, g_ref, k_ref, v_ref, near_ref, dq_out, mix_out, mid_out, send_out,
                 *scratch):
    kw, vw, kt, qs, gs, dqs, dkw, dvw = scratch[:8]
    parity, border, high, wide = flags(info)
    scale = 1.0 / HD**0.5
    frames = q_ref.shape[0]
    full = frames * TILE_H * TILE_W
    half, both = full // 2, 2 * full
    b_off = parity * 0
    a_off = 8 - parity * 8
    b_off = parity * 4
    mix_off = parity * 8
    out_off = 4 - parity * 4
    for ht in range(2):
        for dst, src in ((qs, q_ref), (gs, g_ref)):
            dst[ht * half : (ht + 1) * half, :] = rows_of(src, (), 0, 4, ht)
        for which, dst, src in ((0, kw, k_ref), (1, vw, v_ref)):
            lo = ht * full
            dst[lo : lo + full, :] = rows_of(src, (), b_off, 8, ht)
            lo += both
            dst[lo : lo + half, :] = rows_of(src, (), a_off, 4, ht)
            dst[lo + half : lo + full, :] = rows_of(near_ref, (which,), mix_off, 4, ht)
            lo += both
            dst[lo : lo + full, :] = rows_of(near_ref, (which,), out_off, 8, ht)
    dkw[...] = jnp.zeros_like(dkw)
    dvw[...] = jnp.zeros_like(dvw)
    attend("A", full, half, border, high, wide, *scratch)
    put(dq_out, (), 0, 4, block_of(dqs, 0, half, frames, 4))
    for which, src, factor in ((0, dkw, scale), (1, dvw, 1.0)):
        mid_out[which, 0] = src[0:both, :]
        mix_out[which, 0] = src[both : 2 * both, :]
        put(send_out, (which,), 0, 8, block_of(src, 2 * both, full, frames, 8) * factor)


def outer_kernel(info, q_ref, g_ref, k_ref, v_ref, far_ref, mid_ref, dq_out, sum_out, send_out,
                 *scratch):
    kw, vw, kt, qs, gs, dqs, dkw, dvw = scratch[:8]
    bias = scratch[-1]
    parity, border, high, wide = flags(info)
    scale = 1.0 / HD**0.5
    frames = q_ref.shape[0]
    full = frames * TILE_H * TILE_W
    both = 2 * full
    c_off = parity * 8
    b_off = 8 - parity * 8
    for ht in range(2):
        for dst, src in ((qs, q_ref), (gs, g_ref)):
            dst[ht * full : (ht + 1) * full, :] = rows_of(src, (), 0, 8, ht)
        for which, dst, src in ((0, kw, k_ref), (1, vw, v_ref)):
            lo = ht * full
            dst[lo : lo + full, :] = rows_of(far_ref, (which,), 0, 8, ht)
            lo += both
            dst[lo : lo + full, :] = rows_of(src, (), c_off, 8, ht)
            lo += both
            dst[lo : lo + full, :] = rows_of(src, (), b_off, 8, ht)

    @pl.when((border == 1) & (pl.program_id(0) == 0))
    def _():
        fill_bias(bias, info, full)

    for which, dst in ((0, dkw), (1, dvw)):
        dst[0 : 2 * both, :] = jnp.zeros((2 * both, HD), jnp.float32)
        dst[2 * both :, :] = mid_ref[which, 0]
    attend("C", both, full, border, high, wide, *scratch)
    put(dq_out, (), 0, 8, block_of(dqs, 0, full, frames, 8))
    for which, src, factor in ((0, dkw, scale), (1, dvw, 1.0)):
        sum_out[which, 0] = src[both:, :]
        put(send_out, (which,), 0, 8, block_of(src, 0, full, frames, 8) * factor)


def inner_kernel(info, q_ref, g_ref, k_ref, v_ref, near_ref, sum_ref, mix_ref, dqa_ref, dqc_ref,
                 dq_out, own_out, send_out, *scratch):
    kw, vw, kt, qs, gs, dqs, dkw, dvw = scratch[:8]
    bias = scratch[-1]
    parity, border, high, wide = flags(info)
    scale = 1.0 / HD**0.5
    frames = q_ref.shape[0]
    full = frames * TILE_H * TILE_W
    half, both = full // 2, 2 * full
    c_off = parity * 12
    b_off = 8 - parity * 4
    a_off = 16 - parity * 16
    mix_off = parity * 8
    for ht in range(2):
        for dst, src in ((qs, q_ref), (gs, g_ref)):
            dst[ht * full : (ht + 1) * full, :] = rows_of(src, (), 0, 8, ht)
        for which, dst, src in ((0, kw, k_ref), (1, vw, v_ref)):
            lo = ht * full
            dst[lo : lo + full, :] = rows_of(src, (), c_off, 8, ht)
            lo += both
            dst[lo : lo + full, :] = rows_of(src, (), b_off, 8, ht)
            lo += both
            dst[lo : lo + half, :] = rows_of(src, (), a_off, 4, ht)
            dst[lo + half : lo + full, :] = rows_of(near_ref, (which,), mix_off, 4, ht)

    @pl.when((border == 1) & (pl.program_id(0) == 0))
    def _():
        fill_bias(bias, info, full)

    for which, dst in ((0, dkw), (1, dvw)):
        dst[0 : 2 * both, :] = sum_ref[which, 0]
        dst[2 * both :, :] = mix_ref[which, 0]
    attend("B", both, full, border, high, wide, *scratch)
    put(dq_out, (), b_off, 8, block_of(dqs, 0, full, frames, 8))
    put(dq_out, (), a_off, 4, dqa_ref[...])
    put(dq_out, (), c_off, 8, dqc_ref[...])
    for which, src, factor in ((0, dkw, scale), (1, dvw, 1.0)):
        lead = (which,)
        put(own_out, lead, c_off, 8, block_of(src, 0, full, frames, 8) * factor)
        put(own_out, lead, b_off, 8, block_of(src, both, full, frames, 8) * factor)
        put(own_out, lead, a_off, 4, block_of(src, 2 * both, full, frames, 4) * factor)
        put(send_out, lead, 0, 4, block_of(src, 2 * both + half, full, frames, 4) * factor)


def scratch_of(n_q, full):
    both = 2 * full
    groups = 3 * both // ROWS_A
    return [
        pltpu.VMEM((3 * both, HD), jnp.bfloat16),
        pltpu.VMEM((3 * both, HD), jnp.bfloat16),
        pltpu.VMEM((HD, 3 * both), jnp.bfloat16),
        pltpu.VMEM((n_q, HD), jnp.bfloat16),
        pltpu.VMEM((n_q, HD), jnp.bfloat16),
        pltpu.VMEM((n_q, HD), jnp.float32),
        pltpu.VMEM((3 * both, HD), jnp.float32),
        pltpu.VMEM((3 * both, HD), jnp.float32),
        pltpu.VMEM((3 * both, n_q), jnp.float32),
        pltpu.VMEM((3 * both, n_q), jnp.float32),
        pltpu.VMEM((groups, 8, n_q), jnp.float32),
        pltpu.VMEM((groups, 8, n_q), jnp.float32),
        pltpu.VMEM((groups, 8, n_q), jnp.float32),
        pltpu.VMEM((HD, n_q), jnp.float32),
        pltpu.VMEM((both, HD), jnp.float32),
    ]


def launch(kernel, name, n_q, full, heads, in_specs, out_specs, out_shape, args):
    flops = heads * 10 * n_q * 6 * full * HD
    return pl.pallas_call(
        kernel,
        name=name,
        grid_spec=pltpu.PrefetchScalarGridSpec(
            num_scalar_prefetch=1,
            grid=(heads,),
            in_specs=in_specs,
            out_specs=out_specs,
            scratch_shapes=scratch_of(n_q, full),
        ),
        out_shape=out_shape,
        compiler_params=pltpu.CompilerParams(vmem_limit_bytes=56 * 1024 * 1024),
        cost_estimate=pl.CostEstimate(
            flops=flops, transcendentals=flops // (10 * HD), bytes_accessed=8 << 20
        ),
    )(*args)


def column_block(frames, rows, cols, offset):
    if isinstance(offset, int):
        return pl.BlockSpec((frames, cols, rows, HD), lambda h, info: (0, offset, 0, h))
    return pl.BlockSpec(
        (pl.Element(frames), pl.Element(cols), pl.Element(rows), pl.Element(HD)),
        lambda h, info: (0, offset(info[0]), 0, h * HD),
    )


def attention_parts(info, q, k, v, g, near, heads):
    frames, width, rows, _ = q.shape
    full = frames * TILE_H * TILE_W
    both = 2 * full
    channels = heads * HD

    def pair(cols):
        return pl.BlockSpec((2, frames, cols, rows, HD), lambda h, info: (0, 0, 0, 0, h))

    def chain(n):
        return pl.BlockSpec((2, 1, n, HD), lambda h, info: (0, h, 0, 0))

    def columns(n, dtype=jnp.bfloat16):
        return jax.ShapeDtypeStruct((2, frames, n, rows, channels), dtype)

    def kept(n):
        return jax.ShapeDtypeStruct((2, heads, n, HD), jnp.float32)

    def dq_shape(n):
        return jax.ShapeDtypeStruct((frames, n, rows, channels), jnp.bfloat16)

    def at(cols, offset):
        return column_block(frames, rows, cols, offset)

    def mixed():
        a, ab = at(4, lambda p: 16 - 16 * p), at(12, lambda p: 8 - 8 * p)
        return launch(
            mixed_kernel, "mixed", full, full, heads,
            [a, a, ab, ab, pair(12)],
            [at(4, 0), chain(both), chain(both), pair(8)],
            [dq_shape(4), kept(both), kept(both), columns(8)],
            (info, q, g, k, v, near),
        )

    def outer(far, mid):
        c, cb = at(8, lambda p: 12 * p), at(16, lambda p: 4 * p)
        return launch(
            outer_kernel, "outer", both, full, heads,
            [c, c, cb, cb, pair(8), chain(both)],
            [at(8, 0), chain(2 * both), pair(8)],
            [dq_shape(8), kept(2 * both), columns(8)],
            (info, q, g, k, v, far, mid),
        )

    def inner(info, sums, mix, dqa, dqc):
        b, every = at(8, lambda p: 8 - 4 * p), at(width, 0)
        return launch(
            inner_kernel, "inner", both, full, heads,
            [b, b, every, every, pair(12), chain(2 * both), chain(both), at(4, 0), at(8, 0)],
            [every, pair(width), pair(4)],
            [dq_shape(width), columns(width, jnp.float32), columns(4)],
            (info, q, g, k, v, near, sums, mix, dqa, dqc),
        )

    return mixed, outer, inner


def attention(info, q, k, v, g, near, far, heads):
    mixed, outer, inner = attention_parts(info, q, k, v, g, near, heads)
    dqa, mix, mid, sent = mixed()
    dqc, sums, far_part = outer(far, mid)
    dq, own, last = inner(info, sums, mix, dqa, dqc)
    return dq, own, sent, far_part, last


def quarter_body(queries, keys, values, out_grad, extents, counts):
    frames, rows, width, channels = queries.shape
    heads = channels // HD
    devices = lax.axis_size("sw")
    position = lax.axis_index("sw")
    shifted = position * width + LW // 2
    group = shifted // LW % HEAD_GROUPS
    place = shifted % LW // width
    parity = place % 2
    border = ((place == 0) | (place == 3)).astype(jnp.int32)
    edge = jnp.where(place == 0, 0, counts.shape[1] - 1)
    limits = lax.dynamic_slice_in_dim(counts, edge, 1, 1)[:, 0]
    radius = lax.dynamic_slice_in_dim((extents - 1) // 2, group * heads, heads, 0)
    info = jnp.concatenate(
        [jnp.stack([parity, border]).astype(jnp.int32), limits, radius.reshape(-1)]
    )
    q, k, v, g = [jnp.transpose(x, (0, 2, 1, 3)) for x in (queries, keys, values, out_grad)]
    first = LW // 2 // width
    near_route = []
    far_route = []
    for i in range(devices):
        at = (i + first) % 4
        near_route.append((i, i + 1 if at % 2 == 0 else i - 1))
        if at == 1:
            far_route.append((i, (i + 1) % devices))
        if at == 2:
            far_route.append((i, (i - 1) % devices))
    near_route = [(a, b % devices) for a, b in near_route]
    stacked = jnp.stack([k, v])
    near_own = lax.dynamic_slice_in_dim(stacked, 8 - 8 * parity, 12, 2)
    far_own = lax.dynamic_slice_in_dim(stacked, 12 * parity, 8, 2)
    near = lax.ppermute(near_own, "sw", near_route)
    far = lax.ppermute(far_own, "sw", far_route)
    mixed, outer, inner = attention_parts(info, q, k, v, g, near, heads)
    dqa, mix, mid, sent = mixed()
    mid_back = lax.ppermute(sent, "sw", near_route)
    dqc, sums, far_part = outer(far, mid)
    far_back = lax.ppermute(far_part, "sw", far_route)
    dq, own, last = inner(info, sums, mix, dqa, dqc)
    edge_back = lax.ppermute(last, "sw", near_route)
    back = jnp.where(
        parity == 0,
        jnp.concatenate([far_back, mid_back, edge_back], axis=2),
        jnp.concatenate([edge_back, mid_back, far_back], axis=2),
    )
    total = (own + back.astype(jnp.float32)).astype(jnp.bfloat16)
    outs = (dq, total[0], total[1])
    return tuple(jnp.transpose(x, (0, 2, 1, 3)) for x in outs)


def from_behind(block, axis, distance):
    devices = range(lax.axis_size(axis))
    route = [((i - distance) % len(devices), i) for i in devices]
    return lax.ppermute(block, axis, route)


def layout(cols, counts, frames, rows):
    tile_rows, tile_cols = counts.shape
    col_tile = cols // TILE_W
    col_ok = (cols >= 0) & (cols < LW)
    safe = jnp.clip(col_tile, 0, tile_cols - 1)
    row_ids = jnp.arange(rows)
    frame_ids = jnp.arange(frames)
    row_tile = row_ids // TILE_H
    pick_rows = (row_tile[:, None] == jnp.arange(tile_rows)[None, :]).astype(jnp.int32)
    pick_cols = (safe[:, None] == jnp.arange(tile_cols)[None, :]).astype(jnp.int32)
    limit = jnp.dot(jnp.dot(pick_rows, counts), jnp.transpose(pick_cols))
    place = (frame_ids[:, None, None] * TILE_H + (row_ids % TILE_H)[None, :, None]) * TILE_W + (
        cols % TILE_W
    )[None, None, :]
    valid = col_ok[None, None, :] & (place < limit[None, :, :])
    shape = (frames, rows, cols.shape[0])
    flat_tile = jnp.broadcast_to(col_tile[None, None, :], shape).reshape(-1)
    flat_rowtile = jnp.broadcast_to(row_tile[None, :, None], shape).reshape(-1)
    flat_colok = jnp.broadcast_to(col_ok[None, None, :], shape).reshape(-1)
    return (flat_tile, flat_rowtile, flat_colok, valid.reshape(-1))


def contract_rows(left, right):
    return lax.dot_general(
        left, right, (((0,), (0,)), ((), ())), preferred_element_type=jnp.float32
    )


def contract_cols(left, right):
    return lax.dot_general(
        left, right, (((1,), (1,)), ((), ())), preferred_element_type=jnp.float32
    )


def near_keys_values(stacked, reach):
    pieces = []
    for step_by in range(reach, -reach - 1, -1):
        if step_by == 0:
            pieces.append(stacked)
        else:
            pieces.append(from_behind(stacked, "sw", step_by))
    return jnp.concatenate(pieces, axis=3)


def query_side(
    local_q, local_g, near_keys, near_values, width_gap, height_gap, key_ok, radius, scale
):
    heads = radius.shape[0]
    channels = local_q.shape[1]
    head_dim = channels // heads
    query_rows = local_q.shape[0]
    key_rows = near_keys.shape[0]

    def step(carry, head):
        column_start = head * head_dim
        head_query = lax.dynamic_slice_in_dim(local_q, column_start, head_dim, 1)
        head_grad = lax.dynamic_slice_in_dim(local_g, column_start, head_dim, 1)
        head_key = lax.dynamic_slice_in_dim(near_keys, column_start, head_dim, 1)
        head_value = lax.dynamic_slice_in_dim(near_values, column_start, head_dim, 1)
        allowed = key_ok[None, :] & (width_gap <= radius[head, 1]) & (height_gap <= radius[head, 0])
        scores = contract_cols(head_query, head_key) * scale
        masked = jnp.where(allowed, scores, -1e30)
        row_peak = jnp.max(masked, axis=1, keepdims=True)
        row_total = jnp.sum(
            jnp.where(allowed, jnp.exp(masked - row_peak), 0.0), axis=1, keepdims=True
        )
        log_total = row_peak + jnp.log(row_total)
        probs = jnp.exp(masked - log_total)
        probs_b = probs.astype(jnp.bfloat16)
        attended = jnp.dot(probs_b, head_value, preferred_element_type=jnp.float32)
        delta = jnp.sum(head_grad.astype(jnp.float32) * attended, axis=1, keepdims=True)
        dprobs = contract_cols(head_grad, head_value)
        dscores_b = (probs * (dprobs - delta)).astype(jnp.bfloat16)
        query_part = (
            jnp.dot(dscores_b, head_key, preferred_element_type=jnp.float32) * scale
        ).astype(jnp.bfloat16)
        query_acc = lax.dynamic_update_slice_in_dim(carry[0], query_part, column_start, 1)
        key_part = contract_rows(dscores_b, head_query) * scale
        value_part = contract_rows(probs_b, head_grad)
        key_acc = lax.dynamic_update_slice_in_dim(carry[1], key_part, column_start, 1)
        value_acc = lax.dynamic_update_slice_in_dim(carry[2], value_part, column_start, 1)
        return ((query_acc, key_acc, value_acc), None)

    query_init = jnp.zeros((query_rows, channels), jnp.bfloat16)
    init = (
        query_init,
        jnp.zeros((key_rows, channels), jnp.float32),
        jnp.zeros((key_rows, channels), jnp.float32),
    )
    result, unused = lax.scan(step, init, jnp.arange(heads))
    return result


def general_body(queries, keys, values, out_grad, extents, counts):
    frames, rows, width, channels = queries.shape
    group_heads = channels // HD
    scale = 1.0 / HD**0.5
    reach = (2 * TILE_W - 2 + width) // width
    rim_width = reach * width
    key_span = width + 2 * rim_width
    position = lax.axis_index("sw")
    shifted = position * width + LW // 2
    group = shifted // LW % HEAD_GROUPS
    own_start = shifted % LW
    radius = lax.dynamic_slice_in_dim((extents - 1) // 2, group * group_heads, group_heads, 0)
    near_cols = own_start - rim_width + jnp.arange(key_span)
    own_cols = own_start + jnp.arange(width)
    near_tile, near_rowtile, near_colok, near_ok = layout(near_cols, counts, frames, rows)
    own_tile, own_rowtile, own_colok, own_ok = layout(own_cols, counts, frames, rows)
    local_q = queries.reshape(-1, channels)
    local_g = out_grad.reshape(-1, channels)
    stacked = jnp.stack([keys, values])
    near = near_keys_values(stacked, reach)
    near_keys = near[0].reshape(-1, channels)
    near_values = near[1].reshape(-1, channels)
    width_gap = jnp.abs(own_tile[:, None] - near_tile[None, :])
    height_gap = jnp.abs(own_rowtile[:, None] - near_rowtile[None, :])
    query_grad, key_near, value_near = query_side(
        local_q, local_g, near_keys, near_values, width_gap, height_gap, near_ok, radius, scale
    )
    partial_value = jnp.stack(
        [
            key_near.reshape(frames, rows, key_span, channels),
            value_near.reshape(frames, rows, key_span, channels),
        ]
    )
    summed = lax.slice_in_dim(partial_value, rim_width, rim_width + width, axis=3)
    for step_by in range(-reach, reach + 1):
        if step_by != 0:
            piece = lax.slice_in_dim(
                partial_value,
                rim_width + step_by * width,
                rim_width + (step_by + 1) * width,
                axis=3,
            )
            summed = summed + from_behind(piece, "sw", step_by)
    key_grad = summed[0].astype(jnp.bfloat16)
    value_grad = summed[1].astype(jnp.bfloat16)
    return (query_grad.reshape(frames, rows, width, channels), key_grad, value_grad)


def body(queries, keys, values, out_grad, extents, counts):
    frames, rows, width, channels = queries.shape
    quarters = width == 20 and rows == 16 and LW == 4 * width and counts.shape[0] == 2
    chosen = quarter_body if quarters else general_body
    return chosen(queries, keys, values, out_grad, extents, counts)


def solution(mesh):
    placed = P("clips", None, "sw", None)
    return jax.shard_map(
        body,
        mesh=mesh,
        in_specs=(placed, placed, placed, placed, P(), P()),
        out_specs=(placed, placed, placed),
        check_vma=False,
    )
```

```python
import functools

import jax
import jax.numpy as jnp
from jax import lax
from jax.experimental import pallas as pl
from jax.experimental.pallas import tpu as pltpu
from jax.sharding import PartitionSpec as P

HD = 128
HEAD_GROUPS = 4
TILE_H = 8
TILE_W = 8
LW = 80
ROWS_A = 192
COLS_A = 256
LOG2E = 1.4426950408889634


def attend(role, n_q, n_half, border, high, wide, kw, vw, qs, gs, dqs, dkw, dvw,
           s_scr, p_scr, peaks, totals, weights, dqt, bias):
    scale = 1.0 / HD**0.5
    rate = scale * LOG2E
    both = kw.shape[0] // 3
    full = both // 2

    def unit(subs, n_q, n_k):
        first = 1 - wide
        if role == "C":
            first = jnp.where(border == 1, 1, first)
        last = 2 + wide
        blocks = n_k // ROWS_A
        slices = [(x, min(COLS_A, n_q - x)) for x in range(0, n_q, COLS_A)]

        def products(w, masked):
            for q_lo, col, key_lo in subs:
                start = pl.multiple_of(w * both + key_lo, 128)
                for b in range(blocks):
                    key_rows = pl.ds(start + b * ROWS_A, ROWS_A)
                    to = pl.ds(pl.multiple_of(w * n_k, 128) + b * ROWS_A, ROWS_A)
                    for x, n in slices:
                        s = lax.dot_general(
                            kw[key_rows, :], qs[q_lo + x : q_lo + x + n, :],
                            (((1,), (1,)), ((), ())), preferred_element_type=jnp.float32,
                        )
                        dp = lax.dot_general(
                            vw[key_rows, :], gs[q_lo + x : q_lo + x + n, :],
                            (((1,), (1,)), ((), ())), preferred_element_type=jnp.float32,
                        )
                        if masked:
                            off = bias[key_lo + b * ROWS_A : key_lo + (b + 1) * ROWS_A, :]
                            s = s + jnp.concatenate([off] * pl.cdiv(n, HD), axis=1)[:, :n]
                        s = s.reshape(ROWS_A // 8, 8, n)
                        peak = jnp.max(s, axis=0)
                        e = jnp.exp2(s * rate - peak * rate)
                        dp3 = dp.reshape(ROWS_A // 8, 8, n)
                        at = w * blocks + b
                        here = slice(col + x, col + x + n)
                        peaks[at, :, here] = peak
                        totals[at, :, here] = jnp.sum(e, axis=0)
                        weights[at, :, here] = jnp.sum(e * dp3, axis=0)
                        s_scr[to, here] = e.reshape(ROWS_A, n)
                        p_scr[to, here] = dp

        def plain_step(w, carry):
            products(w, False)
            return carry

        def masked_step(w, carry):
            products(w, True)
            return carry

        split = first
        if role != "A":
            edge = 1 if role == "C" else 0
            split = jnp.where(border == 1, jnp.maximum(first, edge + 1), first)
            lax.fori_loop(first, split, masked_step, 0)
        lax.fori_loop(split, last, plain_step, 0)

        low = first * blocks
        top_group = last * blocks
        cols = [slice(col, col + n_q) for _, col, _ in subs]

        def highest(i, carry):
            return tuple(jnp.maximum(c, peaks[i, :, x]) for c, x in zip(carry, cols))

        start_peak = jnp.full((8, n_q), -3e38, jnp.float32)
        tops = lax.fori_loop(low, top_group, highest, tuple(start_peak for _ in subs))
        tops = [jnp.max(top, axis=0, keepdims=True) for top in tops]

        def combine(i, carry):
            out = []
            for (total, weighted), top, x in zip(carry, tops, cols):
                f = jnp.exp2((peaks[i, :, x] - top) * rate)
                peaks[i, :, x] = f
                out.append((total + f * totals[i, :, x], weighted + f * weights[i, :, x]))
            return tuple(out)

        zero = jnp.zeros((8, n_q), jnp.float32)
        sums = lax.fori_loop(low, top_group, combine, tuple((zero, zero) for _ in subs))
        inverses = [1.0 / jnp.sum(total, axis=0, keepdims=True) for total, _ in sums]
        deltas = [
            jnp.sum(weighted, axis=0, keepdims=True) * inverse
            for (_, weighted), inverse in zip(sums, inverses)
        ]
        for x in cols:
            dqt[:, x] = jnp.zeros((HD, n_q), jnp.float32)

        def gradients(w, carry):
            base = pl.multiple_of(w * n_k, 128)
            for (q_lo, col, key_lo), inverse, delta, x in zip(subs, inverses, deltas, cols):
                here = pl.ds(pl.multiple_of(w * both + key_lo, 128), n_k)
                pbs, dss = [], []
                for r in range(0, n_k, ROWS_A):
                    f = peaks[w * blocks + r // ROWS_A, :, x] * inverse
                    at = pl.ds(base + r, ROWS_A)
                    e = s_scr[at, x].reshape(ROWS_A // 8, 8, n_q)
                    p = (e * f).reshape(ROWS_A, n_q)
                    dss.append((p * (p_scr[at, x] - delta)).astype(jnp.bfloat16))
                    pbs.append(p.astype(jnp.bfloat16))
                pb = jnp.concatenate(pbs, axis=0)
                ds = jnp.concatenate(dss, axis=0)
                grads = gs[q_lo : q_lo + n_q, :]
                queries = qs[q_lo : q_lo + n_q, :]
                dvw[here, :] += jnp.dot(pb, grads, preferred_element_type=jnp.float32)
                dkw[here, :] += jnp.dot(ds, queries, preferred_element_type=jnp.float32)
                dqt[:, x] += lax.dot_general(
                    kw[here, :], ds, (((0,), (0,)), ((), ())), preferred_element_type=jnp.float32
                )
            return carry

        lax.fori_loop(first, last, gradients, 0)
        for (q_lo, _, _), x in zip(subs, cols):
            dqs[q_lo : q_lo + n_q, :] = jnp.transpose(dqt[:, x]) * scale

    @pl.when(high == 1)
    def _():
        unit([(0, 0, 0)], n_q, both)

    @pl.when(high == 0)
    def _():
        step = (n_half + HD - 1) // HD * HD
        unit([(ht * n_half, ht * step, ht * full) for ht in range(2)], n_half, full)


def rows_of(ref, lead, start, cols, ht):
    block = ref[lead + (slice(None), pl.ds(start, cols), pl.ds(ht * 8, 8), slice(None))]
    n = block.shape[0] * cols * 8
    return block.astype(jnp.float32).reshape(n, HD).astype(jnp.bfloat16)


def block_of(src, lo, step, frames, cols):
    n = frames * cols * 8
    shape = (frames, cols, 8, HD)
    low = src[lo : lo + n, :].reshape(shape)
    return jnp.concatenate([low, src[lo + step : lo + step + n, :].reshape(shape)], axis=2)


def put(ref, lead, start, cols, x):
    ref[lead + (slice(None), pl.ds(start, cols), slice(None), slice(None))] = x.astype(ref.dtype)


def fill_bias(bias, info, full):
    at = lax.broadcasted_iota(jnp.int32, (full, HD), 0)
    t = at // 64
    c = at // 8 - t * 8
    r = at - at // 8 * 8
    place = t * 64 + r * 8 + c
    for ht in range(2):
        bias[ht * full : (ht + 1) * full, :] = jnp.where(place < info[2 + ht], 0.0, -1e30)


def flags(info):
    head = pl.program_id(0)
    return info[0], info[1], info[4 + 2 * head], info[5 + 2 * head]


def mixed_kernel(info, q_ref, g_ref, k_ref, v_ref, nk_ref, nv_ref, dq_out, mix_out, mid_out, send_out,
                 *scratch):
    kw, vw, qs, gs, dqs, dkw, dvw = scratch[:7]
    parity, border, high, wide = flags(info)
    scale = 1.0 / HD**0.5
    frames = q_ref.shape[0]
    full = frames * TILE_H * TILE_W
    half, both = full // 2, 2 * full
    b_off = parity * 0
    a_off = 8 - parity * 8
    b_off = parity * 4
    mix_off = parity * 8
    out_off = 4 - parity * 4
    for ht in range(2):
        for dst, src in ((qs, q_ref), (gs, g_ref)):
            dst[ht * half : (ht + 1) * half, :] = rows_of(src, (), 0, 4, ht)
        for dst, src, near_ref in ((kw, k_ref, nk_ref), (vw, v_ref, nv_ref)):
            lo = ht * full
            dst[lo : lo + full, :] = rows_of(src, (), b_off, 8, ht)
            lo += both
            dst[lo : lo + half, :] = rows_of(src, (), a_off, 4, ht)
            dst[lo + half : lo + full, :] = rows_of(near_ref, (), mix_off, 4, ht)
            lo += both
            dst[lo : lo + full, :] = rows_of(near_ref, (), out_off, 8, ht)
    dkw[...] = jnp.zeros_like(dkw)
    dvw[...] = jnp.zeros_like(dvw)
    attend("A", full, half, border, high, wide, *scratch)
    put(dq_out, (), 0, 4, block_of(dqs, 0, half, frames, 4))
    for which, src, factor in ((0, dkw, scale), (1, dvw, 1.0)):
        mid_out[which, 0] = src[0:both, :].astype(mid_out.dtype)
        mix_out[which, 0] = src[both : 2 * both, :].astype(mix_out.dtype)
        put(send_out, (which,), 0, 8, block_of(src, 2 * both, full, frames, 8) * factor)


def outer_kernel(info, q_ref, g_ref, k_ref, v_ref, far_ref, mid_ref, dq_out, sum_out, send_out,
                 *scratch):
    kw, vw, qs, gs, dqs, dkw, dvw = scratch[:7]
    bias = scratch[-1]
    parity, border, high, wide = flags(info)
    scale = 1.0 / HD**0.5
    frames = q_ref.shape[0]
    full = frames * TILE_H * TILE_W
    both = 2 * full
    c_off = parity * 8
    b_off = 8 - parity * 8
    for ht in range(2):
        for dst, src in ((qs, q_ref), (gs, g_ref)):
            dst[ht * full : (ht + 1) * full, :] = rows_of(src, (), 0, 8, ht)
        for which, dst, src in ((0, kw, k_ref), (1, vw, v_ref)):
            lo = ht * full
            dst[lo : lo + full, :] = rows_of(far_ref, (which,), 0, 8, ht)
            lo += both
            dst[lo : lo + full, :] = rows_of(src, (), c_off, 8, ht)
            lo += both
            dst[lo : lo + full, :] = rows_of(src, (), b_off, 8, ht)

    @pl.when((border == 1) & (pl.program_id(0) == 0))
    def _():
        fill_bias(bias, info, full)

    for which, dst in ((0, dkw), (1, dvw)):
        dst[0 : 2 * both, :] = jnp.zeros((2 * both, HD), jnp.float32)
        dst[2 * both :, :] = mid_ref[which, 0].astype(jnp.float32)
    attend("C", both, full, border, high, wide, *scratch)
    put(dq_out, (), 0, 8, block_of(dqs, 0, full, frames, 8))
    for which, src, factor in ((0, dkw, scale), (1, dvw, 1.0)):
        sum_out[which, 0] = src[both:, :].astype(sum_out.dtype)
        put(send_out, (which,), 0, 8, block_of(src, 0, full, frames, 8) * factor)


def inner_kernel(info, q_ref, g_ref, k_ref, v_ref, nk_ref, nv_ref, sum_ref, mix_ref, dqa_ref, dqc_ref,
                 dq_out, dk_out, dv_out, send_out, *scratch):
    kw, vw, qs, gs, dqs, dkw, dvw = scratch[:7]
    bias = scratch[-1]
    parity, border, high, wide = flags(info)
    scale = 1.0 / HD**0.5
    frames = q_ref.shape[0]
    full = frames * TILE_H * TILE_W
    half, both = full // 2, 2 * full
    c_off = parity * 12
    b_off = 8 - parity * 4
    a_off = 16 - parity * 16
    for ht in range(2):
        for dst, src in ((qs, q_ref), (gs, g_ref)):
            dst[ht * full : (ht + 1) * full, :] = rows_of(src, (), 0, 8, ht)
        for dst, src, near_ref in ((kw, k_ref, nk_ref), (vw, v_ref, nv_ref)):
            lo = ht * full
            dst[lo : lo + full, :] = rows_of(src, (), c_off, 8, ht)
            lo += both
            dst[lo : lo + full, :] = rows_of(src, (), b_off, 8, ht)
            lo += both
            dst[lo : lo + half, :] = rows_of(src, (), a_off, 4, ht)
            dst[lo + half : lo + full, :] = rows_of(near_ref, (), 0, 4, ht)

    @pl.when((border == 1) & (pl.program_id(0) == 0))
    def _():
        fill_bias(bias, info, full)

    for which, dst in ((0, dkw), (1, dvw)):
        dst[0 : 2 * both, :] = sum_ref[which, 0].astype(jnp.float32)
        dst[2 * both :, :] = mix_ref[which, 0].astype(jnp.float32)
    attend("B", both, full, border, high, wide, *scratch)
    put(dq_out, (), b_off, 8, block_of(dqs, 0, full, frames, 8))
    put(dq_out, (), a_off, 4, dqa_ref[...])
    put(dq_out, (), c_off, 8, dqc_ref[...])
    for which, src, factor, own_out in ((0, dkw, scale, dk_out), (1, dvw, 1.0, dv_out)):
        lead = ()
        put(own_out, lead, c_off, 8, block_of(src, 0, full, frames, 8) * factor)
        put(own_out, lead, b_off, 8, block_of(src, both, full, frames, 8) * factor)
        put(own_out, lead, a_off, 4, block_of(src, 2 * both, full, frames, 4) * factor)
        put(send_out, (which,), 0, 4, block_of(src, 2 * both + half, full, frames, 4) * factor)


def scratch_of(n_q, full):
    both = 2 * full
    groups = 3 * both // ROWS_A
    n_c = 2 * ((n_q // 2 + HD - 1) // HD * HD)
    return [
        pltpu.VMEM((3 * both, HD), jnp.bfloat16),
        pltpu.VMEM((3 * both, HD), jnp.bfloat16),
        pltpu.VMEM((n_q, HD), jnp.bfloat16),
        pltpu.VMEM((n_q, HD), jnp.bfloat16),
        pltpu.VMEM((n_q, HD), jnp.float32),
        pltpu.VMEM((3 * both, HD), jnp.float32),
        pltpu.VMEM((3 * both, HD), jnp.float32),
        pltpu.VMEM((3 * both, n_c), jnp.float32),
        pltpu.VMEM((3 * both, n_c), jnp.float32),
        pltpu.VMEM((groups, 8, n_c), jnp.float32),
        pltpu.VMEM((groups, 8, n_c), jnp.float32),
        pltpu.VMEM((groups, 8, n_c), jnp.float32),
        pltpu.VMEM((HD, n_c), jnp.float32),
        pltpu.VMEM((both, HD), jnp.float32),
    ]


def launch(kernel, name, n_q, full, heads, in_specs, out_specs, out_shape, args):
    flops = heads * 10 * n_q * 6 * full * HD
    return pl.pallas_call(
        kernel,
        name=name,
        grid_spec=pltpu.PrefetchScalarGridSpec(
            num_scalar_prefetch=1,
            grid=(heads,),
            in_specs=in_specs,
            out_specs=out_specs,
            scratch_shapes=scratch_of(n_q, full),
        ),
        out_shape=out_shape,
        compiler_params=pltpu.CompilerParams(vmem_limit_bytes=60 * 1024 * 1024),
        cost_estimate=pl.CostEstimate(
            flops=flops, transcendentals=flops // (10 * HD), bytes_accessed=8 << 20
        ),
    )(*args)


def column_block(frames, rows, cols, offset):
    if isinstance(offset, int):
        return pl.BlockSpec((frames, cols, rows, HD), lambda h, info: (0, offset, 0, h))
    return pl.BlockSpec(
        (pl.Element(frames), pl.Element(cols), pl.Element(rows), pl.Element(HD)),
        lambda h, info: (0, offset(info[0]), 0, h * HD),
    )


def attention_parts(info, q, k, v, g, near_k, near_v, heads):
    frames, width, rows, _ = q.shape
    full = frames * TILE_H * TILE_W
    both = 2 * full
    channels = heads * HD

    def pair(cols):
        return pl.BlockSpec((2, frames, cols, rows, HD), lambda h, info: (0, 0, 0, 0, h))

    def chain(n):
        return pl.BlockSpec((2, 1, n, HD), lambda h, info: (0, h, 0, 0))

    def columns(n, dtype=jnp.bfloat16):
        return jax.ShapeDtypeStruct((2, frames, n, rows, channels), dtype)

    def kept(n):
        return jax.ShapeDtypeStruct((2, heads, n, HD), jnp.bfloat16)

    def dq_shape(n):
        return jax.ShapeDtypeStruct((frames, n, rows, channels), jnp.bfloat16)

    def at(cols, offset):
        return column_block(frames, rows, cols, offset)

    def mixed():
        a, ab, nb = at(4, lambda p: 16 - 16 * p), at(12, lambda p: 8 - 8 * p), at(12, lambda p: 8 * p)
        return launch(
            mixed_kernel, "mixed", full, full, heads,
            [a, a, ab, ab, nb, nb],
            [at(4, 0), chain(both), chain(both), pair(8)],
            [dq_shape(4), kept(both), kept(both), columns(8)],
            (info, q, g, k, v, near_k, near_v),
        )

    def outer(far, mid):
        c, cb = at(8, lambda p: 12 * p), at(16, lambda p: 4 * p)
        return launch(
            outer_kernel, "outer", both, full, heads,
            [c, c, cb, cb, pair(8), chain(both)],
            [at(8, 0), chain(2 * both), pair(8)],
            [dq_shape(8), kept(2 * both), columns(8)],
            (info, q, g, k, v, far, mid),
        )

    def inner(info, sums, mix, dqa, dqc):
        b, every, na = at(8, lambda p: 8 - 4 * p), at(width, 0), at(4, lambda p: 16 * p)
        return launch(
            inner_kernel, "inner", both, full, heads,
            [b, b, every, every, na, na, chain(2 * both), chain(both), at(4, 0), at(8, 0)],
            [every, every, every, pair(4)],
            [dq_shape(width), dq_shape(width), dq_shape(width), columns(4)],
            (info, q, g, k, v, near_k, near_v, sums, mix, dqa, dqc),
        )

    return mixed, outer, inner


def attention(info, q, k, v, g, near, far, heads):
    mixed, outer, inner = attention_parts(info, q, k, v, g, k, v, heads)
    dqa, mix, mid, sent = mixed()
    dqc, sums, far_part = outer(far, mid)
    return tuple(inner(info, sums, mix, dqa, dqc)) + (sent, far_part)


def quarter_body(queries, keys, values, out_grad, extents, counts):
    frames, rows, width, channels = queries.shape
    heads = channels // HD
    devices = lax.axis_size("sw")
    position = lax.axis_index("sw")
    shifted = position * width + LW // 2
    group = shifted // LW % HEAD_GROUPS
    place = shifted % LW // width
    parity = place % 2
    border = ((place == 0) | (place == 3)).astype(jnp.int32)
    edge = jnp.where(place == 0, 0, counts.shape[1] - 1)
    limits = lax.dynamic_slice_in_dim(counts, edge, 1, 1)[:, 0]
    radius = lax.dynamic_slice_in_dim((extents - 1) // 2, group * heads, heads, 0)
    info = jnp.concatenate(
        [jnp.stack([parity, border]).astype(jnp.int32), limits, radius.reshape(-1)]
    )
    q, k, v, g = [jnp.transpose(x, (0, 2, 1, 3)) for x in (queries, keys, values, out_grad)]
    first = LW // 2 // width
    near_route = []
    far_route = []
    for i in range(devices):
        at = (i + first) % 4
        near_route.append((i, i + 1 if at % 2 == 0 else i - 1))
        if at == 1:
            far_route.append((i, (i + 1) % devices))
        if at == 2:
            far_route.append((i, (i - 1) % devices))
    near_route = [(a, b % devices) for a, b in near_route]
    near_k = lax.ppermute(k, "sw", near_route)
    near_v = lax.ppermute(v, "sw", near_route)
    far_own = jnp.stack([lax.dynamic_slice_in_dim(x, 12 * parity, 8, 1) for x in (k, v)])
    far = lax.ppermute(far_own, "sw", far_route)
    mixed, outer, inner = attention_parts(info, q, k, v, g, near_k, near_v, heads)
    dqa, mix, mid, sent = mixed()
    mid_back = lax.ppermute(sent, "sw", near_route)
    dqc, sums, far_part = outer(far, mid)
    far_back = lax.ppermute(far_part, "sw", far_route)
    dq, dk, dv, last = inner(info, sums, mix, dqa, dqc)
    edge_back = lax.ppermute(last, "sw", near_route)
    outs = [dq]
    for which, own in ((0, dk), (1, dv)):
        parts = ((8 - 4 * parity, mid_back), (12 * parity, far_back), (16 - 16 * parity, edge_back))
        for start, back in parts:
            got = back[which]
            held = lax.dynamic_slice_in_dim(own, start, got.shape[1], 1)
            both = held.astype(jnp.float32) + got.astype(jnp.float32)
            own = lax.dynamic_update_slice_in_dim(own, both.astype(jnp.bfloat16), start, 1)
        outs.append(own)
    return tuple(jnp.transpose(x, (0, 2, 1, 3)) for x in outs)


def from_behind(block, axis, distance):
    devices = range(lax.axis_size(axis))
    route = [((i - distance) % len(devices), i) for i in devices]
    return lax.ppermute(block, axis, route)


def layout(cols, counts, frames, rows):
    tile_rows, tile_cols = counts.shape
    col_tile = cols // TILE_W
    col_ok = (cols >= 0) & (cols < LW)
    safe = jnp.clip(col_tile, 0, tile_cols - 1)
    row_ids = jnp.arange(rows)
    frame_ids = jnp.arange(frames)
    row_tile = row_ids // TILE_H
    pick_rows = (row_tile[:, None] == jnp.arange(tile_rows)[None, :]).astype(jnp.int32)
    pick_cols = (safe[:, None] == jnp.arange(tile_cols)[None, :]).astype(jnp.int32)
    limit = jnp.dot(jnp.dot(pick_rows, counts), jnp.transpose(pick_cols))
    place = (frame_ids[:, None, None] * TILE_H + (row_ids % TILE_H)[None, :, None]) * TILE_W + (
        cols % TILE_W
    )[None, None, :]
    valid = col_ok[None, None, :] & (place < limit[None, :, :])
    shape = (frames, rows, cols.shape[0])
    flat_tile = jnp.broadcast_to(col_tile[None, None, :], shape).reshape(-1)
    flat_rowtile = jnp.broadcast_to(row_tile[None, :, None], shape).reshape(-1)
    flat_colok = jnp.broadcast_to(col_ok[None, None, :], shape).reshape(-1)
    return (flat_tile, flat_rowtile, flat_colok, valid.reshape(-1))


def contract_rows(left, right):
    return lax.dot_general(
        left, right, (((0,), (0,)), ((), ())), preferred_element_type=jnp.float32
    )


def contract_cols(left, right):
    return lax.dot_general(
        left, right, (((1,), (1,)), ((), ())), preferred_element_type=jnp.float32
    )


def near_keys_values(stacked, reach):
    pieces = []
    for step_by in range(reach, -reach - 1, -1):
        if step_by == 0:
            pieces.append(stacked)
        else:
            pieces.append(from_behind(stacked, "sw", step_by))
    return jnp.concatenate(pieces, axis=3)


def query_side(
    local_q, local_g, near_keys, near_values, width_gap, height_gap, key_ok, radius, scale
):
    heads = radius.shape[0]
    channels = local_q.shape[1]
    head_dim = channels // heads
    query_rows = local_q.shape[0]
    key_rows = near_keys.shape[0]

    def step(carry, head):
        column_start = head * head_dim
        head_query = lax.dynamic_slice_in_dim(local_q, column_start, head_dim, 1)
        head_grad = lax.dynamic_slice_in_dim(local_g, column_start, head_dim, 1)
        head_key = lax.dynamic_slice_in_dim(near_keys, column_start, head_dim, 1)
        head_value = lax.dynamic_slice_in_dim(near_values, column_start, head_dim, 1)
        allowed = key_ok[None, :] & (width_gap <= radius[head, 1]) & (height_gap <= radius[head, 0])
        scores = contract_cols(head_query, head_key) * scale
        masked = jnp.where(allowed, scores, -1e30)
        row_peak = jnp.max(masked, axis=1, keepdims=True)
        row_total = jnp.sum(
            jnp.where(allowed, jnp.exp(masked - row_peak), 0.0), axis=1, keepdims=True
        )
        log_total = row_peak + jnp.log(row_total)
        probs = jnp.exp(masked - log_total)
        probs_b = probs.astype(jnp.bfloat16)
        attended = jnp.dot(probs_b, head_value, preferred_element_type=jnp.float32)
        delta = jnp.sum(head_grad.astype(jnp.float32) * attended, axis=1, keepdims=True)
        dprobs = contract_cols(head_grad, head_value)
        dscores_b = (probs * (dprobs - delta)).astype(jnp.bfloat16)
        query_part = (
            jnp.dot(dscores_b, head_key, preferred_element_type=jnp.float32) * scale
        ).astype(jnp.bfloat16)
        query_acc = lax.dynamic_update_slice_in_dim(carry[0], query_part, column_start, 1)
        key_part = contract_rows(dscores_b, head_query) * scale
        value_part = contract_rows(probs_b, head_grad)
        key_acc = lax.dynamic_update_slice_in_dim(carry[1], key_part, column_start, 1)
        value_acc = lax.dynamic_update_slice_in_dim(carry[2], value_part, column_start, 1)
        return ((query_acc, key_acc, value_acc), None)

    query_init = jnp.zeros((query_rows, channels), jnp.bfloat16)
    init = (
        query_init,
        jnp.zeros((key_rows, channels), jnp.float32),
        jnp.zeros((key_rows, channels), jnp.float32),
    )
    result, unused = lax.scan(step, init, jnp.arange(heads))
    return result


def general_body(queries, keys, values, out_grad, extents, counts):
    frames, rows, width, channels = queries.shape
    group_heads = channels // HD
    scale = 1.0 / HD**0.5
    reach = (2 * TILE_W - 2 + width) // width
    rim_width = reach * width
    key_span = width + 2 * rim_width
    position = lax.axis_index("sw")
    shifted = position * width + LW // 2
    group = shifted // LW % HEAD_GROUPS
    own_start = shifted % LW
    radius = lax.dynamic_slice_in_dim((extents - 1) // 2, group * group_heads, group_heads, 0)
    near_cols = own_start - rim_width + jnp.arange(key_span)
    own_cols = own_start + jnp.arange(width)
    near_tile, near_rowtile, near_colok, near_ok = layout(near_cols, counts, frames, rows)
    own_tile, own_rowtile, own_colok, own_ok = layout(own_cols, counts, frames, rows)
    local_q = queries.reshape(-1, channels)
    local_g = out_grad.reshape(-1, channels)
    stacked = jnp.stack([keys, values])
    near = near_keys_values(stacked, reach)
    near_keys = near[0].reshape(-1, channels)
    near_values = near[1].reshape(-1, channels)
    width_gap = jnp.abs(own_tile[:, None] - near_tile[None, :])
    height_gap = jnp.abs(own_rowtile[:, None] - near_rowtile[None, :])
    query_grad, key_near, value_near = query_side(
        local_q, local_g, near_keys, near_values, width_gap, height_gap, near_ok, radius, scale
    )
    partial_value = jnp.stack(
        [
            key_near.reshape(frames, rows, key_span, channels),
            value_near.reshape(frames, rows, key_span, channels),
        ]
    )
    summed = lax.slice_in_dim(partial_value, rim_width, rim_width + width, axis=3)
    for step_by in range(-reach, reach + 1):
        if step_by != 0:
            piece = lax.slice_in_dim(
                partial_value,
                rim_width + step_by * width,
                rim_width + (step_by + 1) * width,
                axis=3,
            )
            summed = summed + from_behind(piece, "sw", step_by)
    key_grad = summed[0].astype(jnp.bfloat16)
    value_grad = summed[1].astype(jnp.bfloat16)
    return (query_grad.reshape(frames, rows, width, channels), key_grad, value_grad)


def body(queries, keys, values, out_grad, extents, counts):
    frames, rows, width, channels = queries.shape
    quarters = width == 20 and rows == 16 and LW == 4 * width and counts.shape[0] == 2
    chosen = quarter_body if quarters else general_body
    return chosen(queries, keys, values, out_grad, extents, counts)


def solution(mesh):
    placed = P("clips", None, "sw", None)
    return jax.shard_map(
        body,
        mesh=mesh,
        in_specs=(placed, placed, placed, placed, P(), P()),
        out_specs=(placed, placed, placed),
        check_vma=False,
    )
```

```python
import functools

import jax
import jax.numpy as jnp
from jax import lax
from jax.experimental import pallas as pl
from jax.experimental.pallas import tpu as pltpu
from jax.sharding import PartitionSpec as P

HD = 128
HEAD_GROUPS = 4
TILE_H = 8
TILE_W = 8
LW = 80
ROWS_A = 48
DOT_ROWS = 384
COLS_A = 256
LOG2E = 1.4426950408889634


def attend(role, n_q, n_half, border, high, wide, kw, vw, qs, gs, dqs, dkw, dvw,
           s_scr, p_scr, peaks, totals, weights, dqt, bias):
    scale = 1.0 / HD**0.5
    rate = scale * LOG2E
    both = kw.shape[0] // 3
    full = both // 2

    def unit(subs, n_q, n_k):
        first = 1 - wide
        if role == "C":
            first = jnp.where(border == 1, 1, first)
        last = 2 + wide
        blocks = n_k // ROWS_A
        slices = [(x, min(COLS_A, n_q - x)) for x in range(0, n_q, COLS_A)]

        def products(w, masked):
            for q_lo, col, key_lo in subs:
                start = pl.multiple_of(w * both + key_lo, 128)
                for b in range(0, n_k, min(DOT_ROWS, n_k)):
                    n_d = min(DOT_ROWS, n_k)
                    key_rows = pl.ds(start + b, n_d)
                    for x, n in slices:
                        s_all = lax.dot_general(
                            kw[key_rows, :], qs[q_lo + x : q_lo + x + n, :],
                            (((1,), (1,)), ((), ())), preferred_element_type=jnp.float32,
                        )
                        dp_all = lax.dot_general(
                            vw[key_rows, :], gs[q_lo + x : q_lo + x + n, :],
                            (((1,), (1,)), ((), ())), preferred_element_type=jnp.float32,
                        )
                        here = slice(col + x, col + x + n)
                        for y in range(0, n_d, ROWS_A):
                            s = s_all[y : y + ROWS_A]
                            dp = dp_all[y : y + ROWS_A]
                            to = pl.ds(pl.multiple_of(w * n_k, 128) + b + y, ROWS_A)
                            if masked:
                                off = bias[key_lo + b + y : key_lo + b + y + ROWS_A, :]
                                s = s + jnp.concatenate([off] * pl.cdiv(n, HD), axis=1)[:, :n]
                            s = s.reshape(ROWS_A // 8, 8, n)
                            peak = jnp.max(s, axis=0)
                            e = jnp.exp2(s * rate - peak * rate)
                            dp3 = dp.reshape(ROWS_A // 8, 8, n)
                            at = w * blocks + (b + y) // ROWS_A
                            peaks[at, :, here] = peak
                            totals[at, :, here] = jnp.sum(e, axis=0)
                            weights[at, :, here] = jnp.sum(e * dp3, axis=0)
                            s_scr[to, here] = e.reshape(ROWS_A, n)
                            p_scr[to, here] = dp

        def plain_step(w, carry):
            products(w, False)
            return carry

        def masked_step(w, carry):
            products(w, True)
            return carry

        split = first
        if role != "A":
            edge = 1 if role == "C" else 0
            split = jnp.where(border == 1, jnp.maximum(first, edge + 1), first)
            lax.fori_loop(first, split, masked_step, 0)
        lax.fori_loop(split, last, plain_step, 0)

        cols = [slice(col, col + n_q) for _, col, _ in subs]

        def highest(w, carry):
            out = []
            for c, x in zip(carry, cols):
                for b in range(blocks):
                    c = jnp.maximum(c, peaks[w * blocks + b, :, x])
                out.append(c)
            return tuple(out)

        start_peak = jnp.full((8, n_q), -3e38, jnp.float32)
        tops = lax.fori_loop(first, last, highest, tuple(start_peak for _ in subs))
        tops = [jnp.max(top, axis=0, keepdims=True) for top in tops]

        def combine(w, carry):
            out = []
            for (total, weighted), top, x in zip(carry, tops, cols):
                for b in range(blocks):
                    i = w * blocks + b
                    f = jnp.exp2((peaks[i, :, x] - top) * rate)
                    peaks[i, :, x] = f
                    total = total + f * totals[i, :, x]
                    weighted = weighted + f * weights[i, :, x]
                out.append((total, weighted))
            return tuple(out)

        zero = jnp.zeros((8, n_q), jnp.float32)
        sums = lax.fori_loop(first, last, combine, tuple((zero, zero) for _ in subs))
        inverses = [1.0 / jnp.sum(total, axis=0, keepdims=True) for total, _ in sums]
        deltas = [
            jnp.sum(weighted, axis=0, keepdims=True) * inverse
            for (_, weighted), inverse in zip(sums, inverses)
        ]
        for x in cols:
            dqt[:, x] = jnp.zeros((HD, n_q), jnp.float32)

        def gradients(w, carry):
            base = pl.multiple_of(w * n_k, 128)
            for (q_lo, col, key_lo), inverse, delta, x in zip(subs, inverses, deltas, cols):
                here = pl.ds(pl.multiple_of(w * both + key_lo, 128), n_k)
                pbs, dss = [], []
                for r in range(0, n_k, ROWS_A):
                    f = peaks[w * blocks + r // ROWS_A, :, x] * inverse
                    at = pl.ds(base + r, ROWS_A)
                    e = s_scr[at, x].reshape(ROWS_A // 8, 8, n_q)
                    p = (e * f).reshape(ROWS_A, n_q)
                    dss.append((p * (p_scr[at, x] - delta)).astype(jnp.bfloat16))
                    pbs.append(p.astype(jnp.bfloat16))
                pb = jnp.concatenate(pbs, axis=0)
                ds = jnp.concatenate(dss, axis=0)
                grads = gs[q_lo : q_lo + n_q, :]
                queries = qs[q_lo : q_lo + n_q, :]
                dvw[here, :] += jnp.dot(pb, grads, preferred_element_type=jnp.float32)
                dkw[here, :] += jnp.dot(ds, queries, preferred_element_type=jnp.float32)
                dqt[:, x] += lax.dot_general(
                    kw[here, :], ds, (((0,), (0,)), ((), ())), preferred_element_type=jnp.float32
                )
            return carry

        lax.fori_loop(first, last, gradients, 0)
        for (q_lo, _, _), x in zip(subs, cols):
            dqs[q_lo : q_lo + n_q, :] = jnp.transpose(dqt[:, x]) * scale

    @pl.when(high == 1)
    def _():
        unit([(0, 0, 0)], n_q, both)

    @pl.when(high == 0)
    def _():
        step = (n_half + HD - 1) // HD * HD
        unit([(ht * n_half, ht * step, ht * full) for ht in range(2)], n_half, full)


def rows_of(ref, lead, start, cols, ht):
    block = ref[lead + (slice(None), pl.ds(start, cols), pl.ds(ht * 8, 8), slice(None))]
    n = block.shape[0] * cols * 8
    return block.astype(jnp.float32).reshape(n, HD).astype(jnp.bfloat16)


def block_of(src, lo, step, frames, cols):
    n = frames * cols * 8
    shape = (frames, cols, 8, HD)
    low = src[lo : lo + n, :].reshape(shape)
    return jnp.concatenate([low, src[lo + step : lo + step + n, :].reshape(shape)], axis=2)


def put(ref, lead, start, cols, x):
    ref[lead + (slice(None), pl.ds(start, cols), slice(None), slice(None))] = x.astype(ref.dtype)


def fill_bias(bias, info, full):
    at = lax.broadcasted_iota(jnp.int32, (full, HD), 0)
    t = at // 64
    c = at // 8 - t * 8
    r = at - at // 8 * 8
    place = t * 64 + r * 8 + c
    for ht in range(2):
        bias[ht * full : (ht + 1) * full, :] = jnp.where(place < info[2 + ht], 0.0, -1e30)


def flags(info):
    head = pl.program_id(0)
    return info[0], info[1], info[4 + 2 * head], info[5 + 2 * head]


def mixed_kernel(info, q_ref, g_ref, k_ref, v_ref, nk_ref, nv_ref, dq_out, mix_out, mid_out, send_out,
                 *scratch):
    kw, vw, qs, gs, dqs, dkw, dvw = scratch[:7]
    parity, border, high, wide = flags(info)
    scale = 1.0 / HD**0.5
    frames = q_ref.shape[0]
    full = frames * TILE_H * TILE_W
    half, both = full // 2, 2 * full
    b_off = parity * 0
    a_off = 8 - parity * 8
    b_off = parity * 4
    mix_off = parity * 8
    out_off = 4 - parity * 4
    for ht in range(2):
        for dst, src in ((qs, q_ref), (gs, g_ref)):
            dst[ht * half : (ht + 1) * half, :] = rows_of(src, (), 0, 4, ht)
        for dst, src, near_ref in ((kw, k_ref, nk_ref), (vw, v_ref, nv_ref)):
            lo = ht * full
            dst[lo : lo + full, :] = rows_of(src, (), b_off, 8, ht)
            lo += both
            dst[lo : lo + half, :] = rows_of(src, (), a_off, 4, ht)
            dst[lo + half : lo + full, :] = rows_of(near_ref, (), mix_off, 4, ht)
            lo += both
            dst[lo : lo + full, :] = rows_of(near_ref, (), out_off, 8, ht)
    dkw[...] = jnp.zeros_like(dkw)
    dvw[...] = jnp.zeros_like(dvw)
    attend("A", full, half, border, high, wide, *scratch)
    put(dq_out, (), 0, 4, block_of(dqs, 0, half, frames, 4))
    for which, src, factor in ((0, dkw, scale), (1, dvw, 1.0)):
        mid_out[which, 0] = src[0:both, :].astype(mid_out.dtype)
        mix_out[which, 0] = src[both : 2 * both, :].astype(mix_out.dtype)
        put(send_out, (which,), 0, 8, block_of(src, 2 * both, full, frames, 8) * factor)


def outer_kernel(info, q_ref, g_ref, k_ref, v_ref, far_ref, mid_ref, dq_out, sum_out, send_out,
                 *scratch):
    kw, vw, qs, gs, dqs, dkw, dvw = scratch[:7]
    bias = scratch[-1]
    parity, border, high, wide = flags(info)
    scale = 1.0 / HD**0.5
    frames = q_ref.shape[0]
    full = frames * TILE_H * TILE_W
    both = 2 * full
    c_off = parity * 8
    b_off = 8 - parity * 8
    for ht in range(2):
        for dst, src in ((qs, q_ref), (gs, g_ref)):
            dst[ht * full : (ht + 1) * full, :] = rows_of(src, (), 0, 8, ht)
        for which, dst, src in ((0, kw, k_ref), (1, vw, v_ref)):
            lo = ht * full
            dst[lo : lo + full, :] = rows_of(far_ref, (which,), 0, 8, ht)
            lo += both
            dst[lo : lo + full, :] = rows_of(src, (), c_off, 8, ht)
            lo += both
            dst[lo : lo + full, :] = rows_of(src, (), b_off, 8, ht)

    @pl.when((border == 1) & (pl.program_id(0) == 0))
    def _():
        fill_bias(bias, info, full)

    for which, dst in ((0, dkw), (1, dvw)):
        dst[0 : 2 * both, :] = jnp.zeros((2 * both, HD), jnp.float32)
        dst[2 * both :, :] = mid_ref[which, 0].astype(jnp.float32)
    attend("C", both, full, border, high, wide, *scratch)
    put(dq_out, (), 0, 8, block_of(dqs, 0, full, frames, 8))
    for which, src, factor in ((0, dkw, scale), (1, dvw, 1.0)):
        sum_out[which, 0] = src[both:, :].astype(sum_out.dtype)
        put(send_out, (which,), 0, 8, block_of(src, 0, full, frames, 8) * factor)


def inner_kernel(info, q_ref, g_ref, k_ref, v_ref, nk_ref, nv_ref, sum_ref, mix_ref, dqa_ref, dqc_ref,
                 dq_out, dk_out, dv_out, send_out, *scratch):
    kw, vw, qs, gs, dqs, dkw, dvw = scratch[:7]
    bias = scratch[-1]
    parity, border, high, wide = flags(info)
    scale = 1.0 / HD**0.5
    frames = q_ref.shape[0]
    full = frames * TILE_H * TILE_W
    half, both = full // 2, 2 * full
    c_off = parity * 12
    b_off = 8 - parity * 4
    a_off = 16 - parity * 16
    for ht in range(2):
        for dst, src in ((qs, q_ref), (gs, g_ref)):
            dst[ht * full : (ht + 1) * full, :] = rows_of(src, (), 0, 8, ht)
        for dst, src, near_ref in ((kw, k_ref, nk_ref), (vw, v_ref, nv_ref)):
            lo = ht * full
            dst[lo : lo + full, :] = rows_of(src, (), c_off, 8, ht)
            lo += both
            dst[lo : lo + full, :] = rows_of(src, (), b_off, 8, ht)
            lo += both
            dst[lo : lo + half, :] = rows_of(src, (), a_off, 4, ht)
            dst[lo + half : lo + full, :] = rows_of(near_ref, (), 0, 4, ht)

    @pl.when((border == 1) & (pl.program_id(0) == 0))
    def _():
        fill_bias(bias, info, full)

    for which, dst in ((0, dkw), (1, dvw)):
        dst[0 : 2 * both, :] = sum_ref[which, 0].astype(jnp.float32)
        dst[2 * both :, :] = mix_ref[which, 0].astype(jnp.float32)
    attend("B", both, full, border, high, wide, *scratch)
    put(dq_out, (), b_off, 8, block_of(dqs, 0, full, frames, 8))
    put(dq_out, (), a_off, 4, dqa_ref[...])
    put(dq_out, (), c_off, 8, dqc_ref[...])
    for which, src, factor, own_out in ((0, dkw, scale, dk_out), (1, dvw, 1.0, dv_out)):
        lead = ()
        put(own_out, lead, c_off, 8, block_of(src, 0, full, frames, 8) * factor)
        put(own_out, lead, b_off, 8, block_of(src, both, full, frames, 8) * factor)
        put(own_out, lead, a_off, 4, block_of(src, 2 * both, full, frames, 4) * factor)
        put(send_out, (which,), 0, 4, block_of(src, 2 * both + half, full, frames, 4) * factor)


def scratch_of(n_q, full):
    both = 2 * full
    groups = 3 * both // ROWS_A
    n_c = 2 * ((n_q // 2 + HD - 1) // HD * HD)
    return [
        pltpu.VMEM((3 * both, HD), jnp.bfloat16),
        pltpu.VMEM((3 * both, HD), jnp.bfloat16),
        pltpu.VMEM((n_q, HD), jnp.bfloat16),
        pltpu.VMEM((n_q, HD), jnp.bfloat16),
        pltpu.VMEM((n_q, HD), jnp.float32),
        pltpu.VMEM((3 * both, HD), jnp.float32),
        pltpu.VMEM((3 * both, HD), jnp.float32),
        pltpu.VMEM((3 * both, n_c), jnp.float32),
        pltpu.VMEM((3 * both, n_c), jnp.float32),
        pltpu.VMEM((groups, 8, n_c), jnp.float32),
        pltpu.VMEM((groups, 8, n_c), jnp.float32),
        pltpu.VMEM((groups, 8, n_c), jnp.float32),
        pltpu.VMEM((HD, n_c), jnp.float32),
        pltpu.VMEM((both, HD), jnp.float32),
    ]


def launch(kernel, name, n_q, full, heads, in_specs, out_specs, out_shape, args):
    flops = heads * 10 * n_q * 6 * full * HD
    return pl.pallas_call(
        kernel,
        name=name,
        grid_spec=pltpu.PrefetchScalarGridSpec(
            num_scalar_prefetch=1,
            grid=(heads,),
            in_specs=in_specs,
            out_specs=out_specs,
            scratch_shapes=scratch_of(n_q, full),
        ),
        out_shape=out_shape,
        compiler_params=pltpu.CompilerParams(vmem_limit_bytes=60 * 1024 * 1024),
        cost_estimate=pl.CostEstimate(
            flops=flops, transcendentals=flops // (10 * HD), bytes_accessed=8 << 20
        ),
    )(*args)


def column_block(frames, rows, cols, offset):
    if isinstance(offset, int):
        return pl.BlockSpec((frames, cols, rows, HD), lambda h, info: (0, offset, 0, h))
    return pl.BlockSpec(
        (pl.Element(frames), pl.Element(cols), pl.Element(rows), pl.Element(HD)),
        lambda h, info: (0, offset(info[0]), 0, h * HD),
    )


def attention_parts(info, q, k, v, g, near_k, near_v, heads):
    frames, width, rows, _ = q.shape
    full = frames * TILE_H * TILE_W
    both = 2 * full
    channels = heads * HD

    def pair(cols):
        return pl.BlockSpec((2, frames, cols, rows, HD), lambda h, info: (0, 0, 0, 0, h))

    def chain(n):
        return pl.BlockSpec((2, 1, n, HD), lambda h, info: (0, h, 0, 0))

    def columns(n, dtype=jnp.bfloat16):
        return jax.ShapeDtypeStruct((2, frames, n, rows, channels), dtype)

    def kept(n):
        return jax.ShapeDtypeStruct((2, heads, n, HD), jnp.bfloat16)

    def dq_shape(n):
        return jax.ShapeDtypeStruct((frames, n, rows, channels), jnp.bfloat16)

    def at(cols, offset):
        return column_block(frames, rows, cols, offset)

    def mixed():
        a, ab, nb = at(4, lambda p: 16 - 16 * p), at(12, lambda p: 8 - 8 * p), at(12, lambda p: 8 * p)
        return launch(
            mixed_kernel, "mixed", full, full, heads,
            [a, a, ab, ab, nb, nb],
            [at(4, 0), chain(both), chain(both), pair(8)],
            [dq_shape(4), kept(both), kept(both), columns(8)],
            (info, q, g, k, v, near_k, near_v),
        )

    def outer(far, mid):
        c, cb = at(8, lambda p: 12 * p), at(16, lambda p: 4 * p)
        return launch(
            outer_kernel, "outer", both, full, heads,
            [c, c, cb, cb, pair(8), chain(both)],
            [at(8, 0), chain(2 * both), pair(8)],
            [dq_shape(8), kept(2 * both), columns(8)],
            (info, q, g, k, v, far, mid),
        )

    def inner(info, sums, mix, dqa, dqc):
        b, every, na = at(8, lambda p: 8 - 4 * p), at(width, 0), at(4, lambda p: 16 * p)
        return launch(
            inner_kernel, "inner", both, full, heads,
            [b, b, every, every, na, na, chain(2 * both), chain(both), at(4, 0), at(8, 0)],
            [every, every, every, pair(4)],
            [dq_shape(width), dq_shape(width), dq_shape(width), columns(4)],
            (info, q, g, k, v, near_k, near_v, sums, mix, dqa, dqc),
        )

    return mixed, outer, inner


def attention(info, q, k, v, g, near, far, heads):
    mixed, outer, inner = attention_parts(info, q, k, v, g, k, v, heads)
    dqa, mix, mid, sent = mixed()
    dqc, sums, far_part = outer(far, mid)
    return tuple(inner(info, sums, mix, dqa, dqc)) + (sent, far_part)


def quarter_body(queries, keys, values, out_grad, extents, counts):
    frames, rows, width, channels = queries.shape
    heads = channels // HD
    devices = lax.axis_size("sw")
    position = lax.axis_index("sw")
    shifted = position * width + LW // 2
    group = shifted // LW % HEAD_GROUPS
    place = shifted % LW // width
    parity = place % 2
    border = ((place == 0) | (place == 3)).astype(jnp.int32)
    edge = jnp.where(place == 0, 0, counts.shape[1] - 1)
    limits = lax.dynamic_slice_in_dim(counts, edge, 1, 1)[:, 0]
    radius = lax.dynamic_slice_in_dim((extents - 1) // 2, group * heads, heads, 0)
    info = jnp.concatenate(
        [jnp.stack([parity, border]).astype(jnp.int32), limits, radius.reshape(-1)]
    )
    q, k, v, g = [jnp.transpose(x, (0, 2, 1, 3)) for x in (queries, keys, values, out_grad)]
    first = LW // 2 // width
    near_route = []
    far_route = []
    for i in range(devices):
        at = (i + first) % 4
        near_route.append((i, i + 1 if at % 2 == 0 else i - 1))
        if at == 1:
            far_route.append((i, (i + 1) % devices))
        if at == 2:
            far_route.append((i, (i - 1) % devices))
    near_route = [(a, b % devices) for a, b in near_route]
    near_k = lax.ppermute(k, "sw", near_route)
    near_v = lax.ppermute(v, "sw", near_route)
    far_own = lax.dynamic_slice_in_dim(jnp.stack([k, v]), 12 * parity, 8, 2)
    far = lax.ppermute(far_own, "sw", far_route)
    mixed, outer, inner = attention_parts(info, q, k, v, g, near_k, near_v, heads)
    dqa, mix, mid, sent = mixed()
    mid_back = lax.ppermute(sent, "sw", near_route)
    dqc, sums, far_part = outer(far, mid)
    far_back = lax.ppermute(far_part, "sw", far_route)
    dq, dk, dv, last = inner(info, sums, mix, dqa, dqc)
    edge_back = lax.ppermute(last, "sw", near_route)
    outs = [dq]
    for which, own in ((0, dk), (1, dv)):
        def placed(back, start):
            cols = own.shape[1] - start - back.shape[2]
            return jnp.pad(back[which], ((0, 0), (start, cols), (0, 0), (0, 0)))

        back = jnp.where(
            parity == 0,
            placed(far_back, 0) + placed(mid_back, 8) + placed(edge_back, 16),
            placed(edge_back, 0) + placed(mid_back, 4) + placed(far_back, 12),
        )
        own = (own.astype(jnp.float32) + back.astype(jnp.float32)).astype(jnp.bfloat16)
        outs.append(own)
    return tuple(jnp.transpose(x, (0, 2, 1, 3)) for x in outs)


def from_behind(block, axis, distance):
    devices = range(lax.axis_size(axis))
    route = [((i - distance) % len(devices), i) for i in devices]
    return lax.ppermute(block, axis, route)


def layout(cols, counts, frames, rows):
    tile_rows, tile_cols = counts.shape
    col_tile = cols // TILE_W
    col_ok = (cols >= 0) & (cols < LW)
    safe = jnp.clip(col_tile, 0, tile_cols - 1)
    row_ids = jnp.arange(rows)
    frame_ids = jnp.arange(frames)
    row_tile = row_ids // TILE_H
    pick_rows = (row_tile[:, None] == jnp.arange(tile_rows)[None, :]).astype(jnp.int32)
    pick_cols = (safe[:, None] == jnp.arange(tile_cols)[None, :]).astype(jnp.int32)
    limit = jnp.dot(jnp.dot(pick_rows, counts), jnp.transpose(pick_cols))
    place = (frame_ids[:, None, None] * TILE_H + (row_ids % TILE_H)[None, :, None]) * TILE_W + (
        cols % TILE_W
    )[None, None, :]
    valid = col_ok[None, None, :] & (place < limit[None, :, :])
    shape = (frames, rows, cols.shape[0])
    flat_tile = jnp.broadcast_to(col_tile[None, None, :], shape).reshape(-1)
    flat_rowtile = jnp.broadcast_to(row_tile[None, :, None], shape).reshape(-1)
    flat_colok = jnp.broadcast_to(col_ok[None, None, :], shape).reshape(-1)
    return (flat_tile, flat_rowtile, flat_colok, valid.reshape(-1))


def contract_rows(left, right):
    return lax.dot_general(
        left, right, (((0,), (0,)), ((), ())), preferred_element_type=jnp.float32
    )


def contract_cols(left, right):
    return lax.dot_general(
        left, right, (((1,), (1,)), ((), ())), preferred_element_type=jnp.float32
    )


def near_keys_values(stacked, reach):
    pieces = []
    for step_by in range(reach, -reach - 1, -1):
        if step_by == 0:
            pieces.append(stacked)
        else:
            pieces.append(from_behind(stacked, "sw", step_by))
    return jnp.concatenate(pieces, axis=3)


def query_side(
    local_q, local_g, near_keys, near_values, width_gap, height_gap, key_ok, radius, scale
):
    heads = radius.shape[0]
    channels = local_q.shape[1]
    head_dim = channels // heads
    query_rows = local_q.shape[0]
    key_rows = near_keys.shape[0]

    def step(carry, head):
        column_start = head * head_dim
        head_query = lax.dynamic_slice_in_dim(local_q, column_start, head_dim, 1)
        head_grad = lax.dynamic_slice_in_dim(local_g, column_start, head_dim, 1)
        head_key = lax.dynamic_slice_in_dim(near_keys, column_start, head_dim, 1)
        head_value = lax.dynamic_slice_in_dim(near_values, column_start, head_dim, 1)
        allowed = key_ok[None, :] & (width_gap <= radius[head, 1]) & (height_gap <= radius[head, 0])
        scores = contract_cols(head_query, head_key) * scale
        masked = jnp.where(allowed, scores, -1e30)
        row_peak = jnp.max(masked, axis=1, keepdims=True)
        row_total = jnp.sum(
            jnp.where(allowed, jnp.exp(masked - row_peak), 0.0), axis=1, keepdims=True
        )
        log_total = row_peak + jnp.log(row_total)
        probs = jnp.exp(masked - log_total)
        probs_b = probs.astype(jnp.bfloat16)
        attended = jnp.dot(probs_b, head_value, preferred_element_type=jnp.float32)
        delta = jnp.sum(head_grad.astype(jnp.float32) * attended, axis=1, keepdims=True)
        dprobs = contract_cols(head_grad, head_value)
        dscores_b = (probs * (dprobs - delta)).astype(jnp.bfloat16)
        query_part = (
            jnp.dot(dscores_b, head_key, preferred_element_type=jnp.float32) * scale
        ).astype(jnp.bfloat16)
        query_acc = lax.dynamic_update_slice_in_dim(carry[0], query_part, column_start, 1)
        key_part = contract_rows(dscores_b, head_query) * scale
        value_part = contract_rows(probs_b, head_grad)
        key_acc = lax.dynamic_update_slice_in_dim(carry[1], key_part, column_start, 1)
        value_acc = lax.dynamic_update_slice_in_dim(carry[2], value_part, column_start, 1)
        return ((query_acc, key_acc, value_acc), None)

    query_init = jnp.zeros((query_rows, channels), jnp.bfloat16)
    init = (
        query_init,
        jnp.zeros((key_rows, channels), jnp.float32),
        jnp.zeros((key_rows, channels), jnp.float32),
    )
    result, unused = lax.scan(step, init, jnp.arange(heads))
    return result


def general_body(queries, keys, values, out_grad, extents, counts):
    frames, rows, width, channels = queries.shape
    group_heads = channels // HD
    scale = 1.0 / HD**0.5
    reach = (2 * TILE_W - 2 + width) // width
    rim_width = reach * width
    key_span = width + 2 * rim_width
    position = lax.axis_index("sw")
    shifted = position * width + LW // 2
    group = shifted // LW % HEAD_GROUPS
    own_start = shifted % LW
    radius = lax.dynamic_slice_in_dim((extents - 1) // 2, group * group_heads, group_heads, 0)
    near_cols = own_start - rim_width + jnp.arange(key_span)
    own_cols = own_start + jnp.arange(width)
    near_tile, near_rowtile, near_colok, near_ok = layout(near_cols, counts, frames, rows)
    own_tile, own_rowtile, own_colok, own_ok = layout(own_cols, counts, frames, rows)
    local_q = queries.reshape(-1, channels)
    local_g = out_grad.reshape(-1, channels)
    stacked = jnp.stack([keys, values])
    near = near_keys_values(stacked, reach)
    near_keys = near[0].reshape(-1, channels)
    near_values = near[1].reshape(-1, channels)
    width_gap = jnp.abs(own_tile[:, None] - near_tile[None, :])
    height_gap = jnp.abs(own_rowtile[:, None] - near_rowtile[None, :])
    query_grad, key_near, value_near = query_side(
        local_q, local_g, near_keys, near_values, width_gap, height_gap, near_ok, radius, scale
    )
    partial_value = jnp.stack(
        [
            key_near.reshape(frames, rows, key_span, channels),
            value_near.reshape(frames, rows, key_span, channels),
        ]
    )
    summed = lax.slice_in_dim(partial_value, rim_width, rim_width + width, axis=3)
    for step_by in range(-reach, reach + 1):
        if step_by != 0:
            piece = lax.slice_in_dim(
                partial_value,
                rim_width + step_by * width,
                rim_width + (step_by + 1) * width,
                axis=3,
            )
            summed = summed + from_behind(piece, "sw", step_by)
    key_grad = summed[0].astype(jnp.bfloat16)
    value_grad = summed[1].astype(jnp.bfloat16)
    return (query_grad.reshape(frames, rows, width, channels), key_grad, value_grad)


def body(queries, keys, values, out_grad, extents, counts):
    frames, rows, width, channels = queries.shape
    quarters = width == 20 and rows == 16 and LW == 4 * width and counts.shape[0] == 2
    chosen = quarter_body if quarters else general_body
    return chosen(queries, keys, values, out_grad, extents, counts)


def solution(mesh):
    placed = P("clips", None, "sw", None)
    return jax.shard_map(
        body,
        mesh=mesh,
        in_specs=(placed, placed, placed, placed, P(), P()),
        out_specs=(placed, placed, placed),
        check_vma=False,
    )
```

```python
import functools

import jax
import jax.numpy as jnp
from jax import lax
from jax.experimental import pallas as pl
from jax.experimental.pallas import tpu as pltpu
from jax.sharding import PartitionSpec as P

HD = 128
HEAD_GROUPS = 4
TILE_H = 8
TILE_W = 8
LW = 80
ROWS_A = 48
DOT_ROWS = 384
COLS_A = 256
LOG2E = 1.4426950408889634


def attend(role, n_q, n_half, border, high, wide, kw, vw, qs, gs, dqs, dkw, dvw,
           s_scr, p_scr, peaks, totals, weights, dqt, bias):
    scale = 1.0 / HD**0.5
    rate = scale * LOG2E
    both = kw.shape[0] // 3
    full = both // 2

    def unit(subs, n_q, n_k):
        first = 1 - wide
        if role == "C":
            first = jnp.where(border == 1, 1, first)
        last = 2 + wide
        blocks = n_k // ROWS_A
        slices = [(x, min(COLS_A, n_q - x)) for x in range(0, n_q, COLS_A)]

        def products(w, masked):
            for q_lo, col, key_lo in subs:
                start = pl.multiple_of(w * both + key_lo, 128)
                for b in range(0, n_k, min(DOT_ROWS, n_k)):
                    n_d = min(DOT_ROWS, n_k)
                    key_rows = pl.ds(start + b, n_d)
                    for x, n in slices:
                        s_all = lax.dot_general(
                            kw[key_rows, :], qs[q_lo + x : q_lo + x + n, :],
                            (((1,), (1,)), ((), ())), preferred_element_type=jnp.float32,
                        )
                        dp_all = lax.dot_general(
                            vw[key_rows, :], gs[q_lo + x : q_lo + x + n, :],
                            (((1,), (1,)), ((), ())), preferred_element_type=jnp.float32,
                        )
                        here = slice(col + x, col + x + n)
                        for y in range(0, n_d, ROWS_A):
                            s = s_all[y : y + ROWS_A]
                            dp = dp_all[y : y + ROWS_A]
                            to = pl.ds(pl.multiple_of(w * n_k, 128) + b + y, ROWS_A)
                            if masked:
                                off = bias[key_lo + b + y : key_lo + b + y + ROWS_A, :]
                                s = s + jnp.concatenate([off] * pl.cdiv(n, HD), axis=1)[:, :n]
                            s = s.reshape(ROWS_A // 8, 8, n)
                            peak = jnp.max(s, axis=0)
                            e = jnp.exp2(s * rate - peak * rate)
                            dp3 = dp.reshape(ROWS_A // 8, 8, n)
                            at = w * blocks + (b + y) // ROWS_A
                            peaks[at, :, here] = peak
                            totals[at, :, here] = jnp.sum(e, axis=0)
                            weights[at, :, here] = jnp.sum(e * dp3, axis=0)
                            s_scr[to, here] = e.reshape(ROWS_A, n)
                            p_scr[to, here] = dp

        def plain_step(w, carry):
            products(w, False)
            return carry

        def masked_step(w, carry):
            products(w, True)
            return carry

        split = first
        if role != "A":
            edge = 1 if role == "C" else 0
            split = jnp.where(border == 1, jnp.maximum(first, edge + 1), first)
            lax.fori_loop(first, split, masked_step, 0)
        lax.fori_loop(split, last, plain_step, 0)

        cols = [slice(col, col + n_q) for _, col, _ in subs]

        def highest(w, carry):
            out = []
            for c, x in zip(carry, cols):
                for b in range(blocks):
                    c = jnp.maximum(c, peaks[w * blocks + b, :, x])
                out.append(c)
            return tuple(out)

        start_peak = jnp.full((8, n_q), -3e38, jnp.float32)
        tops = lax.fori_loop(first, last, highest, tuple(start_peak for _ in subs))
        tops = [jnp.max(top, axis=0, keepdims=True) for top in tops]

        def combine(w, carry):
            out = []
            for (total, weighted), top, x in zip(carry, tops, cols):
                for b in range(blocks):
                    i = w * blocks + b
                    f = jnp.exp2((peaks[i, :, x] - top) * rate)
                    peaks[i, :, x] = f
                    total = total + f * totals[i, :, x]
                    weighted = weighted + f * weights[i, :, x]
                out.append((total, weighted))
            return tuple(out)

        zero = jnp.zeros((8, n_q), jnp.float32)
        sums = lax.fori_loop(first, last, combine, tuple((zero, zero) for _ in subs))
        inverses = [1.0 / jnp.sum(total, axis=0, keepdims=True) for total, _ in sums]
        deltas = [
            jnp.sum(weighted, axis=0, keepdims=True) * inverse
            for (_, weighted), inverse in zip(sums, inverses)
        ]
        for x in cols:
            dqt[:, x] = jnp.zeros((HD, n_q), jnp.float32)

        def gradients(w, carry):
            base = pl.multiple_of(w * n_k, 128)
            for (q_lo, col, key_lo), inverse, delta, x in zip(subs, inverses, deltas, cols):
                here = pl.ds(pl.multiple_of(w * both + key_lo, 128), n_k)
                pbs, dss = [], []
                for r in range(0, n_k, ROWS_A):
                    f = peaks[w * blocks + r // ROWS_A, :, x] * inverse
                    at = pl.ds(base + r, ROWS_A)
                    e = s_scr[at, x].reshape(ROWS_A // 8, 8, n_q)
                    p = (e * f).reshape(ROWS_A, n_q)
                    dss.append((p * (p_scr[at, x] - delta)).astype(jnp.bfloat16))
                    pbs.append(p.astype(jnp.bfloat16))
                pb = jnp.concatenate(pbs, axis=0)
                ds = jnp.concatenate(dss, axis=0)
                grads = gs[q_lo : q_lo + n_q, :]
                queries = qs[q_lo : q_lo + n_q, :]
                dvw[here, :] = jnp.dot(pb, grads, preferred_element_type=jnp.float32)
                dkw[here, :] = jnp.dot(ds, queries, preferred_element_type=jnp.float32)
                dqt[:, x] += lax.dot_general(
                    kw[here, :], ds, (((0,), (0,)), ((), ())), preferred_element_type=jnp.float32
                )
            return carry

        lax.fori_loop(first, last, gradients, 0)
        for (q_lo, _, _), x in zip(subs, cols):
            dqs[q_lo : q_lo + n_q, :] = jnp.transpose(dqt[:, x]) * scale

    @pl.when(high == 1)
    def _():
        unit([(0, 0, 0)], n_q, both)

    @pl.when(high == 0)
    def _():
        step = (n_half + HD - 1) // HD * HD
        unit([(ht * n_half, ht * step, ht * full) for ht in range(2)], n_half, full)


def rows_of(ref, lead, start, cols, ht):
    block = ref[lead + (slice(None), pl.ds(start, cols), pl.ds(ht * 8, 8), slice(None))]
    n = block.shape[0] * cols * 8
    return block.astype(jnp.float32).reshape(n, HD).astype(jnp.bfloat16)


def block_of(src, lo, step, frames, cols, more=None, at=0):
    n = frames * cols * 8
    parts = []
    for start in (0, step):
        x = src[lo + start : lo + start + n, :]
        if more is not None:
            x = x + more[at + start : at + start + n, :].astype(jnp.float32)
        parts.append(x.reshape(frames, cols, 8, HD))
    return jnp.concatenate(parts, axis=2)


def clear(skipped, dkw, dvw):
    @pl.when(skipped)
    def _():
        dkw[...] = jnp.zeros_like(dkw)
        dvw[...] = jnp.zeros_like(dvw)


def put(ref, lead, start, cols, x):
    ref[lead + (slice(None), pl.ds(start, cols), slice(None), slice(None))] = x.astype(ref.dtype)


def fill_bias(bias, info, full):
    at = lax.broadcasted_iota(jnp.int32, (full, HD), 0)
    t = at // 64
    c = at // 8 - t * 8
    r = at - at // 8 * 8
    place = t * 64 + r * 8 + c
    for ht in range(2):
        bias[ht * full : (ht + 1) * full, :] = jnp.where(place < info.limit(ht), 0.0, -1e30)


def place_of(position, width):
    shifted = position * width + LW // 2
    return shifted // LW % HEAD_GROUPS, shifted % LW // width


class Scalars:
    def __init__(self, width, heads, position, extents, counts):
        group, self.place = place_of(position[0], width)
        self.first_head = group * heads
        self.extents = extents
        self.counts = counts
        self.parity = self.place % 2
        self.border = ((self.place == 0) | (self.place == 3)).astype(jnp.int32)

    def limit(self, ht):
        last = self.counts.shape[1] - 1
        return self.counts[ht, jnp.where(self.place == 0, 0, last)]


def flags(info):
    head = info.first_head + pl.program_id(0)
    high, wide = [(info.extents[axis, head] - 1) // 2 for axis in (0, 1)]
    return info.parity, info.border, high, wide


def mixed_kernel(info, q_ref, g_ref, k_ref, v_ref, nk_ref, nv_ref, dq_out, mix_out, mid_out, send_out,
                 *scratch):
    kw, vw, qs, gs, dqs, dkw, dvw = scratch[:7]
    parity, border, high, wide = flags(info)
    scale = 1.0 / HD**0.5
    frames = q_ref.shape[0]
    full = frames * TILE_H * TILE_W
    half, both = full // 2, 2 * full
    b_off = parity * 0
    a_off = 8 - parity * 8
    b_off = parity * 4
    mix_off = parity * 8
    out_off = 4 - parity * 4
    for ht in range(2):
        for dst, src in ((qs, q_ref), (gs, g_ref)):
            dst[ht * half : (ht + 1) * half, :] = rows_of(src, (), 0, 4, ht)
        for dst, src, near_ref in ((kw, k_ref, nk_ref), (vw, v_ref, nv_ref)):
            lo = ht * full
            dst[lo : lo + full, :] = rows_of(src, (), b_off, 8, ht)
            lo += both
            dst[lo : lo + half, :] = rows_of(src, (), a_off, 4, ht)
            dst[lo + half : lo + full, :] = rows_of(near_ref, (), mix_off, 4, ht)
            lo += both
            dst[lo : lo + full, :] = rows_of(near_ref, (), out_off, 8, ht)
    clear(wide == 0, dkw, dvw)
    attend("A", full, half, border, high, wide, *scratch)
    put(dq_out, (), 0, 4, block_of(dqs, 0, half, frames, 4))
    for which, src, factor in ((0, dkw, scale), (1, dvw, 1.0)):
        mid_out[which, 0] = src[0:both, :].astype(mid_out.dtype)
        mix_out[which, 0] = src[both : 2 * both, :].astype(mix_out.dtype)
        put(send_out, (which,), 0, 8, block_of(src, 2 * both, full, frames, 8) * factor)


def outer_kernel(info, q_ref, g_ref, k_ref, v_ref, far_ref, mid_ref, dq_out, sum_out, send_out,
                 *scratch):
    kw, vw, qs, gs, dqs, dkw, dvw = scratch[:7]
    bias = scratch[-1]
    parity, border, high, wide = flags(info)
    scale = 1.0 / HD**0.5
    frames = q_ref.shape[0]
    full = frames * TILE_H * TILE_W
    both = 2 * full
    c_off = parity * 8
    b_off = 8 - parity * 8
    for ht in range(2):
        for dst, src in ((qs, q_ref), (gs, g_ref)):
            dst[ht * full : (ht + 1) * full, :] = rows_of(src, (), 0, 8, ht)
        for which, dst, src in ((0, kw, k_ref), (1, vw, v_ref)):
            lo = ht * full
            dst[lo : lo + full, :] = rows_of(far_ref, (which,), 0, 8, ht)
            lo += both
            dst[lo : lo + full, :] = rows_of(src, (), c_off, 8, ht)
            lo += both
            dst[lo : lo + full, :] = rows_of(src, (), b_off, 8, ht)

    @pl.when((border == 1) & (pl.program_id(0) == 0))
    def _():
        fill_bias(bias, info, full)

    clear((wide == 0) | (border == 1), dkw, dvw)
    attend("C", both, full, border, high, wide, *scratch)
    put(dq_out, (), 0, 8, block_of(dqs, 0, full, frames, 8))
    for which, src, factor in ((0, dkw, scale), (1, dvw, 1.0)):
        sum_out[which, 0, :both] = src[both : 2 * both, :].astype(sum_out.dtype)
        last = src[2 * both :, :] + mid_ref[which, 0].astype(jnp.float32)
        sum_out[which, 0, both:] = last.astype(sum_out.dtype)
        put(send_out, (which,), 0, 8, block_of(src, 0, full, frames, 8) * factor)


def inner_kernel(info, q_ref, g_ref, k_ref, v_ref, nk_ref, nv_ref, sum_ref, mix_ref, dqa_ref, dqc_ref,
                 dq_out, dk_out, dv_out, send_out, *scratch):
    kw, vw, qs, gs, dqs, dkw, dvw = scratch[:7]
    bias = scratch[-1]
    parity, border, high, wide = flags(info)
    scale = 1.0 / HD**0.5
    frames = q_ref.shape[0]
    full = frames * TILE_H * TILE_W
    half, both = full // 2, 2 * full
    c_off = parity * 12
    b_off = 8 - parity * 4
    a_off = 16 - parity * 16
    for ht in range(2):
        for dst, src in ((qs, q_ref), (gs, g_ref)):
            dst[ht * full : (ht + 1) * full, :] = rows_of(src, (), 0, 8, ht)
        for dst, src, near_ref in ((kw, k_ref, nk_ref), (vw, v_ref, nv_ref)):
            lo = ht * full
            dst[lo : lo + full, :] = rows_of(src, (), c_off, 8, ht)
            lo += both
            dst[lo : lo + full, :] = rows_of(src, (), b_off, 8, ht)
            lo += both
            dst[lo : lo + half, :] = rows_of(src, (), a_off, 4, ht)
            dst[lo + half : lo + full, :] = rows_of(near_ref, (), 0, 4, ht)

    @pl.when((border == 1) & (pl.program_id(0) == 0))
    def _():
        fill_bias(bias, info, full)

    clear(wide == 0, dkw, dvw)
    attend("B", both, full, border, high, wide, *scratch)
    put(dq_out, (), b_off, 8, block_of(dqs, 0, full, frames, 8))
    put(dq_out, (), a_off, 4, dqa_ref[...])
    put(dq_out, (), c_off, 8, dqc_ref[...])
    for which, src, factor, own_out in ((0, dkw, scale, dk_out), (1, dvw, 1.0, dv_out)):
        kept, mix = sum_ref.at[which, 0], mix_ref.at[which, 0]
        c_part = block_of(src, 0, full, frames, 8, kept, 0)
        b_part = block_of(src, both, full, frames, 8, kept, both)
        a_part = block_of(src, 2 * both, full, frames, 4, mix, 0)
        rest = block_of(src, 2 * both + half, full, frames, 4, mix, half)
        put(own_out, (), c_off, 8, c_part * factor)
        put(own_out, (), b_off, 8, b_part * factor)
        put(own_out, (), a_off, 4, a_part * factor)
        put(send_out, (which,), 0, 4, rest * factor)


def scratch_of(n_q, full):
    both = 2 * full
    groups = 3 * both // ROWS_A
    n_c = 2 * ((n_q // 2 + HD - 1) // HD * HD)
    return [
        pltpu.VMEM((3 * both, HD), jnp.bfloat16),
        pltpu.VMEM((3 * both, HD), jnp.bfloat16),
        pltpu.VMEM((n_q, HD), jnp.bfloat16),
        pltpu.VMEM((n_q, HD), jnp.bfloat16),
        pltpu.VMEM((n_q, HD), jnp.float32),
        pltpu.VMEM((3 * both, HD), jnp.float32),
        pltpu.VMEM((3 * both, HD), jnp.float32),
        pltpu.VMEM((3 * both, n_c), jnp.float32),
        pltpu.VMEM((3 * both, n_c), jnp.float32),
        pltpu.VMEM((groups, 8, n_c), jnp.float32),
        pltpu.VMEM((groups, 8, n_c), jnp.float32),
        pltpu.VMEM((groups, 8, n_c), jnp.float32),
        pltpu.VMEM((HD, n_c), jnp.float32),
        pltpu.VMEM((both, HD), jnp.float32),
    ]


def launch(kernel, name, n_q, width, full, heads, in_specs, out_specs, out_shape, args):
    flops = heads * 10 * n_q * 6 * full * HD

    def body(position, extents, counts, *refs):
        kernel(Scalars(width, heads, position, extents, counts), *refs)

    return pl.pallas_call(
        body,
        name=name,
        grid_spec=pltpu.PrefetchScalarGridSpec(
            num_scalar_prefetch=3,
            grid=(heads,),
            in_specs=in_specs,
            out_specs=out_specs,
            scratch_shapes=scratch_of(n_q, full),
        ),
        out_shape=out_shape,
        compiler_params=pltpu.CompilerParams(vmem_limit_bytes=60 * 1024 * 1024),
        cost_estimate=pl.CostEstimate(
            flops=flops, transcendentals=flops // (10 * HD), bytes_accessed=8 << 20
        ),
    )(*args[0], *args[1:])


def column_block(frames, rows, cols, width, offset):
    if isinstance(offset, int):
        return pl.BlockSpec((frames, cols, rows, HD), lambda h, *_: (0, offset, 0, h))
    return pl.BlockSpec(
        (pl.Element(frames), pl.Element(cols), pl.Element(rows), pl.Element(HD)),
        lambda h, position, *_: (0, offset(place_of(position[0], width)[1] % 2), 0, h * HD),
    )


def attention_parts(info, q, k, v, g, near_k, near_v, heads):
    frames, width, rows, _ = q.shape
    full = frames * TILE_H * TILE_W
    both = 2 * full
    channels = heads * HD

    def pair(cols):
        return pl.BlockSpec((2, frames, cols, rows, HD), lambda h, *_: (0, 0, 0, 0, h))

    def chain(n):
        return pl.BlockSpec((2, 1, n, HD), lambda h, *_: (0, h, 0, 0))

    def columns(n, dtype=jnp.bfloat16):
        return jax.ShapeDtypeStruct((2, frames, n, rows, channels), dtype)

    def kept(n):
        return jax.ShapeDtypeStruct((2, heads, n, HD), jnp.bfloat16)

    def dq_shape(n):
        return jax.ShapeDtypeStruct((frames, n, rows, channels), jnp.bfloat16)

    def at(cols, offset):
        return column_block(frames, rows, cols, width, offset)

    def mixed():
        a, ab, nb = at(4, lambda p: 16 - 16 * p), at(12, lambda p: 8 - 8 * p), at(12, lambda p: 8 * p)
        return launch(
            mixed_kernel, "mixed", full, width, full, heads,
            [a, a, ab, ab, nb, nb],
            [at(4, 0), chain(both), chain(both), pair(8)],
            [dq_shape(4), kept(both), kept(both), columns(8)],
            (info, q, g, k, v, near_k, near_v),
        )

    def outer(far, mid):
        c, cb = at(8, lambda p: 12 * p), at(16, lambda p: 4 * p)
        return launch(
            outer_kernel, "outer", both, width, full, heads,
            [c, c, cb, cb, pair(8), chain(both)],
            [at(8, 0), chain(2 * both), pair(8)],
            [dq_shape(8), kept(2 * both), columns(8)],
            (info, q, g, k, v, far, mid),
        )

    def inner(info, sums, mix, dqa, dqc):
        b, every, na = at(8, lambda p: 8 - 4 * p), at(width, 0), at(4, lambda p: 16 * p)
        return launch(
            inner_kernel, "inner", both, width, full, heads,
            [b, b, every, every, na, na, chain(2 * both), chain(both), at(4, 0), at(8, 0)],
            [every, every, every, pair(4)],
            [dq_shape(width), dq_shape(width), dq_shape(width), columns(4)],
            (info, q, g, k, v, near_k, near_v, sums, mix, dqa, dqc),
        )

    return mixed, outer, inner


def quarter_body(queries, keys, values, out_grad, extents, counts):
    frames, rows, width, channels = queries.shape
    heads = channels // HD
    devices = lax.axis_size("sw")
    position = lax.axis_index("sw")
    parity = place_of(position, width)[1] % 2
    info = (position.reshape(1), jnp.transpose(extents), counts)
    q, k, v, g = [jnp.transpose(x, (0, 2, 1, 3)) for x in (queries, keys, values, out_grad)]
    first = LW // 2 // width
    near_route = []
    far_route = []
    for i in range(devices):
        at = (i + first) % 4
        near_route.append((i, i + 1 if at % 2 == 0 else i - 1))
        if at == 1:
            far_route.append((i, (i + 1) % devices))
        if at == 2:
            far_route.append((i, (i - 1) % devices))
    near_route = [(a, b % devices) for a, b in near_route]
    near_k = lax.ppermute(k, "sw", near_route)
    near_v = lax.ppermute(v, "sw", near_route)
    far_own = lax.dynamic_slice_in_dim(jnp.stack([k, v]), 12 * parity, 8, 2)
    far = lax.ppermute(far_own, "sw", far_route)
    mixed, outer, inner = attention_parts(info, q, k, v, g, near_k, near_v, heads)
    dqa, mix, mid, sent = mixed()
    mid_back = lax.ppermute(sent, "sw", near_route)
    dqc, sums, far_part = outer(far, mid)
    far_back = lax.ppermute(far_part, "sw", far_route)
    dq, dk, dv, last = inner(info, sums, mix, dqa, dqc)
    edge_back = lax.ppermute(last, "sw", near_route)
    outs = [dq]
    for which, own in ((0, dk), (1, dv)):
        def placed(back, start):
            cols = own.shape[1] - start - back.shape[2]
            return jnp.pad(back[which], ((0, 0), (start, cols), (0, 0), (0, 0)))

        back = jnp.where(
            parity == 0,
            placed(far_back, 0) + placed(mid_back, 8) + placed(edge_back, 16),
            placed(edge_back, 0) + placed(mid_back, 4) + placed(far_back, 12),
        )
        own = (own.astype(jnp.float32) + back.astype(jnp.float32)).astype(jnp.bfloat16)
        outs.append(own)
    return tuple(jnp.transpose(x, (0, 2, 1, 3)) for x in outs)


def from_behind(block, axis, distance):
    devices = range(lax.axis_size(axis))
    route = [((i - distance) % len(devices), i) for i in devices]
    return lax.ppermute(block, axis, route)


def layout(cols, counts, frames, rows):
    tile_rows, tile_cols = counts.shape
    col_tile = cols // TILE_W
    col_ok = (cols >= 0) & (cols < LW)
    safe = jnp.clip(col_tile, 0, tile_cols - 1)
    row_ids = jnp.arange(rows)
    frame_ids = jnp.arange(frames)
    row_tile = row_ids // TILE_H
    pick_rows = (row_tile[:, None] == jnp.arange(tile_rows)[None, :]).astype(jnp.int32)
    pick_cols = (safe[:, None] == jnp.arange(tile_cols)[None, :]).astype(jnp.int32)
    limit = jnp.dot(jnp.dot(pick_rows, counts), jnp.transpose(pick_cols))
    place = (frame_ids[:, None, None] * TILE_H + (row_ids % TILE_H)[None, :, None]) * TILE_W + (
        cols % TILE_W
    )[None, None, :]
    valid = col_ok[None, None, :] & (place < limit[None, :, :])
    shape = (frames, rows, cols.shape[0])
    flat_tile = jnp.broadcast_to(col_tile[None, None, :], shape).reshape(-1)
    flat_rowtile = jnp.broadcast_to(row_tile[None, :, None], shape).reshape(-1)
    flat_colok = jnp.broadcast_to(col_ok[None, None, :], shape).reshape(-1)
    return (flat_tile, flat_rowtile, flat_colok, valid.reshape(-1))


def contract_rows(left, right):
    return lax.dot_general(
        left, right, (((0,), (0,)), ((), ())), preferred_element_type=jnp.float32
    )


def contract_cols(left, right):
    return lax.dot_general(
        left, right, (((1,), (1,)), ((), ())), preferred_element_type=jnp.float32
    )


def near_keys_values(stacked, reach):
    pieces = []
    for step_by in range(reach, -reach - 1, -1):
        if step_by == 0:
            pieces.append(stacked)
        else:
            pieces.append(from_behind(stacked, "sw", step_by))
    return jnp.concatenate(pieces, axis=3)


def query_side(
    local_q, local_g, near_keys, near_values, width_gap, height_gap, key_ok, radius, scale
):
    heads = radius.shape[0]
    channels = local_q.shape[1]
    head_dim = channels // heads
    query_rows = local_q.shape[0]
    key_rows = near_keys.shape[0]

    def step(carry, head):
        column_start = head * head_dim
        head_query = lax.dynamic_slice_in_dim(local_q, column_start, head_dim, 1)
        head_grad = lax.dynamic_slice_in_dim(local_g, column_start, head_dim, 1)
        head_key = lax.dynamic_slice_in_dim(near_keys, column_start, head_dim, 1)
        head_value = lax.dynamic_slice_in_dim(near_values, column_start, head_dim, 1)
        allowed = key_ok[None, :] & (width_gap <= radius[head, 1]) & (height_gap <= radius[head, 0])
        scores = contract_cols(head_query, head_key) * scale
        masked = jnp.where(allowed, scores, -1e30)
        row_peak = jnp.max(masked, axis=1, keepdims=True)
        row_total = jnp.sum(
            jnp.where(allowed, jnp.exp(masked - row_peak), 0.0), axis=1, keepdims=True
        )
        log_total = row_peak + jnp.log(row_total)
        probs = jnp.exp(masked - log_total)
        probs_b = probs.astype(jnp.bfloat16)
        attended = jnp.dot(probs_b, head_value, preferred_element_type=jnp.float32)
        delta = jnp.sum(head_grad.astype(jnp.float32) * attended, axis=1, keepdims=True)
        dprobs = contract_cols(head_grad, head_value)
        dscores_b = (probs * (dprobs - delta)).astype(jnp.bfloat16)
        query_part = (
            jnp.dot(dscores_b, head_key, preferred_element_type=jnp.float32) * scale
        ).astype(jnp.bfloat16)
        query_acc = lax.dynamic_update_slice_in_dim(carry[0], query_part, column_start, 1)
        key_part = contract_rows(dscores_b, head_query) * scale
        value_part = contract_rows(probs_b, head_grad)
        key_acc = lax.dynamic_update_slice_in_dim(carry[1], key_part, column_start, 1)
        value_acc = lax.dynamic_update_slice_in_dim(carry[2], value_part, column_start, 1)
        return ((query_acc, key_acc, value_acc), None)

    query_init = jnp.zeros((query_rows, channels), jnp.bfloat16)
    init = (
        query_init,
        jnp.zeros((key_rows, channels), jnp.float32),
        jnp.zeros((key_rows, channels), jnp.float32),
    )
    result, unused = lax.scan(step, init, jnp.arange(heads))
    return result


def general_body(queries, keys, values, out_grad, extents, counts):
    frames, rows, width, channels = queries.shape
    group_heads = channels // HD
    scale = 1.0 / HD**0.5
    reach = (2 * TILE_W - 2 + width) // width
    rim_width = reach * width
    key_span = width + 2 * rim_width
    position = lax.axis_index("sw")
    shifted = position * width + LW // 2
    group = shifted // LW % HEAD_GROUPS
    own_start = shifted % LW
    radius = lax.dynamic_slice_in_dim((extents - 1) // 2, group * group_heads, group_heads, 0)
    near_cols = own_start - rim_width + jnp.arange(key_span)
    own_cols = own_start + jnp.arange(width)
    near_tile, near_rowtile, near_colok, near_ok = layout(near_cols, counts, frames, rows)
    own_tile, own_rowtile, own_colok, own_ok = layout(own_cols, counts, frames, rows)
    local_q = queries.reshape(-1, channels)
    local_g = out_grad.reshape(-1, channels)
    stacked = jnp.stack([keys, values])
    near = near_keys_values(stacked, reach)
    near_keys = near[0].reshape(-1, channels)
    near_values = near[1].reshape(-1, channels)
    width_gap = jnp.abs(own_tile[:, None] - near_tile[None, :])
    height_gap = jnp.abs(own_rowtile[:, None] - near_rowtile[None, :])
    query_grad, key_near, value_near = query_side(
        local_q, local_g, near_keys, near_values, width_gap, height_gap, near_ok, radius, scale
    )
    partial_value = jnp.stack(
        [
            key_near.reshape(frames, rows, key_span, channels),
            value_near.reshape(frames, rows, key_span, channels),
        ]
    )
    summed = lax.slice_in_dim(partial_value, rim_width, rim_width + width, axis=3)
    for step_by in range(-reach, reach + 1):
        if step_by != 0:
            piece = lax.slice_in_dim(
                partial_value,
                rim_width + step_by * width,
                rim_width + (step_by + 1) * width,
                axis=3,
            )
            summed = summed + from_behind(piece, "sw", step_by)
    key_grad = summed[0].astype(jnp.bfloat16)
    value_grad = summed[1].astype(jnp.bfloat16)
    return (query_grad.reshape(frames, rows, width, channels), key_grad, value_grad)


def body(queries, keys, values, out_grad, extents, counts):
    frames, rows, width, channels = queries.shape
    quarters = width == 20 and rows == 16 and LW == 4 * width and counts.shape[0] == 2
    chosen = quarter_body if quarters else general_body
    return chosen(queries, keys, values, out_grad, extents, counts)


def solution(mesh):
    placed = P("clips", None, "sw", None)
    return jax.shard_map(
        body,
        mesh=mesh,
        in_specs=(placed, placed, placed, placed, P(), P()),
        out_specs=(placed, placed, placed),
        check_vma=False,
    )
```

```python
import functools

import jax
import jax.numpy as jnp
from jax import lax
from jax.experimental import pallas as pl
from jax.experimental.pallas import tpu as pltpu
from jax.sharding import PartitionSpec as P

HD = 128
HEAD_GROUPS = 4
TILE_H = 8
TILE_W = 8
LW = 80
ROWS_A = 48
DOT_ROWS = 384
COLS_A = 256
LOG2E = 1.4426950408889634


def attend(role, n_q, n_half, border, high, wide, kw, vw, qs, gs, dqs, dkw, dvw,
           s_scr, p_scr, peaks, totals, weights, dqt, bias):
    scale = 1.0 / HD**0.5
    rate = scale * LOG2E
    both = kw.shape[0] // 3
    full = both // 2

    def unit(subs, n_q, n_k):
        first = 1 - wide
        if role == "C":
            first = jnp.where(border == 1, 1, first)
        last = 2 + wide
        blocks = n_k // ROWS_A
        slices = [(x, min(COLS_A, n_q - x)) for x in range(0, n_q, COLS_A)]

        def products(w, masked):
            for q_lo, col, key_lo in subs:
                start = pl.multiple_of(w * both + key_lo, 128)
                for b in range(0, n_k, min(DOT_ROWS, n_k)):
                    n_d = min(DOT_ROWS, n_k)
                    key_rows = pl.ds(start + b, n_d)
                    for x, n in slices:
                        s_all = lax.dot_general(
                            kw[key_rows, :], qs[q_lo + x : q_lo + x + n, :],
                            (((1,), (1,)), ((), ())), preferred_element_type=jnp.float32,
                        )
                        dp_all = lax.dot_general(
                            vw[key_rows, :], gs[q_lo + x : q_lo + x + n, :],
                            (((1,), (1,)), ((), ())), preferred_element_type=jnp.float32,
                        )
                        here = slice(col + x, col + x + n)
                        for y in range(0, n_d, ROWS_A):
                            s = s_all[y : y + ROWS_A]
                            dp = dp_all[y : y + ROWS_A]
                            to = pl.ds(pl.multiple_of(w * n_k, 128) + b + y, ROWS_A)
                            if masked:
                                off = bias[key_lo + b + y : key_lo + b + y + ROWS_A, :]
                                s = s + jnp.concatenate([off] * pl.cdiv(n, HD), axis=1)[:, :n]
                            s = s.reshape(ROWS_A // 8, 8, n)
                            peak = jnp.max(s, axis=0)
                            e = jnp.exp2(s * rate - peak * rate)
                            dp3 = dp.reshape(ROWS_A // 8, 8, n)
                            at = w * blocks + (b + y) // ROWS_A
                            peaks[at, :, here] = peak
                            totals[at, :, here] = jnp.sum(e, axis=0)
                            weights[at, :, here] = jnp.sum(e * dp3, axis=0)
                            s_scr[to, here] = e.reshape(ROWS_A, n)
                            p_scr[to, here] = dp

        def plain_step(w, carry):
            products(w, False)
            return carry

        def masked_step(w, carry):
            products(w, True)
            return carry

        split = first
        if role != "A":
            edge = 1 if role == "C" else 0
            split = jnp.where(border == 1, jnp.maximum(first, edge + 1), first)
            lax.fori_loop(first, split, masked_step, 0)
        lax.fori_loop(split, last, plain_step, 0)

        cols = [slice(col, col + n_q) for _, col, _ in subs]

        def highest(w, carry):
            out = []
            for c, x in zip(carry, cols):
                for b in range(blocks):
                    c = jnp.maximum(c, peaks[w * blocks + b, :, x])
                out.append(c)
            return tuple(out)

        start_peak = jnp.full((8, n_q), -3e38, jnp.float32)
        tops = lax.fori_loop(first, last, highest, tuple(start_peak for _ in subs))
        tops = [jnp.max(top, axis=0, keepdims=True) for top in tops]

        def combine(w, carry):
            out = []
            for (total, weighted), top, x in zip(carry, tops, cols):
                for b in range(blocks):
                    i = w * blocks + b
                    f = jnp.exp2((peaks[i, :, x] - top) * rate)
                    peaks[i, :, x] = f
                    total = total + f * totals[i, :, x]
                    weighted = weighted + f * weights[i, :, x]
                out.append((total, weighted))
            return tuple(out)

        zero = jnp.zeros((8, n_q), jnp.float32)
        sums = lax.fori_loop(first, last, combine, tuple((zero, zero) for _ in subs))
        inverses = [1.0 / jnp.sum(total, axis=0, keepdims=True) for total, _ in sums]
        deltas = [
            jnp.sum(weighted, axis=0, keepdims=True) * inverse
            for (_, weighted), inverse in zip(sums, inverses)
        ]
        for x in cols:
            dqt[:, x] = jnp.zeros((HD, n_q), jnp.float32)

        def gradients(w, carry):
            base = pl.multiple_of(w * n_k, 128)
            for (q_lo, col, key_lo), inverse, delta, x in zip(subs, inverses, deltas, cols):
                here = pl.ds(pl.multiple_of(w * both + key_lo, 128), n_k)
                pbs, dss = [], []
                for r in range(0, n_k, ROWS_A):
                    f = peaks[w * blocks + r // ROWS_A, :, x] * inverse
                    at = pl.ds(base + r, ROWS_A)
                    e = s_scr[at, x].reshape(ROWS_A // 8, 8, n_q)
                    p = (e * f).reshape(ROWS_A, n_q)
                    dss.append((p * (p_scr[at, x] - delta)).astype(jnp.bfloat16))
                    pbs.append(p.astype(jnp.bfloat16))
                pb = jnp.concatenate(pbs, axis=0)
                ds = jnp.concatenate(dss, axis=0)
                grads = gs[q_lo : q_lo + n_q, :]
                queries = qs[q_lo : q_lo + n_q, :]
                dvw[here, :] = jnp.dot(pb, grads, preferred_element_type=jnp.float32)
                dkw[here, :] = jnp.dot(ds, queries, preferred_element_type=jnp.float32)
                dqt[:, x] += lax.dot_general(
                    kw[here, :], ds, (((0,), (0,)), ((), ())), preferred_element_type=jnp.float32
                )
            return carry

        lax.fori_loop(first, last, gradients, 0)
        for (q_lo, _, _), x in zip(subs, cols):
            dqs[q_lo : q_lo + n_q, :] = jnp.transpose(dqt[:, x]) * scale

    @pl.when(high == 1)
    def _():
        unit([(0, 0, 0)], n_q, both)

    @pl.when(high == 0)
    def _():
        step = (n_half + HD - 1) // HD * HD
        unit([(ht * n_half, ht * step, ht * full) for ht in range(2)], n_half, full)


def rows_of(ref, lead, start, cols, ht):
    block = ref[lead + (slice(None), pl.ds(start, cols), pl.ds(ht * 8, 8), slice(None))]
    n = block.shape[0] * cols * 8
    return block.astype(jnp.float32).reshape(n, HD).astype(jnp.bfloat16)


def block_of(src, lo, step, frames, cols, more=None, at=0):
    n = frames * cols * 8
    parts = []
    for start in (0, step):
        x = src[lo + start : lo + start + n, :]
        if more is not None:
            x = x + more[at + start : at + start + n, :].astype(jnp.float32)
        parts.append(x.reshape(frames, cols, 8, HD))
    return jnp.concatenate(parts, axis=2)


def clear(skipped, dkw, dvw):
    @pl.when(skipped)
    def _():
        dkw[...] = jnp.zeros_like(dkw)
        dvw[...] = jnp.zeros_like(dvw)


def put(ref, lead, start, cols, x):
    ref[lead + (slice(None), pl.ds(start, cols), slice(None), slice(None))] = x.astype(ref.dtype)


def fill_bias(bias, info, full):
    at = lax.broadcasted_iota(jnp.int32, (full, HD), 0)
    t = at // 64
    c = at // 8 - t * 8
    r = at - at // 8 * 8
    place = t * 64 + r * 8 + c
    for ht in range(2):
        bias[ht * full : (ht + 1) * full, :] = jnp.where(place < info.limit(ht), 0.0, -1e30)


def place_of(position, width):
    shifted = position * width + LW // 2
    return shifted // LW % HEAD_GROUPS, shifted % LW // width


class Scalars:
    def __init__(self, heads, position, extents, counts):
        self.place = position[0] & 3
        self.first_head = (position[0] >> 2) * heads
        self.extents = extents
        self.counts = counts
        self.parity = self.place & 1
        self.border = ((self.place == 0) | (self.place == 3)).astype(jnp.int32)

    def limit(self, ht):
        last = self.counts.shape[1] - 1
        return self.counts[ht, jnp.where(self.place == 0, 0, last)]


def flags(info):
    head = info.first_head + pl.program_id(0)
    high, wide = [(info.extents[axis, head] - 1) // 2 for axis in (0, 1)]
    return info.parity, info.border, high, wide


def mixed_kernel(info, q_ref, g_ref, k_ref, v_ref, nk_ref, nv_ref, dq_out, mix_out, mid_out, send_out,
                 *scratch):
    kw, vw, qs, gs, dqs, dkw, dvw = scratch[:7]
    parity, border, high, wide = flags(info)
    scale = 1.0 / HD**0.5
    frames = q_ref.shape[0]
    full = frames * TILE_H * TILE_W
    half, both = full // 2, 2 * full
    b_off = parity * 0
    a_off = 8 - parity * 8
    b_off = parity * 4
    mix_off = parity * 8
    out_off = 4 - parity * 4
    for ht in range(2):
        for dst, src in ((qs, q_ref), (gs, g_ref)):
            dst[ht * half : (ht + 1) * half, :] = rows_of(src, (), 0, 4, ht)
        for dst, src, near_ref in ((kw, k_ref, nk_ref), (vw, v_ref, nv_ref)):
            lo = ht * full
            dst[lo : lo + full, :] = rows_of(src, (), b_off, 8, ht)
            lo += both
            dst[lo : lo + half, :] = rows_of(src, (), a_off, 4, ht)
            dst[lo + half : lo + full, :] = rows_of(near_ref, (), mix_off, 4, ht)
            lo += both
            dst[lo : lo + full, :] = rows_of(near_ref, (), out_off, 8, ht)
    clear(wide == 0, dkw, dvw)
    attend("A", full, half, border, high, wide, *scratch)
    put(dq_out, (), 0, 4, block_of(dqs, 0, half, frames, 4))
    for which, src, factor in ((0, dkw, scale), (1, dvw, 1.0)):
        mid_out[which, 0] = src[0:both, :].astype(mid_out.dtype)
        mix_out[which, 0] = src[both : 2 * both, :].astype(mix_out.dtype)
        put(send_out, (which,), 0, 8, block_of(src, 2 * both, full, frames, 8) * factor)


def outer_kernel(info, q_ref, g_ref, k_ref, v_ref, far_ref, mid_ref, dq_held, dq_out, sum_out, send_out,
                 *scratch):
    kw, vw, qs, gs, dqs, dkw, dvw = scratch[:7]
    bias = scratch[-1]
    parity, border, high, wide = flags(info)
    scale = 1.0 / HD**0.5
    frames = q_ref.shape[0]
    full = frames * TILE_H * TILE_W
    both = 2 * full
    c_off = parity * 8
    b_off = 8 - parity * 8
    for ht in range(2):
        for dst, src in ((qs, q_ref), (gs, g_ref)):
            dst[ht * full : (ht + 1) * full, :] = rows_of(src, (), 0, 8, ht)
        for which, dst, src in ((0, kw, k_ref), (1, vw, v_ref)):
            lo = ht * full
            dst[lo : lo + full, :] = rows_of(far_ref, (which,), 0, 8, ht)
            lo += both
            dst[lo : lo + full, :] = rows_of(src, (), c_off, 8, ht)
            lo += both
            dst[lo : lo + full, :] = rows_of(src, (), b_off, 8, ht)

    @pl.when((border == 1) & (pl.program_id(0) == 0))
    def _():
        fill_bias(bias, info, full)

    clear((wide == 0) | (border == 1), dkw, dvw)
    attend("C", both, full, border, high, wide, *scratch)
    put(dq_out, (), 0, 8, block_of(dqs, 0, full, frames, 8))
    for which, src, factor in ((0, dkw, scale), (1, dvw, 1.0)):
        sum_out[which, 0, :both] = src[both : 2 * both, :].astype(sum_out.dtype)
        last = src[2 * both :, :] + mid_ref[which, 0].astype(jnp.float32)
        sum_out[which, 0, both:] = last.astype(sum_out.dtype)
        put(send_out, (which,), 0, 8, block_of(src, 0, full, frames, 8) * factor)


def inner_kernel(info, q_ref, g_ref, k_ref, v_ref, nk_ref, nv_ref, sum_ref, mix_ref, dq_held,
                 dq_out, dk_out, dv_out, send_out, *scratch):
    kw, vw, qs, gs, dqs, dkw, dvw = scratch[:7]
    bias = scratch[-1]
    parity, border, high, wide = flags(info)
    scale = 1.0 / HD**0.5
    frames = q_ref.shape[0]
    full = frames * TILE_H * TILE_W
    half, both = full // 2, 2 * full
    c_off = parity * 12
    b_off = 8 - parity * 4
    a_off = 16 - parity * 16
    for ht in range(2):
        for dst, src in ((qs, q_ref), (gs, g_ref)):
            dst[ht * full : (ht + 1) * full, :] = rows_of(src, (), 0, 8, ht)
        for dst, src, near_ref in ((kw, k_ref, nk_ref), (vw, v_ref, nv_ref)):
            lo = ht * full
            dst[lo : lo + full, :] = rows_of(src, (), c_off, 8, ht)
            lo += both
            dst[lo : lo + full, :] = rows_of(src, (), b_off, 8, ht)
            lo += both
            dst[lo : lo + half, :] = rows_of(src, (), a_off, 4, ht)
            dst[lo + half : lo + full, :] = rows_of(near_ref, (), 0, 4, ht)

    @pl.when((border == 1) & (pl.program_id(0) == 0))
    def _():
        fill_bias(bias, info, full)

    clear(wide == 0, dkw, dvw)
    attend("B", both, full, border, high, wide, *scratch)
    put(dq_out, (), 0, 8, block_of(dqs, 0, full, frames, 8))
    for which, src, factor, own_out in ((0, dkw, scale, dk_out), (1, dvw, 1.0, dv_out)):
        kept, mix = sum_ref.at[which, 0], mix_ref.at[which, 0]
        c_part = block_of(src, 0, full, frames, 8, kept, 0)
        b_part = block_of(src, both, full, frames, 8, kept, both)
        a_part = block_of(src, 2 * both, full, frames, 4, mix, 0)
        rest = block_of(src, 2 * both + half, full, frames, 4, mix, half)
        put(own_out, (), c_off, 8, c_part * factor)
        put(own_out, (), b_off, 8, b_part * factor)
        put(own_out, (), a_off, 4, a_part * factor)
        put(send_out, (which,), 0, 4, rest * factor)


def scratch_of(n_q, full):
    both = 2 * full
    groups = 3 * both // ROWS_A
    n_c = 2 * ((n_q // 2 + HD - 1) // HD * HD)
    return [
        pltpu.VMEM((3 * both, HD), jnp.bfloat16),
        pltpu.VMEM((3 * both, HD), jnp.bfloat16),
        pltpu.VMEM((n_q, HD), jnp.bfloat16),
        pltpu.VMEM((n_q, HD), jnp.bfloat16),
        pltpu.VMEM((n_q, HD), jnp.float32),
        pltpu.VMEM((3 * both, HD), jnp.float32),
        pltpu.VMEM((3 * both, HD), jnp.float32),
        pltpu.VMEM((3 * both, n_c), jnp.float32),
        pltpu.VMEM((3 * both, n_c), jnp.float32),
        pltpu.VMEM((groups, 8, n_c), jnp.float32),
        pltpu.VMEM((groups, 8, n_c), jnp.float32),
        pltpu.VMEM((groups, 8, n_c), jnp.float32),
        pltpu.VMEM((HD, n_c), jnp.float32),
        pltpu.VMEM((both, HD), jnp.float32),
    ]


def launch(kernel, name, n_q, width, full, heads, in_specs, out_specs, out_shape, args,
           aliases=None):
    flops = heads * 10 * n_q * 6 * full * HD

    def body(position, extents, counts, *refs):
        kernel(Scalars(heads, position, extents, counts), *refs)

    return pl.pallas_call(
        body,
        name=name,
        grid_spec=pltpu.PrefetchScalarGridSpec(
            num_scalar_prefetch=3,
            grid=(heads,),
            in_specs=in_specs,
            out_specs=out_specs,
            scratch_shapes=scratch_of(n_q, full),
        ),
        out_shape=out_shape,
        input_output_aliases=aliases or {},
        compiler_params=pltpu.CompilerParams(vmem_limit_bytes=60 * 1024 * 1024),
        cost_estimate=pl.CostEstimate(
            flops=flops, transcendentals=flops // (10 * HD), bytes_accessed=8 << 20
        ),
    )(*args[0], *args[1:])


def column_block(frames, rows, cols, width, offset):
    if isinstance(offset, int):
        return pl.BlockSpec((frames, cols, rows, HD), lambda h, *_: (0, offset, 0, h))
    return pl.BlockSpec(
        (pl.Element(frames), pl.Element(cols), pl.Element(rows), pl.Element(HD)),
        lambda h, position, *_: (0, offset(position[0] & 1), 0, h * HD),
    )


def attention_parts(info, q, k, v, g, near_k, near_v, heads):
    frames, width, rows, _ = q.shape
    full = frames * TILE_H * TILE_W
    both = 2 * full
    channels = heads * HD

    def pair(cols):
        return pl.BlockSpec((2, frames, cols, rows, HD), lambda h, *_: (0, 0, 0, 0, h))

    def chain(n):
        return pl.BlockSpec((2, 1, n, HD), lambda h, *_: (0, h, 0, 0))

    def columns(n, dtype=jnp.bfloat16):
        return jax.ShapeDtypeStruct((2, frames, n, rows, channels), dtype)

    def kept(n):
        return jax.ShapeDtypeStruct((2, heads, n, HD), jnp.bfloat16)

    def dq_shape(n):
        return jax.ShapeDtypeStruct((frames, n, rows, channels), jnp.bfloat16)

    def at(cols, offset):
        return column_block(frames, rows, cols, width, offset)

    held = pl.BlockSpec(memory_space=pl.ANY)

    def mixed():
        a, ab, nb = at(4, lambda p: 16 - 16 * p), at(12, lambda p: 8 - 8 * p), at(12, lambda p: 8 * p)
        return launch(
            mixed_kernel, "mixed", full, width, full, heads,
            [a, a, ab, ab, nb, nb],
            [a, chain(both), chain(both), pair(8)],
            [dq_shape(width), kept(both), kept(both), columns(8)],
            (info, q, g, k, v, near_k, near_v),
        )

    def outer(far, mid, dq):
        c, cb = at(8, lambda p: 12 * p), at(16, lambda p: 4 * p)
        return launch(
            outer_kernel, "outer", both, width, full, heads,
            [c, c, cb, cb, pair(8), chain(both), held],
            [c, chain(2 * both), pair(8)],
            [dq_shape(width), kept(2 * both), columns(8)],
            (info, q, g, k, v, far, mid, dq),
            {9: 0},
        )

    def inner(info, sums, mix, dq):
        b, every, na = at(8, lambda p: 8 - 4 * p), at(width, 0), at(4, lambda p: 16 * p)
        return launch(
            inner_kernel, "inner", both, width, full, heads,
            [b, b, every, every, na, na, chain(2 * both), chain(both), held],
            [b, every, every, pair(4)],
            [dq_shape(width), dq_shape(width), dq_shape(width), columns(4)],
            (info, q, g, k, v, near_k, near_v, sums, mix, dq),
            {11: 0},
        )

    return mixed, outer, inner


def quarter_body(queries, keys, values, out_grad, extents, counts):
    frames, rows, width, channels = queries.shape
    heads = channels // HD
    devices = lax.axis_size("sw")
    position = lax.axis_index("sw")
    group, place = place_of(position, width)
    parity = place % 2
    info = ((group * 4 + place).astype(jnp.int32).reshape(1), jnp.transpose(extents), counts)
    q, k, v, g = [jnp.transpose(x, (0, 2, 1, 3)) for x in (queries, keys, values, out_grad)]
    first = LW // 2 // width
    near_route = []
    far_route = []
    for i in range(devices):
        at = (i + first) % 4
        near_route.append((i, i + 1 if at % 2 == 0 else i - 1))
        if at == 1:
            far_route.append((i, (i + 1) % devices))
        if at == 2:
            far_route.append((i, (i - 1) % devices))
    near_route = [(a, b % devices) for a, b in near_route]
    near_k = lax.ppermute(k, "sw", near_route)
    near_v = lax.ppermute(v, "sw", near_route)
    far_own = lax.dynamic_slice_in_dim(jnp.stack([k, v]), 12 * parity, 8, 2)
    far = lax.ppermute(far_own, "sw", far_route)
    mixed, outer, inner = attention_parts(info, q, k, v, g, near_k, near_v, heads)
    dq, mix, mid, sent = mixed()
    mid_back = lax.ppermute(sent, "sw", near_route)
    dq, sums, far_part = outer(far, mid, dq)
    far_back = lax.ppermute(far_part, "sw", far_route)
    dq, dk, dv, last = inner(info, sums, mix, dq)
    edge_back = lax.ppermute(last, "sw", near_route)
    outs = [dq]
    for which, own in ((0, dk), (1, dv)):
        def placed(back, start):
            cols = own.shape[1] - start - back.shape[2]
            return jnp.pad(back[which], ((0, 0), (start, cols), (0, 0), (0, 0)))

        back = jnp.where(
            parity == 0,
            placed(far_back, 0) + placed(mid_back, 8) + placed(edge_back, 16),
            placed(edge_back, 0) + placed(mid_back, 4) + placed(far_back, 12),
        )
        own = (own.astype(jnp.float32) + back.astype(jnp.float32)).astype(jnp.bfloat16)
        outs.append(own)
    return tuple(jnp.transpose(x, (0, 2, 1, 3)) for x in outs)


def from_behind(block, axis, distance):
    devices = range(lax.axis_size(axis))
    route = [((i - distance) % len(devices), i) for i in devices]
    return lax.ppermute(block, axis, route)


def layout(cols, counts, frames, rows):
    tile_rows, tile_cols = counts.shape
    col_tile = cols // TILE_W
    col_ok = (cols >= 0) & (cols < LW)
    safe = jnp.clip(col_tile, 0, tile_cols - 1)
    row_ids = jnp.arange(rows)
    frame_ids = jnp.arange(frames)
    row_tile = row_ids // TILE_H
    pick_rows = (row_tile[:, None] == jnp.arange(tile_rows)[None, :]).astype(jnp.int32)
    pick_cols = (safe[:, None] == jnp.arange(tile_cols)[None, :]).astype(jnp.int32)
    limit = jnp.dot(jnp.dot(pick_rows, counts), jnp.transpose(pick_cols))
    place = (frame_ids[:, None, None] * TILE_H + (row_ids % TILE_H)[None, :, None]) * TILE_W + (
        cols % TILE_W
    )[None, None, :]
    valid = col_ok[None, None, :] & (place < limit[None, :, :])
    shape = (frames, rows, cols.shape[0])
    flat_tile = jnp.broadcast_to(col_tile[None, None, :], shape).reshape(-1)
    flat_rowtile = jnp.broadcast_to(row_tile[None, :, None], shape).reshape(-1)
    flat_colok = jnp.broadcast_to(col_ok[None, None, :], shape).reshape(-1)
    return (flat_tile, flat_rowtile, flat_colok, valid.reshape(-1))


def contract_rows(left, right):
    return lax.dot_general(
        left, right, (((0,), (0,)), ((), ())), preferred_element_type=jnp.float32
    )


def contract_cols(left, right):
    return lax.dot_general(
        left, right, (((1,), (1,)), ((), ())), preferred_element_type=jnp.float32
    )


def near_keys_values(stacked, reach):
    pieces = []
    for step_by in range(reach, -reach - 1, -1):
        if step_by == 0:
            pieces.append(stacked)
        else:
            pieces.append(from_behind(stacked, "sw", step_by))
    return jnp.concatenate(pieces, axis=3)


def query_side(
    local_q, local_g, near_keys, near_values, width_gap, height_gap, key_ok, radius, scale
):
    heads = radius.shape[0]
    channels = local_q.shape[1]
    head_dim = channels // heads
    query_rows = local_q.shape[0]
    key_rows = near_keys.shape[0]

    def step(carry, head):
        column_start = head * head_dim
        head_query = lax.dynamic_slice_in_dim(local_q, column_start, head_dim, 1)
        head_grad = lax.dynamic_slice_in_dim(local_g, column_start, head_dim, 1)
        head_key = lax.dynamic_slice_in_dim(near_keys, column_start, head_dim, 1)
        head_value = lax.dynamic_slice_in_dim(near_values, column_start, head_dim, 1)
        allowed = key_ok[None, :] & (width_gap <= radius[head, 1]) & (height_gap <= radius[head, 0])
        scores = contract_cols(head_query, head_key) * scale
        masked = jnp.where(allowed, scores, -1e30)
        row_peak = jnp.max(masked, axis=1, keepdims=True)
        row_total = jnp.sum(
            jnp.where(allowed, jnp.exp(masked - row_peak), 0.0), axis=1, keepdims=True
        )
        log_total = row_peak + jnp.log(row_total)
        probs = jnp.exp(masked - log_total)
        probs_b = probs.astype(jnp.bfloat16)
        attended = jnp.dot(probs_b, head_value, preferred_element_type=jnp.float32)
        delta = jnp.sum(head_grad.astype(jnp.float32) * attended, axis=1, keepdims=True)
        dprobs = contract_cols(head_grad, head_value)
        dscores_b = (probs * (dprobs - delta)).astype(jnp.bfloat16)
        query_part = (
            jnp.dot(dscores_b, head_key, preferred_element_type=jnp.float32) * scale
        ).astype(jnp.bfloat16)
        query_acc = lax.dynamic_update_slice_in_dim(carry[0], query_part, column_start, 1)
        key_part = contract_rows(dscores_b, head_query) * scale
        value_part = contract_rows(probs_b, head_grad)
        key_acc = lax.dynamic_update_slice_in_dim(carry[1], key_part, column_start, 1)
        value_acc = lax.dynamic_update_slice_in_dim(carry[2], value_part, column_start, 1)
        return ((query_acc, key_acc, value_acc), None)

    query_init = jnp.zeros((query_rows, channels), jnp.bfloat16)
    init = (
        query_init,
        jnp.zeros((key_rows, channels), jnp.float32),
        jnp.zeros((key_rows, channels), jnp.float32),
    )
    result, unused = lax.scan(step, init, jnp.arange(heads))
    return result


def general_body(queries, keys, values, out_grad, extents, counts):
    frames, rows, width, channels = queries.shape
    group_heads = channels // HD
    scale = 1.0 / HD**0.5
    reach = (2 * TILE_W - 2 + width) // width
    rim_width = reach * width
    key_span = width + 2 * rim_width
    position = lax.axis_index("sw")
    shifted = position * width + LW // 2
    group = shifted // LW % HEAD_GROUPS
    own_start = shifted % LW
    radius = lax.dynamic_slice_in_dim((extents - 1) // 2, group * group_heads, group_heads, 0)
    near_cols = own_start - rim_width + jnp.arange(key_span)
    own_cols = own_start + jnp.arange(width)
    near_tile, near_rowtile, near_colok, near_ok = layout(near_cols, counts, frames, rows)
    own_tile, own_rowtile, own_colok, own_ok = layout(own_cols, counts, frames, rows)
    local_q = queries.reshape(-1, channels)
    local_g = out_grad.reshape(-1, channels)
    stacked = jnp.stack([keys, values])
    near = near_keys_values(stacked, reach)
    near_keys = near[0].reshape(-1, channels)
    near_values = near[1].reshape(-1, channels)
    width_gap = jnp.abs(own_tile[:, None] - near_tile[None, :])
    height_gap = jnp.abs(own_rowtile[:, None] - near_rowtile[None, :])
    query_grad, key_near, value_near = query_side(
        local_q, local_g, near_keys, near_values, width_gap, height_gap, near_ok, radius, scale
    )
    partial_value = jnp.stack(
        [
            key_near.reshape(frames, rows, key_span, channels),
            value_near.reshape(frames, rows, key_span, channels),
        ]
    )
    summed = lax.slice_in_dim(partial_value, rim_width, rim_width + width, axis=3)
    for step_by in range(-reach, reach + 1):
        if step_by != 0:
            piece = lax.slice_in_dim(
                partial_value,
                rim_width + step_by * width,
                rim_width + (step_by + 1) * width,
                axis=3,
            )
            summed = summed + from_behind(piece, "sw", step_by)
    key_grad = summed[0].astype(jnp.bfloat16)
    value_grad = summed[1].astype(jnp.bfloat16)
    return (query_grad.reshape(frames, rows, width, channels), key_grad, value_grad)


def body(queries, keys, values, out_grad, extents, counts):
    frames, rows, width, channels = queries.shape
    quarters = width == 20 and rows == 16 and LW == 4 * width and counts.shape[0] == 2
    chosen = quarter_body if quarters else general_body
    return chosen(queries, keys, values, out_grad, extents, counts)


def solution(mesh):
    placed = P("clips", None, "sw", None)
    return jax.shard_map(
        body,
        mesh=mesh,
        in_specs=(placed, placed, placed, placed, P(), P()),
        out_specs=(placed, placed, placed),
        check_vma=False,
    )
```

```python
import functools

import jax
import jax.numpy as jnp
from jax import lax
from jax.experimental import pallas as pl
from jax.experimental.pallas import tpu as pltpu
from jax.sharding import PartitionSpec as P

HD = 128
HEAD_GROUPS = 4
TILE_H = 8
TILE_W = 8
LW = 80
ROWS_A = 64
DOT_ROWS = 768
COLS_A = 256
LOG2E = 1.4426950408889634


def attend(role, n_q, n_half, border, high, wide, kw, vw, qs, gs, dqs, dkw, dvw,
           s_scr, p_scr, peaks, totals, weights, dqt, bias):
    scale = 1.0 / HD**0.5
    rate = scale * LOG2E
    both = kw.shape[0] // 3
    full = both // 2

    def unit(subs, n_q, n_k):
        first = 1 - wide
        if role == "C":
            first = jnp.where(border == 1, 1, first)
        last = 2 + wide
        blocks = n_k // ROWS_A
        slices = [(x, min(COLS_A, n_q - x)) for x in range(0, n_q, COLS_A)]

        def products(w, masked):
            for q_lo, col, key_lo in subs:
                start = pl.multiple_of(w * both + key_lo, 128)
                for b in range(0, n_k, min(DOT_ROWS, n_k)):
                    n_d = min(DOT_ROWS, n_k)
                    key_rows = pl.ds(start + b, n_d)
                    for x, n in slices:
                        s_all = lax.dot_general(
                            kw[key_rows, :], qs[q_lo + x : q_lo + x + n, :],
                            (((1,), (1,)), ((), ())), preferred_element_type=jnp.float32,
                        )
                        dp_all = lax.dot_general(
                            vw[key_rows, :], gs[q_lo + x : q_lo + x + n, :],
                            (((1,), (1,)), ((), ())), preferred_element_type=jnp.float32,
                        )
                        here = slice(col + x, col + x + n)
                        for y in range(0, n_d, ROWS_A):
                            s = s_all[y : y + ROWS_A]
                            dp = dp_all[y : y + ROWS_A]
                            to = pl.ds(pl.multiple_of(w * n_k, 128) + b + y, ROWS_A)
                            if masked:
                                off = bias[key_lo + b + y : key_lo + b + y + ROWS_A, :]
                                s = s + jnp.concatenate([off] * pl.cdiv(n, HD), axis=1)[:, :n]
                            s = s.reshape(ROWS_A // 8, 8, n)
                            peak = jnp.max(s, axis=0)
                            e = jnp.exp2(s * rate - peak * rate)
                            dp3 = dp.reshape(ROWS_A // 8, 8, n)
                            at = w * blocks + (b + y) // ROWS_A
                            peaks[at, :, here] = peak
                            totals[at, :, here] = jnp.sum(e, axis=0)
                            weights[at, :, here] = jnp.sum(e * dp3, axis=0)
                            s_scr[to, here] = e.reshape(ROWS_A, n)
                            p_scr[to, here] = dp

        def plain_step(w, carry):
            products(w, False)
            return carry

        def masked_step(w, carry):
            products(w, True)
            return carry

        split = first
        if role != "A":
            edge = 1 if role == "C" else 0
            split = jnp.where(border == 1, jnp.maximum(first, edge + 1), first)
            lax.fori_loop(first, split, masked_step, 0)
        lax.fori_loop(split, last, plain_step, 0)

        cols = [slice(col, col + n_q) for _, col, _ in subs]

        def highest(w, carry):
            out = []
            for c, x in zip(carry, cols):
                for b in range(blocks):
                    c = jnp.maximum(c, peaks[w * blocks + b, :, x])
                out.append(c)
            return tuple(out)

        start_peak = jnp.full((8, n_q), -3e38, jnp.float32)
        tops = lax.fori_loop(first, last, highest, tuple(start_peak for _ in subs))
        tops = [jnp.max(top, axis=0, keepdims=True) for top in tops]

        def combine(w, carry):
            out = []
            for (total, weighted), top, x in zip(carry, tops, cols):
                for b in range(blocks):
                    i = w * blocks + b
                    f = jnp.exp2((peaks[i, :, x] - top) * rate)
                    peaks[i, :, x] = f
                    total = total + f * totals[i, :, x]
                    weighted = weighted + f * weights[i, :, x]
                out.append((total, weighted))
            return tuple(out)

        zero = jnp.zeros((8, n_q), jnp.float32)
        sums = lax.fori_loop(first, last, combine, tuple((zero, zero) for _ in subs))
        inverses = [1.0 / jnp.sum(total, axis=0, keepdims=True) for total, _ in sums]
        deltas = [
            jnp.sum(weighted, axis=0, keepdims=True) * inverse
            for (_, weighted), inverse in zip(sums, inverses)
        ]
        for x in cols:
            dqt[:, x] = jnp.zeros((HD, n_q), jnp.float32)

        def gradients(w, carry):
            base = pl.multiple_of(w * n_k, 128)
            for (q_lo, col, key_lo), inverse, delta, x in zip(subs, inverses, deltas, cols):
                here = pl.ds(pl.multiple_of(w * both + key_lo, 128), n_k)
                pbs, dss = [], []
                for r in range(0, n_k, ROWS_A):
                    f = peaks[w * blocks + r // ROWS_A, :, x] * inverse
                    at = pl.ds(base + r, ROWS_A)
                    e = s_scr[at, x].reshape(ROWS_A // 8, 8, n_q)
                    p = (e * f).reshape(ROWS_A, n_q)
                    dss.append((p * (p_scr[at, x] - delta)).astype(jnp.bfloat16))
                    pbs.append(p.astype(jnp.bfloat16))
                pb = jnp.concatenate(pbs, axis=0)
                ds = jnp.concatenate(dss, axis=0)
                grads = gs[q_lo : q_lo + n_q, :]
                queries = qs[q_lo : q_lo + n_q, :]
                dvw[here, :] = jnp.dot(pb, grads, preferred_element_type=jnp.float32)
                dkw[here, :] = jnp.dot(ds, queries, preferred_element_type=jnp.float32)
                dqt[:, x] += lax.dot_general(
                    kw[here, :], ds, (((0,), (0,)), ((), ())), preferred_element_type=jnp.float32
                )
            return carry

        lax.fori_loop(first, last, gradients, 0)
        for (q_lo, _, _), x in zip(subs, cols):
            dqs[q_lo : q_lo + n_q, :] = jnp.transpose(dqt[:, x]) * scale

    @pl.when(high == 1)
    def _():
        unit([(0, 0, 0)], n_q, both)

    @pl.when(high == 0)
    def _():
        step = (n_half + HD - 1) // HD * HD
        unit([(ht * n_half, ht * step, ht * full) for ht in range(2)], n_half, full)


def rows_of(ref, lead, start, cols, ht):
    block = ref[lead + (slice(None), pl.ds(start, cols), pl.ds(ht * 8, 8), slice(None))]
    n = block.shape[0] * cols * 8
    return block.astype(jnp.float32).reshape(n, HD).astype(jnp.bfloat16)


def block_of(src, lo, step, frames, cols, more=None, at=0):
    n = frames * cols * 8
    parts = []
    for start in (0, step):
        x = src[lo + start : lo + start + n, :]
        if more is not None:
            x = x + more[at + start : at + start + n, :].astype(jnp.float32)
        parts.append(x.reshape(frames, cols, 8, HD))
    return jnp.concatenate(parts, axis=2)


def clear(skipped, dkw, dvw):
    @pl.when(skipped)
    def _():
        dkw[...] = jnp.zeros_like(dkw)
        dvw[...] = jnp.zeros_like(dvw)


def put(ref, lead, start, cols, x):
    ref[lead + (slice(None), pl.ds(start, cols), slice(None), slice(None))] = x.astype(ref.dtype)


def fill_bias(bias, info, full):
    at = lax.broadcasted_iota(jnp.int32, (full, HD), 0)
    t = at // 64
    c = at // 8 - t * 8
    r = at - at // 8 * 8
    place = t * 64 + r * 8 + c
    for ht in range(2):
        bias[ht * full : (ht + 1) * full, :] = jnp.where(place < info.limit(ht), 0.0, -1e30)


def place_of(position, width):
    shifted = position * width + LW // 2
    return shifted // LW % HEAD_GROUPS, shifted % LW // width


class Scalars:
    def __init__(self, heads, position, extents, counts):
        self.place = position[0] & 3
        self.first_head = (position[0] >> 2) * heads
        self.extents = extents
        self.counts = counts
        self.parity = self.place & 1
        self.border = ((self.place == 0) | (self.place == 3)).astype(jnp.int32)

    def limit(self, ht):
        last = self.counts.shape[1] - 1
        return self.counts[ht, jnp.where(self.place == 0, 0, last)]


def flags(info):
    head = info.first_head + pl.program_id(0)
    high, wide = [(info.extents[axis, head] - 1) // 2 for axis in (0, 1)]
    return info.parity, info.border, high, wide


def mixed_kernel(info, q_ref, g_ref, k_ref, v_ref, nk_ref, nv_ref, dq_out, mix_out, mid_out, send_out,
                 *scratch):
    kw, vw, qs, gs, dqs, dkw, dvw = scratch[:7]
    parity, border, high, wide = flags(info)
    scale = 1.0 / HD**0.5
    frames = q_ref.shape[0]
    full = frames * TILE_H * TILE_W
    half, both = full // 2, 2 * full
    b_off = parity * 0
    a_off = 8 - parity * 8
    b_off = parity * 4
    mix_off = parity * 8
    out_off = 4 - parity * 4
    for ht in range(2):
        for dst, src in ((qs, q_ref), (gs, g_ref)):
            dst[ht * half : (ht + 1) * half, :] = rows_of(src, (), 0, 4, ht)
        for dst, src, near_ref in ((kw, k_ref, nk_ref), (vw, v_ref, nv_ref)):
            lo = ht * full
            dst[lo : lo + full, :] = rows_of(src, (), b_off, 8, ht)
            lo += both
            dst[lo : lo + half, :] = rows_of(src, (), a_off, 4, ht)
            dst[lo + half : lo + full, :] = rows_of(near_ref, (), mix_off, 4, ht)
            lo += both
            dst[lo : lo + full, :] = rows_of(near_ref, (), out_off, 8, ht)
    clear(wide == 0, dkw, dvw)
    attend("A", full, half, border, high, wide, *scratch)
    put(dq_out, (), 0, 4, block_of(dqs, 0, half, frames, 4))
    for which, src, factor in ((0, dkw, scale), (1, dvw, 1.0)):
        mid_out[which, 0] = src[0:both, :].astype(mid_out.dtype)
        mix_out[which, 0] = src[both : 2 * both, :].astype(mix_out.dtype)
        put(send_out, (which,), 0, 8, block_of(src, 2 * both, full, frames, 8) * factor)


def outer_kernel(info, q_ref, g_ref, k_ref, v_ref, far_ref, mid_ref, dq_held, dq_out, sum_out, send_out,
                 *scratch):
    kw, vw, qs, gs, dqs, dkw, dvw = scratch[:7]
    bias = scratch[-1]
    parity, border, high, wide = flags(info)
    scale = 1.0 / HD**0.5
    frames = q_ref.shape[0]
    full = frames * TILE_H * TILE_W
    both = 2 * full
    c_off = parity * 8
    b_off = 8 - parity * 8
    for ht in range(2):
        for dst, src in ((qs, q_ref), (gs, g_ref)):
            dst[ht * full : (ht + 1) * full, :] = rows_of(src, (), 0, 8, ht)
        for which, dst, src in ((0, kw, k_ref), (1, vw, v_ref)):
            lo = ht * full
            dst[lo : lo + full, :] = rows_of(far_ref, (which,), 0, 8, ht)
            lo += both
            dst[lo : lo + full, :] = rows_of(src, (), c_off, 8, ht)
            lo += both
            dst[lo : lo + full, :] = rows_of(src, (), b_off, 8, ht)

    @pl.when((border == 1) & (pl.program_id(0) == 0))
    def _():
        fill_bias(bias, info, full)

    clear((wide == 0) | (border == 1), dkw, dvw)
    attend("C", both, full, border, high, wide, *scratch)
    put(dq_out, (), 0, 8, block_of(dqs, 0, full, frames, 8))
    for which, src, factor in ((0, dkw, scale), (1, dvw, 1.0)):
        sum_out[which, 0, :both] = src[both : 2 * both, :].astype(sum_out.dtype)
        last = src[2 * both :, :] + mid_ref[which, 0].astype(jnp.float32)
        sum_out[which, 0, both:] = last.astype(sum_out.dtype)
        put(send_out, (which,), 0, 8, block_of(src, 0, full, frames, 8) * factor)


def inner_kernel(info, q_ref, g_ref, k_ref, v_ref, nk_ref, nv_ref, sum_ref, mix_ref, dq_held,
                 dq_out, dk_out, dv_out, send_out, *scratch):
    kw, vw, qs, gs, dqs, dkw, dvw = scratch[:7]
    bias = scratch[-1]
    parity, border, high, wide = flags(info)
    scale = 1.0 / HD**0.5
    frames = q_ref.shape[0]
    full = frames * TILE_H * TILE_W
    half, both = full // 2, 2 * full
    c_off = parity * 12
    b_off = 8 - parity * 4
    a_off = 16 - parity * 16
    for ht in range(2):
        for dst, src in ((qs, q_ref), (gs, g_ref)):
            dst[ht * full : (ht + 1) * full, :] = rows_of(src, (), 0, 8, ht)
        for dst, src, near_ref in ((kw, k_ref, nk_ref), (vw, v_ref, nv_ref)):
            lo = ht * full
            dst[lo : lo + full, :] = rows_of(src, (), c_off, 8, ht)
            lo += both
            dst[lo : lo + full, :] = rows_of(src, (), b_off, 8, ht)
            lo += both
            dst[lo : lo + half, :] = rows_of(src, (), a_off, 4, ht)
            dst[lo + half : lo + full, :] = rows_of(near_ref, (), 0, 4, ht)

    @pl.when((border == 1) & (pl.program_id(0) == 0))
    def _():
        fill_bias(bias, info, full)

    clear(wide == 0, dkw, dvw)
    attend("B", both, full, border, high, wide, *scratch)
    put(dq_out, (), 0, 8, block_of(dqs, 0, full, frames, 8))
    for which, src, factor, own_out in ((0, dkw, scale, dk_out), (1, dvw, 1.0, dv_out)):
        kept, mix = sum_ref.at[which, 0], mix_ref.at[which, 0]
        c_part = block_of(src, 0, full, frames, 8, kept, 0)
        b_part = block_of(src, both, full, frames, 8, kept, both)
        a_part = block_of(src, 2 * both, full, frames, 4, mix, 0)
        rest = block_of(src, 2 * both + half, full, frames, 4, mix, half)
        put(own_out, (), c_off, 8, c_part * factor)
        put(own_out, (), b_off, 8, b_part * factor)
        put(own_out, (), a_off, 4, a_part * factor)
        put(send_out, (which,), 0, 4, rest * factor)


def scratch_of(n_q, full):
    both = 2 * full
    groups = 3 * both // ROWS_A
    n_c = 2 * ((n_q // 2 + HD - 1) // HD * HD)
    return [
        pltpu.VMEM((3 * both, HD), jnp.bfloat16),
        pltpu.VMEM((3 * both, HD), jnp.bfloat16),
        pltpu.VMEM((n_q, HD), jnp.bfloat16),
        pltpu.VMEM((n_q, HD), jnp.bfloat16),
        pltpu.VMEM((n_q, HD), jnp.float32),
        pltpu.VMEM((3 * both, HD), jnp.float32),
        pltpu.VMEM((3 * both, HD), jnp.float32),
        pltpu.VMEM((3 * both, n_c), jnp.float32),
        pltpu.VMEM((3 * both, n_c), jnp.float32),
        pltpu.VMEM((groups, 8, n_c), jnp.float32),
        pltpu.VMEM((groups, 8, n_c), jnp.float32),
        pltpu.VMEM((groups, 8, n_c), jnp.float32),
        pltpu.VMEM((HD, n_c), jnp.float32),
        pltpu.VMEM((both, HD), jnp.float32),
    ]


def launch(kernel, name, n_q, width, full, heads, in_specs, out_specs, out_shape, args,
           aliases=None):
    flops = heads * 10 * n_q * 6 * full * HD

    def body(position, extents, counts, *refs):
        kernel(Scalars(heads, position, extents, counts), *refs)

    return pl.pallas_call(
        body,
        name=name,
        grid_spec=pltpu.PrefetchScalarGridSpec(
            num_scalar_prefetch=3,
            grid=(heads,),
            in_specs=in_specs,
            out_specs=out_specs,
            scratch_shapes=scratch_of(n_q, full),
        ),
        out_shape=out_shape,
        input_output_aliases=aliases or {},
        compiler_params=pltpu.CompilerParams(vmem_limit_bytes=60 * 1024 * 1024),
        cost_estimate=pl.CostEstimate(
            flops=flops, transcendentals=flops // (10 * HD), bytes_accessed=8 << 20
        ),
    )(*args[0], *args[1:])


def column_block(frames, rows, cols, width, offset):
    if isinstance(offset, int):
        return pl.BlockSpec((frames, cols, rows, HD), lambda h, *_: (0, offset, 0, h))
    return pl.BlockSpec(
        (pl.Element(frames), pl.Element(cols), pl.Element(rows), pl.Element(HD)),
        lambda h, position, *_: (0, offset(position[0] & 1), 0, h * HD),
    )


def attention_parts(info, q, k, v, g, near_k, near_v, heads):
    frames, width, rows, _ = q.shape
    full = frames * TILE_H * TILE_W
    both = 2 * full
    channels = heads * HD

    def pair(cols):
        return pl.BlockSpec((2, frames, cols, rows, HD), lambda h, *_: (0, 0, 0, 0, h))

    def chain(n):
        return pl.BlockSpec((2, 1, n, HD), lambda h, *_: (0, h, 0, 0))

    def columns(n, dtype=jnp.bfloat16):
        return jax.ShapeDtypeStruct((2, frames, n, rows, channels), dtype)

    def kept(n):
        return jax.ShapeDtypeStruct((2, heads, n, HD), jnp.bfloat16)

    def dq_shape(n):
        return jax.ShapeDtypeStruct((frames, n, rows, channels), jnp.bfloat16)

    def at(cols, offset):
        return column_block(frames, rows, cols, width, offset)

    held = pl.BlockSpec(memory_space=pl.ANY)

    def mixed():
        a, ab, nb = at(4, lambda p: 16 - 16 * p), at(12, lambda p: 8 - 8 * p), at(12, lambda p: 8 * p)
        return launch(
            mixed_kernel, "mixed", full, width, full, heads,
            [a, a, ab, ab, nb, nb],
            [a, chain(both), chain(both), pair(8)],
            [dq_shape(width), kept(both), kept(both), columns(8)],
            (info, q, g, k, v, near_k, near_v),
        )

    def outer(far, mid, dq):
        c, cb = at(8, lambda p: 12 * p), at(16, lambda p: 4 * p)
        return launch(
            outer_kernel, "outer", both, width, full, heads,
            [c, c, cb, cb, pair(8), chain(both), held],
            [c, chain(2 * both), pair(8)],
            [dq_shape(width), kept(2 * both), columns(8)],
            (info, q, g, k, v, far, mid, dq),
            {9: 0},
        )

    def inner(info, sums, mix, dq):
        b, every, na = at(8, lambda p: 8 - 4 * p), at(width, 0), at(4, lambda p: 16 * p)
        return launch(
            inner_kernel, "inner", both, width, full, heads,
            [b, b, every, every, na, na, chain(2 * both), chain(both), held],
            [b, every, every, pair(4)],
            [dq_shape(width), dq_shape(width), dq_shape(width), columns(4)],
            (info, q, g, k, v, near_k, near_v, sums, mix, dq),
            {11: 0},
        )

    return mixed, outer, inner


def quarter_body(queries, keys, values, out_grad, extents, counts):
    frames, rows, width, channels = queries.shape
    heads = channels // HD
    devices = lax.axis_size("sw")
    position = lax.axis_index("sw")
    group, place = place_of(position, width)
    parity = place % 2
    info = ((group * 4 + place).astype(jnp.int32).reshape(1), jnp.transpose(extents), counts)
    q, k, v, g = [jnp.transpose(x, (0, 2, 1, 3)) for x in (queries, keys, values, out_grad)]
    first = LW // 2 // width
    near_route = []
    far_route = []
    for i in range(devices):
        at = (i + first) % 4
        near_route.append((i, i + 1 if at % 2 == 0 else i - 1))
        if at == 1:
            far_route.append((i, (i + 1) % devices))
        if at == 2:
            far_route.append((i, (i - 1) % devices))
    near_route = [(a, b % devices) for a, b in near_route]
    near_k = lax.ppermute(k, "sw", near_route)
    near_v = lax.ppermute(v, "sw", near_route)
    far_own = lax.dynamic_slice_in_dim(jnp.stack([k, v]), 12 * parity, 8, 2)
    far = lax.ppermute(far_own, "sw", far_route)
    mixed, outer, inner = attention_parts(info, q, k, v, g, near_k, near_v, heads)
    dq, mix, mid, sent = mixed()
    mid_back = lax.ppermute(sent, "sw", near_route)
    dq, sums, far_part = outer(far, mid, dq)
    far_back = lax.ppermute(far_part, "sw", far_route)
    dq, dk, dv, last = inner(info, sums, mix, dq)
    edge_back = lax.ppermute(last, "sw", near_route)
    outs = [dq]
    for which, own in ((0, dk), (1, dv)):
        def placed(back, start):
            cols = own.shape[1] - start - back.shape[2]
            return jnp.pad(back[which], ((0, 0), (start, cols), (0, 0), (0, 0)))

        back = jnp.where(
            parity == 0,
            placed(far_back, 0) + placed(mid_back, 8) + placed(edge_back, 16),
            placed(edge_back, 0) + placed(mid_back, 4) + placed(far_back, 12),
        )
        own = (own.astype(jnp.float32) + back.astype(jnp.float32)).astype(jnp.bfloat16)
        outs.append(own)
    return tuple(jnp.transpose(x, (0, 2, 1, 3)) for x in outs)


def from_behind(block, axis, distance):
    devices = range(lax.axis_size(axis))
    route = [((i - distance) % len(devices), i) for i in devices]
    return lax.ppermute(block, axis, route)


def layout(cols, counts, frames, rows):
    tile_rows, tile_cols = counts.shape
    col_tile = cols // TILE_W
    col_ok = (cols >= 0) & (cols < LW)
    safe = jnp.clip(col_tile, 0, tile_cols - 1)
    row_ids = jnp.arange(rows)
    frame_ids = jnp.arange(frames)
    row_tile = row_ids // TILE_H
    pick_rows = (row_tile[:, None] == jnp.arange(tile_rows)[None, :]).astype(jnp.int32)
    pick_cols = (safe[:, None] == jnp.arange(tile_cols)[None, :]).astype(jnp.int32)
    limit = jnp.dot(jnp.dot(pick_rows, counts), jnp.transpose(pick_cols))
    place = (frame_ids[:, None, None] * TILE_H + (row_ids % TILE_H)[None, :, None]) * TILE_W + (
        cols % TILE_W
    )[None, None, :]
    valid = col_ok[None, None, :] & (place < limit[None, :, :])
    shape = (frames, rows, cols.shape[0])
    flat_tile = jnp.broadcast_to(col_tile[None, None, :], shape).reshape(-1)
    flat_rowtile = jnp.broadcast_to(row_tile[None, :, None], shape).reshape(-1)
    flat_colok = jnp.broadcast_to(col_ok[None, None, :], shape).reshape(-1)
    return (flat_tile, flat_rowtile, flat_colok, valid.reshape(-1))


def contract_rows(left, right):
    return lax.dot_general(
        left, right, (((0,), (0,)), ((), ())), preferred_element_type=jnp.float32
    )


def contract_cols(left, right):
    return lax.dot_general(
        left, right, (((1,), (1,)), ((), ())), preferred_element_type=jnp.float32
    )


def near_keys_values(stacked, reach):
    pieces = []
    for step_by in range(reach, -reach - 1, -1):
        if step_by == 0:
            pieces.append(stacked)
        else:
            pieces.append(from_behind(stacked, "sw", step_by))
    return jnp.concatenate(pieces, axis=3)


def query_side(
    local_q, local_g, near_keys, near_values, width_gap, height_gap, key_ok, radius, scale
):
    heads = radius.shape[0]
    channels = local_q.shape[1]
    head_dim = channels // heads
    query_rows = local_q.shape[0]
    key_rows = near_keys.shape[0]

    def step(carry, head):
        column_start = head * head_dim
        head_query = lax.dynamic_slice_in_dim(local_q, column_start, head_dim, 1)
        head_grad = lax.dynamic_slice_in_dim(local_g, column_start, head_dim, 1)
        head_key = lax.dynamic_slice_in_dim(near_keys, column_start, head_dim, 1)
        head_value = lax.dynamic_slice_in_dim(near_values, column_start, head_dim, 1)
        allowed = key_ok[None, :] & (width_gap <= radius[head, 1]) & (height_gap <= radius[head, 0])
        scores = contract_cols(head_query, head_key) * scale
        masked = jnp.where(allowed, scores, -1e30)
        row_peak = jnp.max(masked, axis=1, keepdims=True)
        row_total = jnp.sum(
            jnp.where(allowed, jnp.exp(masked - row_peak), 0.0), axis=1, keepdims=True
        )
        log_total = row_peak + jnp.log(row_total)
        probs = jnp.exp(masked - log_total)
        probs_b = probs.astype(jnp.bfloat16)
        attended = jnp.dot(probs_b, head_value, preferred_element_type=jnp.float32)
        delta = jnp.sum(head_grad.astype(jnp.float32) * attended, axis=1, keepdims=True)
        dprobs = contract_cols(head_grad, head_value)
        dscores_b = (probs * (dprobs - delta)).astype(jnp.bfloat16)
        query_part = (
            jnp.dot(dscores_b, head_key, preferred_element_type=jnp.float32) * scale
        ).astype(jnp.bfloat16)
        query_acc = lax.dynamic_update_slice_in_dim(carry[0], query_part, column_start, 1)
        key_part = contract_rows(dscores_b, head_query) * scale
        value_part = contract_rows(probs_b, head_grad)
        key_acc = lax.dynamic_update_slice_in_dim(carry[1], key_part, column_start, 1)
        value_acc = lax.dynamic_update_slice_in_dim(carry[2], value_part, column_start, 1)
        return ((query_acc, key_acc, value_acc), None)

    query_init = jnp.zeros((query_rows, channels), jnp.bfloat16)
    init = (
        query_init,
        jnp.zeros((key_rows, channels), jnp.float32),
        jnp.zeros((key_rows, channels), jnp.float32),
    )
    result, unused = lax.scan(step, init, jnp.arange(heads))
    return result


def general_body(queries, keys, values, out_grad, extents, counts):
    frames, rows, width, channels = queries.shape
    group_heads = channels // HD
    scale = 1.0 / HD**0.5
    reach = (2 * TILE_W - 2 + width) // width
    rim_width = reach * width
    key_span = width + 2 * rim_width
    position = lax.axis_index("sw")
    shifted = position * width + LW // 2
    group = shifted // LW % HEAD_GROUPS
    own_start = shifted % LW
    radius = lax.dynamic_slice_in_dim((extents - 1) // 2, group * group_heads, group_heads, 0)
    near_cols = own_start - rim_width + jnp.arange(key_span)
    own_cols = own_start + jnp.arange(width)
    near_tile, near_rowtile, near_colok, near_ok = layout(near_cols, counts, frames, rows)
    own_tile, own_rowtile, own_colok, own_ok = layout(own_cols, counts, frames, rows)
    local_q = queries.reshape(-1, channels)
    local_g = out_grad.reshape(-1, channels)
    stacked = jnp.stack([keys, values])
    near = near_keys_values(stacked, reach)
    near_keys = near[0].reshape(-1, channels)
    near_values = near[1].reshape(-1, channels)
    width_gap = jnp.abs(own_tile[:, None] - near_tile[None, :])
    height_gap = jnp.abs(own_rowtile[:, None] - near_rowtile[None, :])
    query_grad, key_near, value_near = query_side(
        local_q, local_g, near_keys, near_values, width_gap, height_gap, near_ok, radius, scale
    )
    partial_value = jnp.stack(
        [
            key_near.reshape(frames, rows, key_span, channels),
            value_near.reshape(frames, rows, key_span, channels),
        ]
    )
    summed = lax.slice_in_dim(partial_value, rim_width, rim_width + width, axis=3)
    for step_by in range(-reach, reach + 1):
        if step_by != 0:
            piece = lax.slice_in_dim(
                partial_value,
                rim_width + step_by * width,
                rim_width + (step_by + 1) * width,
                axis=3,
            )
            summed = summed + from_behind(piece, "sw", step_by)
    key_grad = summed[0].astype(jnp.bfloat16)
    value_grad = summed[1].astype(jnp.bfloat16)
    return (query_grad.reshape(frames, rows, width, channels), key_grad, value_grad)


def body(queries, keys, values, out_grad, extents, counts):
    frames, rows, width, channels = queries.shape
    quarters = width == 20 and rows == 16 and LW == 4 * width and counts.shape[0] == 2
    chosen = quarter_body if quarters else general_body
    return chosen(queries, keys, values, out_grad, extents, counts)


def solution(mesh):
    placed = P("clips", None, "sw", None)
    return jax.shard_map(
        body,
        mesh=mesh,
        in_specs=(placed, placed, placed, placed, P(), P()),
        out_specs=(placed, placed, placed),
        check_vma=False,
    )
```
